32 devices in a mesh: section: 2 (over x), seq: 4 (over y, core), dp: 4 (over z).
Axes of the slice: x: 2, y: 2, z: 4, core: 2. Of those that a mesh axis runs over, the one named last changes fastest.
Arguments:
- boundary: bfloat16 [2, 8, 1024, 1024], P('section', 'dp', 'seq'), may hold values from -6 to 6
- positions: int32 [8, 1024], P('dp', 'seq'), may hold values from 0 to 1023, as said below
- decay_exp: int32 [2, 8], P('section'), may hold values from 8 to 32
- mixer_in: bfloat16 [2, 1024, 4096], P('section'), may hold values from -0.1875 to 0.1875
- mixer_out: bfloat16 [2, 1024, 1024], P('section'), may hold values from -0.1875 to 0.1875
- channel_in: bfloat16 [2, 1024, 5632], P('section'), may hold values from -0.1875 to 0.1875
- channel_out: bfloat16 [2, 2816, 1024], P('section'), may hold values from -0.109375 to 0.109375
Outputs:
- boundary_out: bfloat16 [2, 8, 1024, 1024], P('section', 'dp', 'seq')
- grad_mixer_in: float32 [2, 1024, 4096], P('section', 'seq')
- grad_mixer_out: float32 [2, 1024, 1024], P('section', 'seq')
- grad_channel_in: float32 [2, 1024, 5632], P('section', 'seq')
- grad_channel_out: float32 [2, 2816, 1024], P('section', 'seq')
The draws below stay inside these ranges and needn't reach their ends.
Inputs may be any that keep to these rules, and one draw needn't show every extreme that they name: `positions`: each sequence is cut into documents, the first token of every sequence starting one, and the first sequence is one whole document; a position counts the tokens since its document's start.
All inputs are finite; a program needn't handle non-finite values.
Results may differ from the reference program's by a relative error of at most 0.028.
Values may be sent and summed in bfloat16 or wider, within the bound.
No kernel may reach another device: no remote copies, remote signals or barrier semaphores. Data moves between devices by JAX's collectives and lax.ppermute only.
A program may use at most 256 MiB of HBM per device.

```python
import math
import jax
import jax.numpy as jnp
from jax import lax

D = 1024
FF = 2816
HEADS = 8
BLK = 256
LEN = 1024
BATCH = 8


def draw_positions(key, part):
    starts = jax.random.randint(key, (BATCH, LEN), 0, max(LEN // 8, 2)) == 0
    sequence_rows = jnp.arange(BATCH, dtype=jnp.int32)[:, None]
    starts = starts & (sequence_rows > 0)
    offsets = jnp.arange(LEN, dtype=jnp.int32)
    marked = jnp.where(starts | (offsets[None, :] == 0), offsets[None, :], 0)
    return offsets[None, :] - lax.cummax(marked, axis=1)


def plant(values, key, low, high):
    longest = values.shape.index(max(values.shape))
    spots = []
    for shift in (0, 1):
        where = [jax.random.randint(jax.random.fold_in(key, axis), (), 0, length) for axis, length in enumerate(values.shape)]
        where[longest] = (where[longest] + shift) % values.shape[longest]
        spots.append(tuple(where))
    return values.at[spots[0]].set(low).at[spots[1]].set(high)


def steps_of(key, dims, split, least, largest):
    loudness, own = 1.0, jax.random.fold_in(key, 6)
    for position, parts in split:
        steps = jnp.exp(jax.random.uniform(jax.random.fold_in(own, position), (parts,), jnp.float32, least / len(split), largest / len(split)))
        loudness = loudness * jnp.repeat(steps, dims[position] // parts).reshape([-1 if axis == position else 1 for axis in range(len(dims))])
    return loudness


def bell_draw(rng, extent, deviation, bound, cuts=(), kind=jnp.bfloat16):
    entries = deviation * jax.random.normal(rng, extent, jnp.float32)
    if cuts:
        entries = entries * steps_of(rng, extent, cuts, -0.22, 0.18)
    return jnp.clip(entries, -bound, bound).astype(kind)


def setup_inputs(seed: int = 0) -> dict:
    arg_keys = jax.random.split(jax.random.key(seed), 8)
    boundary = bell_draw(arg_keys[0], (2, BATCH, LEN, D), 1.0, 6.0, ((0, 2), (1, 4), (2, 4)))
    positions = draw_positions(jax.random.fold_in(arg_keys[7], 71), 0)
    decay_exp = plant(jax.random.randint(arg_keys[2], (2, HEADS), 8, 33), jax.random.fold_in(arg_keys[2], 1), 8, 32).astype(jnp.int32)
    mixer_in = bell_draw(arg_keys[3], (2, D, 4 * D), D ** -0.5, 0.1875, ((0, 2),))
    mixer_out = bell_draw(arg_keys[4], (2, D, D), D ** -0.5, 0.1875, ((0, 2),))
    channel_in = bell_draw(arg_keys[5], (2, D, 2 * FF), D ** -0.5, 0.1875, ((0, 2),))
    channel_out = bell_draw(arg_keys[6], (2, FF, D), FF ** -0.5, 0.109375, ((0, 2),))
    return dict(boundary=boundary, positions=positions, decay_exp=decay_exp, mixer_in=mixer_in, mixer_out=mixer_out, channel_in=channel_in, channel_out=channel_out)


@jax.custom_vjp
def low(v):
    return lax.optimization_barrier(v.astype(jnp.bfloat16)).astype(jnp.float32)

@jax.custom_vjp
def low_back(v):
    return v

def low_keep(v):
    return (low(v), None)

def low_pass(kept, grad):
    return (grad,)

def back_keep(v):
    return (v, None)

def back_low(kept, grad):
    return (low(grad),)
low.defvjp(low_keep, low_pass)
low_back.defvjp(back_keep, back_low)
epsilon = 1e-06
theta_base = 10000.0
highest = lax.Precision.HIGHEST

def simple_norm(source):
    return source * lax.rsqrt(lax.optimization_barrier(jnp.mean(source * source, axis=-1, keepdims=True)) + epsilon)

def angle_tables(position_row, half_size):
    frequency = jnp.exp(jnp.arange(half_size, dtype=jnp.float32) * (-math.log(theta_base) / half_size))
    angles = position_row.astype(jnp.float32)[:, None] * frequency[None, :]
    cosine = jnp.cos(angles)[:, None, :]
    sine_rows = jnp.sin(angles)[:, None, :]
    return (jnp.concatenate([cosine, cosine], axis=-1), jnp.concatenate([-sine_rows, sine_rows], axis=-1))

def rotate(source, cosine, sine_rows):
    half_size = source.shape[-1] // 2
    return source * cosine + jnp.roll(source, half_size, axis=-1) * sine_rows

def decay_tables(slopes, block_rows):
    offsets = jnp.arange(block_rows, dtype=jnp.float32)
    distance = offsets[:, None] - offsets[None, :]
    decay_mask = jnp.where(distance[None] >= 0.0, jnp.exp(-slopes[:, None, None] * jnp.maximum(distance, 0.0)[None]), 0.0)
    query_decay = jnp.exp(-slopes[None, :] * offsets[:, None])
    key_decay = jnp.exp(-slopes[None, :] * (block_rows - offsets)[:, None])
    block_decay = jnp.exp(-slopes * block_rows)
    return (decay_mask, query_decay, key_decay, block_decay)

def attend(queries, key_rows, values, slopes):
    length, head_count, head_size = queries.shape
    blocks = length // BLK
    decay_mask, query_decay, key_decay, block_decay = decay_tables(slopes, BLK)

    @jax.checkpoint
    def advance(carry_state, pieces):
        query_blk, key_blk, value_blk = pieces
        scores = low_back(jnp.einsum('ihe,jhe->hij', query_blk, key_blk, precision=highest))
        weights = low(decay_mask * scores)
        inner_term = jnp.einsum('hij,jhe->ihe', weights, value_blk, precision=highest)
        carried = low_back(jnp.einsum('ihe,hef->ihf', query_blk, low(carry_state), precision=highest))
        keyed_rows = low(key_blk * key_decay[:, :, None])
        contribution = low_back(jnp.einsum('jhe,jhf->hef', keyed_rows, value_blk, precision=highest))
        return (block_decay[:, None, None] * carry_state + contribution, inner_term + query_decay[:, :, None] * carried)
    pieces = tuple((member.reshape(blocks, BLK, head_count, head_size) for member in (queries, key_rows, values)))
    start_state = jnp.zeros((head_count, head_size, head_size), jnp.float32)
    final_state, attended = lax.scan(advance, start_state, pieces)
    return attended.reshape(length, head_count * head_size)

def apply_layer(inputs, cosine, sine_rows, slopes, first_in, first_out, second_in, second_out):
    model_width = inputs.shape[1]
    head_size = model_width // HEADS
    normed = low(simple_norm(inputs))
    projected = low_back(jnp.dot(normed, first_in, precision=highest))
    queries = low(rotate(jax.nn.silu(projected[:, :model_width]).reshape(-1, HEADS, head_size), cosine, sine_rows))
    key_rows = low(rotate(jax.nn.silu(projected[:, model_width:2 * model_width]).reshape(-1, HEADS, head_size), cosine, sine_rows))
    values = low(projected[:, 2 * model_width:3 * model_width].reshape(-1, HEADS, head_size))
    attended = low_back(attend(queries, key_rows, values, slopes))
    gated_rows = low(simple_norm(attended) * projected[:, 3 * model_width:])
    middle = inputs + low_back(jnp.dot(gated_rows, first_out, precision=highest))
    second = low(simple_norm(middle))
    gate_up = low_back(jnp.dot(second, second_in, precision=highest))
    hidden = second_out.shape[0]
    product = low(gate_up[:, :hidden] * gate_up[:, hidden:])
    return middle + low_back(jnp.dot(product, second_out, precision=highest))

def reference(boundary, positions, decay_exp, mixer_in, mixer_out, channel_in, channel_out):
    weights = tuple((member.astype(jnp.float32) for member in (mixer_in, mixer_out, channel_in, channel_out)))
    slopes = jnp.exp2(-0.5 * decay_exp.astype(jnp.float32))
    half_size = mixer_in.shape[1] // HEADS // 2

    def per_sequence(totals, pieces):
        inputs, cotangent, position_row = pieces
        cosine, sine_rows = angle_tables(position_row, half_size)

        def two_layers(source, layer_in, layer_out, unit_in, unit_out):
            between = apply_layer(source, cosine, sine_rows, slopes[0], layer_in[0], layer_out[0], unit_in[0], unit_out[0])
            between = low(low_back(between))
            return apply_layer(between, cosine, sine_rows, slopes[1], layer_in[1], layer_out[1], unit_in[1], unit_out[1])
        result, pullback = jax.vjp(two_layers, inputs, *weights)
        pulled = pullback(cotangent)
        totals = tuple((running_total + addend for running_total, addend in zip(totals, pulled[1:])))
        return (totals, (result, pulled[0]))
    zero_grads = tuple((jnp.zeros_like(member) for member in weights))
    items = (boundary[0].astype(jnp.float32), boundary[1].astype(jnp.float32), positions)
    totals, outputs = lax.scan(per_sequence, zero_grads, items)
    results, input_grads = outputs
    joined = jnp.stack([input_grads, results]).astype(jnp.bfloat16)
    return (joined, totals[0], totals[1], totals[2], totals[3])
```

```python
import functools
import math

import jax
import jax.numpy as jnp
from jax import lax
from jax.experimental import pallas as pl
from jax.experimental.pallas import tpu as pltpu
from jax.sharding import PartitionSpec as P

HEADS = 8
BLK = 256
LANES = 128
VMEM_BYTES = 56 * 1024 * 1024

epsilon = 1e-06
theta_base = 10000.0
f32 = jnp.float32
bf16 = jnp.bfloat16


def nn(a, b):
    return jnp.dot(a, b, preferred_element_type=f32)


def nt(a, b):
    return lax.dot_general(a, b, (((1,), (1,)), ((), ())), preferred_element_type=f32)


def tn(a, b):
    return lax.dot_general(a, b, (((0,), (0,)), ((), ())), preferred_element_type=f32)


def sigmoid(v):
    return 1.0 / (1.0 + jnp.exp(-v))


def norm_factor(v, width):
    return lax.rsqrt(jnp.sum(v * v, axis=-1, keepdims=True) * (1.0 / width) + epsilon)


def norm_back(cotangent, normed, factor, width):
    mean = jnp.sum(cotangent * normed, axis=-1, keepdims=True) * (1.0 / width)
    return factor * (cotangent - normed * mean)


def row_index(rows, columns):
    return lax.broadcasted_iota(jnp.int32, (rows, columns), 0).astype(f32)


def decay_mask(slope, rows):
    row = lax.broadcasted_iota(jnp.int32, (rows, rows), 0)
    column = lax.broadcasted_iota(jnp.int32, (rows, rows), 1)
    distance = jnp.maximum(row - column, 0).astype(f32)
    return jnp.where(row >= column, jnp.exp(distance * (-slope)), 0.0)


def head(number):
    return slice(number * LANES, (number + 1) * LANES)


def half_turn(v):
    return pltpu.roll(v, LANES // 2, 1)


def whole(shape):
    return pl.BlockSpec(shape, lambda j: (0,) * len(shape))


def params():
    return pltpu.CompilerParams(vmem_limit_bytes=VMEM_BYTES)


SMEM = pl.BlockSpec(memory_space=pltpu.SMEM)
ANY = pl.BlockSpec(memory_space=pl.ANY)


def project_body(slope, x, cosine, sine, w, h1, r1, pre, qk, state, keys, steps):
    j = pl.program_id(0)
    rows, width = x.shape
    columns = w.shape[1]
    heads = columns // LANES
    quarter = steps // 4

    @pl.when(j == 0)
    def _():
        v = x[...].astype(f32)
        factor = norm_factor(v, width)
        h1[...] = (v * factor).astype(bf16)
        r1[...] = jnp.broadcast_to(factor, r1.shape)

    p = nn(h1[...], w[...])
    pre[...] = p.astype(bf16)

    @pl.when(j < 2 * quarter)
    def _():
        for n in range(heads):
            v = p[:, head(n)]
            v = v * sigmoid(v)
            qk[:, head(n)] = (v * cosine[...] + half_turn(v) * sine[...]).astype(bf16)

    for part in range(quarter):

        @pl.when(j == quarter + part)
        def _():
            keys[:, part * columns : (part + 1) * columns] = qk[...]

        @pl.when(j == 2 * quarter + part)
        def _():
            values = p.astype(bf16)
            ahead = rows - row_index(rows, LANES)
            for n in range(heads):
                number = part * heads + n
                decay = jnp.exp(ahead * (-slope[number]))
                keyed = (keys[:, head(number)].astype(f32) * decay).astype(bf16)
                state[number] = tn(keyed, values[:, head(n)]).astype(bf16)


def project(slopes, x, cosine, sine, w):
    rows, width = x.shape
    total = w.shape[1]
    steps = 8
    columns = total // steps
    heads = width // LANES
    body = functools.partial(project_body, steps=steps)
    return pl.pallas_call(
        body,
        grid=(steps,),
        in_specs=[
            SMEM,
            whole((rows, width)),
            whole((rows, LANES)),
            whole((rows, LANES)),
            pl.BlockSpec((width, columns), lambda j: (0, j)),
        ],
        out_specs=[
            whole((rows, width)),
            whole((rows, LANES)),
            pl.BlockSpec((rows, columns), lambda j: (0, j)),
            pl.BlockSpec((rows, columns), lambda j: (0, jnp.minimum(j, steps // 2 - 1))),
            whole((heads, LANES, LANES)),
        ],
        out_shape=[
            jax.ShapeDtypeStruct((rows, width), bf16),
            jax.ShapeDtypeStruct((rows, LANES), f32),
            jax.ShapeDtypeStruct((rows, total), bf16),
            jax.ShapeDtypeStruct((rows, total // 2), bf16),
            jax.ShapeDtypeStruct((heads, LANES, LANES), bf16),
        ],
        scratch_shapes=[pltpu.VMEM((rows, width), bf16)],
        compiler_params=params(),
        cost_estimate=pl.CostEstimate(
            flops=2 * rows * width * total, bytes_accessed=2 * width * total, transcendentals=0
        ),
        name="project",
    )(slopes, x, cosine, sine, w)


def finish_body(
    slope, far, near, x, q, k, v, u, far_state, near_state, wo, wg, wu, wd,
    mixed, gated, ra, h2, r2, low, g, up, product, y, attended, total, steps,
):
    j = pl.program_id(0)
    rows, width = x.shape

    @pl.when(j == 0)
    def _():
        ahead = row_index(rows, LANES)
        for n in range(HEADS):
            state = far[n] * far_state[n].astype(f32) + near[n] * near_state[n].astype(f32)
            low[n] = state.astype(bf16)
            query = q[:, head(n)]
            weights = (decay_mask(slope[n], rows) * nt(query, k[:, head(n)])).astype(bf16)
            inner = nn(weights, v[:, head(n)])
            carried = nn(query, low[n])
            attended[:, head(n)] = inner + jnp.exp(ahead * (-slope[n])) * carried
        rows_out = attended[...]
        factor = norm_factor(rows_out, width)
        ra[...] = jnp.broadcast_to(factor, ra.shape)
        normed = rows_out * factor
        mixed[...] = normed.astype(bf16)
        gated[...] = (normed * u[...].astype(f32)).astype(bf16)
        middle = x[...].astype(f32) + nn(gated[...], wo[...])
        total[...] = middle
        factor = norm_factor(middle, width)
        r2[...] = jnp.broadcast_to(factor, r2.shape)
        h2[...] = (middle * factor).astype(bf16)

    gate = nn(h2[...], wg[...])
    rise = nn(h2[...], wu[...])
    g[...] = gate.astype(bf16)
    up[...] = rise.astype(bf16)
    product[...] = (gate * rise).astype(bf16)
    total[...] += nn(product[...], wd[...])

    @pl.when(j == steps - 1)
    def _():
        y[...] = total[...].astype(bf16)


def finish(slopes, far, near, x, qk, pre, far_state, near_state, wo, wi, wd):
    rows, width = x.shape
    hidden = wd.shape[0]
    columns = 256
    steps = hidden // columns
    states = (HEADS, LANES, LANES)
    wide = whole((rows, width))
    thin = whole((rows, LANES))
    side = lambda number: pl.BlockSpec((rows, width), lambda j: (0, number))
    column = pl.BlockSpec((rows, columns), lambda j: (0, j))
    body = functools.partial(finish_body, steps=steps)
    act = jax.ShapeDtypeStruct((rows, width), bf16)
    factor = jax.ShapeDtypeStruct((rows, LANES), f32)
    unit = jax.ShapeDtypeStruct((rows, hidden), bf16)
    return pl.pallas_call(
        body,
        grid=(steps,),
        in_specs=[
            SMEM, SMEM, SMEM, wide, side(0), side(1), side(2), side(3),
            whole(states), whole(states), whole((width, width)),
            pl.BlockSpec((width, columns), lambda j: (0, j)),
            pl.BlockSpec((width, columns), lambda j: (0, j + steps)),
            pl.BlockSpec((columns, width), lambda j: (j, 0)),
        ],
        out_specs=[wide, wide, thin, wide, thin, whole(states), column, column, column, wide],
        out_shape=[
            act, act, factor, act, factor,
            jax.ShapeDtypeStruct(states, bf16), unit, unit, unit, act,
        ],
        scratch_shapes=[pltpu.VMEM((rows, width), f32), pltpu.VMEM((rows, width), f32)],
        compiler_params=params(),
        cost_estimate=pl.CostEstimate(
            flops=2 * rows * width * (width + 3 * hidden),
            bytes_accessed=2 * width * (width + 3 * hidden),
            transcendentals=0,
        ),
        name="finish",
    )(slopes, far, near, x, qk, qk, pre, pre, far_state, near_state, wo, wi, wi, wd)


def back_channel_body(
    slope, dy, wd, wg, wu, g, up, h2, r2, wo, mixed, ra, u, q, k, v, low, qp, cosine, sine,
    dg, dup, dmid, dm, dq, du, dk, dv, state, total, datt, steps,
):
    j = pl.program_id(0)
    rows, width = dy.shape
    product = nt(dy[...], wd[...])
    dg[...] = (product * up[...].astype(f32)).astype(bf16)
    dup[...] = (product * g[...].astype(f32)).astype(bf16)
    step = nt(dg[...], wg[...]) + nt(dup[...], wu[...])

    @pl.when(j == 0)
    def _():
        total[...] = step

    @pl.when(j > 0)
    def _():
        total[...] += step

    @pl.when(j == steps - 1)
    def _():
        middle = dy[...].astype(f32) + norm_back(
            total[...], h2[...].astype(f32), r2[:, 0:1], width
        )
        dmid[...] = middle
        dm[...] = middle.astype(bf16)
        dgated = nt(dm[...], wo[...])
        normed = mixed[...].astype(f32)
        du[...] = (dgated * normed).astype(bf16)
        datt[...] = norm_back(dgated * u[...].astype(f32), normed, ra[:, 0:1], width).astype(bf16)
        ahead = row_index(rows, LANES)
        for n in range(HEADS):
            query, key, value, cot = q[:, head(n)], k[:, head(n)], v[:, head(n)], datt[:, head(n)]
            mask = decay_mask(slope[n], rows)
            weights = (mask * nt(query, key)).astype(bf16)
            scores = (mask * nt(cot, value)).astype(bf16)
            scaled = (jnp.exp(ahead * (-slope[n])) * cot.astype(f32)).astype(bf16)
            state[n] = tn(query, scaled).astype(bf16)
            dquery = nn(scores, key) + nt(scaled, low[n])
            back = dquery * cosine[...] + half_turn(dquery * sine[...])
            p = qp[:, head(n)].astype(f32)
            s = sigmoid(p)
            dq[:, head(n)] = (back * (s * (1.0 + p * (1.0 - s)))).astype(bf16)
            dk[:, head(n)] = tn(scores, query)
            dv[:, head(n)] = tn(weights, cot)


def back_channel(slopes, dy, r, cosine, sine, wo, wi, wd):
    rows, width = dy.shape
    hidden = wd.shape[0]
    columns = 256
    steps = hidden // columns
    states = (HEADS, LANES, LANES)
    wide = whole((rows, width))
    thin = whole((rows, LANES))
    side = lambda number: pl.BlockSpec((rows, width), lambda j: (0, number))
    column = pl.BlockSpec((rows, columns), lambda j: (0, j))
    act = jax.ShapeDtypeStruct((rows, width), bf16)
    full = jax.ShapeDtypeStruct((rows, width), f32)
    unit = jax.ShapeDtypeStruct((rows, hidden), bf16)
    return pl.pallas_call(
        functools.partial(back_channel_body, steps=steps),
        grid=(steps,),
        in_specs=[
            SMEM, wide,
            pl.BlockSpec((columns, width), lambda j: (j, 0)),
            pl.BlockSpec((width, columns), lambda j: (0, j)),
            pl.BlockSpec((width, columns), lambda j: (0, j + steps)),
            column, column, wide, thin, whole((width, width)), wide, thin,
            side(3), side(0), side(1), side(2), whole(states), side(0), thin, thin,
        ],
        out_specs=[column, column, wide, wide, wide, wide, wide, wide, whole(states)],
        out_shape=[unit, unit, full, act, act, act, full, full, jax.ShapeDtypeStruct(states, bf16)],
        scratch_shapes=[pltpu.VMEM((rows, width), f32), pltpu.VMEM((rows, width), bf16)],
        compiler_params=params(),
        cost_estimate=pl.CostEstimate(
            flops=2 * rows * width * (width + 3 * hidden),
            bytes_accessed=2 * width * (width + 3 * hidden),
            transcendentals=0,
        ),
        name="back_channel",
    )(
        slopes, dy, wd, wi, wi, r["g"], r["up"], r["h2"], r["r2"], wo, r["mixed"], r["ra"],
        r["pre"], r["qk"], r["qk"], r["pre"], r["low"], r["pre"], cosine, sine,
    )


def back_mixer_body(
    slope, far, near, dq, du, dk, dv, k, v, kp, far_state, near_state, cosine, sine, h1, r1, dmid, w,
    dkp, dvp, dx, parts, total, steps,
):
    j = pl.program_id(0)
    rows, width = dq.shape
    columns = w.shape[1]

    @pl.when(j == 0)
    def _():
        ahead = rows - row_index(rows, LANES)
        for n in range(HEADS):
            state = far[n] * far_state[n].astype(f32) + near[n] * near_state[n].astype(f32)
            state = state.astype(bf16)
            decay = jnp.exp(ahead * (-slope[n]))
            keyed = (k[:, head(n)].astype(f32) * decay).astype(bf16)
            dkey = dk[:, head(n)] + decay * nt(v[:, head(n)], state)
            back = dkey * cosine[...] + half_turn(dkey * sine[...])
            p = kp[:, head(n)].astype(f32)
            s = sigmoid(p)
            dkp[:, head(n)] = (back * (s * (1.0 + p * (1.0 - s)))).astype(bf16)
            dvp[:, head(n)] = (dv[:, head(n)] + nn(keyed, state)).astype(bf16)
        for number, part in enumerate((dq, dkp, dvp, du)):
            for piece in range(width // columns):
                parts[number * (width // columns) + piece] = part[
                    :, piece * columns : (piece + 1) * columns
                ]
        total[...] = jnp.zeros_like(total)

    total[...] += nt(parts[j], w[...])

    @pl.when(j == steps - 1)
    def _():
        dx[...] = (
            dmid[...] + norm_back(total[...], h1[...].astype(f32), r1[:, 0:1], width)
        ).astype(bf16)


def back_mixer(slopes, far, near, dq, du, dk, dv, r, far_state, near_state, cosine, sine, dmid, w):
    rows, width = dq.shape
    steps = 8
    columns = w.shape[1] // steps
    states = (HEADS, LANES, LANES)
    wide = whole((rows, width))
    thin = whole((rows, LANES))
    side = lambda number: pl.BlockSpec((rows, width), lambda j: (0, number))
    act = jax.ShapeDtypeStruct((rows, width), bf16)
    return pl.pallas_call(
        functools.partial(back_mixer_body, steps=steps),
        grid=(steps,),
        in_specs=[
            SMEM, SMEM, SMEM, wide, wide, wide, wide, side(1), side(2), side(1),
            whole(states), whole(states), thin, thin, wide, thin, wide,
            pl.BlockSpec((width, columns), lambda j: (0, j)),
        ],
        out_specs=[wide, wide, wide],
        out_shape=[act, act, act],
        scratch_shapes=[pltpu.VMEM((steps, rows, columns), bf16), pltpu.VMEM((rows, width), f32)],
        compiler_params=params(),
        cost_estimate=pl.CostEstimate(
            flops=2 * rows * width * w.shape[1],
            bytes_accessed=2 * width * w.shape[1],
            transcendentals=0,
        ),
        name="back_mixer",
    )(
        slopes, far, near, dq, du, dk, dv, r["qk"], r["pre"], r["pre"], far_state, near_state,
        cosine, sine, r["h1"], r["r1"], dmid, w,
    )


def weight_body(*refs, batch, sides, groups, wide):
    place = refs[0]
    lefts = refs[1 : 1 + 2 * batch]
    rights = refs[1 + 2 * batch : 1 + 2 * batch + 2 * batch * sides]
    outs = refs[1 + 2 * batch + 2 * batch * sides : -7]
    x, xt, ys, stage, xsem, ysem, osem = refs[-7:]
    rows = lefts[0].shape[0]
    columns = x.shape[1]
    quarter = columns // 4
    span = ys.shape[2]

    def copies(section):
        found = []
        for b in range(batch):
            found.append(
                pltpu.make_async_copy(
                    lefts[section * batch + b], x.at[pl.ds(b * rows, rows)], xsem.at[b]
                )
            )
        for s in range(sides):
            for b in range(batch):
                source = rights[(section * sides + s) * batch + b]
                found.append(
                    pltpu.make_async_copy(source, ys.at[s, pl.ds(b * rows, rows)], ysem.at[s, b])
                )
        return found

    for section in range(2):

        @pl.when(place[4] == section)
        def _():
            for copy in copies(section):
                copy.start()

    first = copies(0)
    for copy in first[:batch]:
        copy.wait()
    for piece in range(columns // LANES):
        xt[piece * LANES : (piece + 1) * LANES, :] = x[:, piece * LANES : (piece + 1) * LANES].T

    pending = []
    for number, (out, (s, start, blocks)) in enumerate(zip(outs, groups)):
        if all(s != done for done, _, _ in groups[:number]):
            for copy in first[batch + s * batch : batch + (s + 1) * batch]:
                copy.wait()
        for role in range(4):
            left = xt[pl.ds(pl.multiple_of(place[role] * quarter, 16), quarter), :]
            slot = number * 4 + role
            for block in range(0, blocks, wide):
                size = min(wide, blocks - block)
                at = (start + block) * LANES
                tile = nn(left, ys[s, :, at : at + size * LANES]).astype(bf16)
                for n in range(size):
                    stage[slot, block + n] = tile[:, head(n)]
            copy = pltpu.make_async_copy(
                stage.at[slot, pl.ds(0, blocks)], out.at[pl.ds(role * blocks, blocks)], osem.at[slot]
            )
            copy.start()
            pending.append(copy)
    for copy in pending:
        copy.wait()


def weight_gradient(place, lefts, rights, groups):
    batch = len(lefts[0])
    sides = len(rights[0])
    rows, columns = lefts[0][0].shape
    span = rights[0][0][0].shape[1]
    quarter = columns // 4
    most = max(blocks for _, _, blocks in groups)
    flat_left = [a for section in lefts for a in section]
    flat_right = [a for section in rights for side in section for a in side]
    return pl.pallas_call(
        functools.partial(weight_body, batch=batch, sides=sides, groups=groups, wide=4),
        in_specs=[SMEM] + [ANY] * (len(flat_left) + len(flat_right)),
        out_specs=[ANY] * len(groups),
        out_shape=[
            jax.ShapeDtypeStruct((4 * blocks, quarter, LANES), bf16) for _, _, blocks in groups
        ],
        scratch_shapes=[
            pltpu.VMEM((batch * rows, columns), bf16),
            pltpu.VMEM((columns, batch * rows), bf16),
            pltpu.VMEM((sides, batch * rows, span), bf16),
            pltpu.VMEM((4 * len(groups), most, quarter, LANES), bf16),
            pltpu.SemaphoreType.DMA((batch,)),
            pltpu.SemaphoreType.DMA((sides, batch)),
            pltpu.SemaphoreType.DMA((4 * len(groups),)),
        ],
        compiler_params=params(),
        cost_estimate=pl.CostEstimate(
            flops=2 * batch * rows * columns * sides * span,
            bytes_accessed=2 * columns * sides * span,
            transcendentals=0,
        ),
        name="weight_gradient",
    )(place, *flat_left, *flat_right)


def settle_body(edge, outer, inner, *rest):
    out = rest[-1]

    @pl.when(edge[0] == 1)
    def _():
        for n in range(outer.shape[0]):
            out[:, head(n)] = outer[n].astype(f32)

    @pl.when(edge[0] == 0)
    def _():
        for n in range(inner.shape[0]):
            out[:, head(n)] = inner[n].astype(f32)


def settle(edge, outer, inner, total, held, number):
    blocks, quarter, _ = outer.shape
    more = [] if held is None else [held]
    return pl.pallas_call(
        settle_body,
        grid=(1,),
        in_specs=[SMEM, whole(outer.shape), whole(inner.shape)] + [ANY] * len(more),
        out_specs=pl.BlockSpec((quarter, blocks * LANES), lambda j: (0, number)),
        out_shape=jax.ShapeDtypeStruct((quarter, total), f32),
        input_output_aliases={3: 0} if more else {},
        compiler_params=params(),
        name="settle",
    )(edge, outer, inner, *more)


def add(a, b):
    return (a.astype(f32) + b.astype(f32)).astype(bf16)


def mixed_states(own, slopes, forward):
    count = lax.axis_size("seq")
    place = lax.axis_index("seq")
    decay = jnp.exp(-slopes * BLK)
    if count != 4:
        gathered = lax.all_gather(own, "seq")
        distance = place - 1 - jnp.arange(count) if forward else jnp.arange(count) - place - 1
        factors = jnp.where(
            distance[:, None] >= 0,
            jnp.exp(-slopes[None, :] * (BLK * jnp.maximum(distance, 0)[:, None]).astype(f32)),
            0.0,
        )
        state = jnp.sum(factors[:, :, None, None] * gathered.astype(f32), axis=0).astype(bf16)
        return state, state, jnp.ones_like(slopes), jnp.zeros_like(slopes)
    late = (place % 2 == 1) if forward else (place % 2 == 0)
    near_state = lax.ppermute(own, "seq", [(0, 1), (1, 0), (2, 3), (3, 2)])
    here, there = own.astype(f32), near_state.astype(f32)
    factor = decay[:, None, None]
    joined = jnp.where(late, factor * there + here, factor * here + there).astype(bf16)
    route = [(0, 2), (1, 3)] if forward else [(2, 0), (3, 1)]
    far_state = lax.ppermute(joined, "seq", route)
    far = jnp.where(late, decay, jnp.ones_like(decay))
    near = jnp.where(late, jnp.ones_like(decay), jnp.zeros_like(decay))
    return far_state, near_state, far, near


def sum_quarters(chunks):
    sums = []
    previous = None
    for chunk in chunks:
        blocks = chunk.shape[0] // 4
        given, kept = chunk[: 2 * blocks], chunk[2 * blocks :]
        taken = lax.ppermute(given, "seq", [(0, 1), (1, 0), (2, 3), (3, 2)])
        far = add(kept[:blocks], taken[:blocks])
        own = add(kept[blocks:], taken[blocks:])
        if previous is not None:
            far, _ = lax.optimization_barrier((far, previous))
        previous = lax.ppermute(far, "seq", [(0, 2), (2, 0), (1, 3), (3, 1)])
        sums.append(add(own, previous))
    return sums


def sum_line(parts):
    place = lax.axis_index("dp")
    edge = (place == 0) | (place == 3)
    count = len(parts)
    partial = [None] * count
    across = [None] * count
    out = []
    for step in range(count + 2):
        part = parts[step] if step < count else None
        done = None
        if step >= 2:
            done = partial[step - 2].astype(f32) + across[step - 2].astype(f32)
        if 1 <= step <= count:
            across[step - 1] = lax.ppermute(partial[step - 1], "dp", [(1, 2), (2, 1)])
        if part is not None and done is not None and part.shape == done.shape:
            sent = jnp.where(edge, part.astype(f32), done).astype(bf16)
            got = lax.ppermute(sent, "dp", [(0, 1), (1, 0), (2, 3), (3, 2)])
            out.append((got, sent))
            partial[step] = add(part, got)
            continue
        if part is not None:
            partial[step] = add(part, lax.ppermute(part, "dp", [(0, 1), (3, 2)]))
        if done is not None:
            done = done.astype(bf16)
            out.append((lax.ppermute(done, "dp", [(1, 0), (2, 3)]), done))
    return out


def sum_any(chunk, place):
    part = lax.psum_scatter(chunk, "seq", scatter_dimension=0, tiled=True)
    part = lax.psum(part, "dp")
    return part


def angle_tables(position_row, half_size):
    frequency = jnp.exp(
        jnp.arange(half_size, dtype=jnp.float32) * (-math.log(theta_base) / half_size)
    )
    angles = position_row.astype(jnp.float32)[..., None] * frequency
    cosine = jnp.cos(angles)
    sine_rows = jnp.sin(angles)
    return (
        jnp.concatenate([cosine, cosine], axis=-1),
        jnp.concatenate([-sine_rows, sine_rows], axis=-1),
    )


def first_half(x, slopes, cosine, sine, w):
    h1, r1, pre, qk, state = project(slopes, x, cosine, sine, w)
    return dict(x=x, h1=h1, r1=r1, pre=pre, qk=qk), mixed_states(state, slopes, True)


def second_half(record, states, slopes, wo, wi, wd):
    far_state, near_state, far, near = states
    mixed, gated, ra, h2, r2, low, g, up, product, y = finish(
        slopes, far, near, record["x"], record["qk"], record["pre"], far_state, near_state,
        wo, wi, wd,
    )
    record.update(
        mixed=mixed, gated=gated, ra=ra, h2=h2, r2=r2, low=low, g=g, up=up, product=product
    )
    return y


def back_first(dy, record, slopes, cosine, sine, wo, wi, wd):
    dg, dup, dmid, dm, dq, du, dk, dv, state = back_channel(
        slopes, dy, record, cosine, sine, wo, wi, wd
    )
    record.update(dy=dy, dg=dg, dup=dup, dmid=dmid, dm=dm, dq=dq, du=du, dk=dk, dv=dv)
    return mixed_states(state, slopes, False)


def back_second(record, states, slopes, cosine, sine, w):
    far_state, near_state, far, near = states
    dkp, dvp, dx = back_mixer(
        slopes, far, near, record["dq"], record["du"], record["dk"], record["dv"], record,
        far_state, near_state, cosine, sine, record["dmid"], w,
    )
    record.update(dkp=dkp, dvp=dvp)
    return dx


def per_device(boundary, positions, decay_exp, mixer_in, mixer_out, channel_in, channel_out):
    section = lax.axis_index("section")
    is_first = section == 0
    own = boundary[0]
    batch, rows, width = own.shape
    assert rows == BLK
    slopes = jnp.exp2(-0.5 * decay_exp[0].astype(jnp.float32))
    w, wo, wi, wd = mixer_in[0], mixer_out[0], channel_in[0], channel_out[0]
    hidden = wd.shape[0]
    half_size = width // HEADS // 2
    cosine, sine = angle_tables(positions, half_size)
    every = range(batch)

    early, states = [None] * batch, [None] * batch
    for b in every:
        early[b], states[b] = first_half(own[b], slopes, cosine[b], sine[b], w)
    arrived = []
    for b in every:
        y = second_half(early[b], states[b], slopes, wo, wi, wd)
        arrived.append(lax.ppermute(y, "section", [(0, 1)]))
    late = [None] * batch
    for b in every:
        late[b], states[b] = first_half(arrived[b], slopes, cosine[b], sine[b], w)
    outputs, later = [None] * batch, [None] * batch
    for b in every:
        outputs[b] = second_half(late[b], states[b], slopes, wo, wi, wd)
        later[b] = back_first(own[b], late[b], slopes, cosine[b], sine[b], wo, wi, wd)
    returned = []
    for b in every:
        dx = back_second(late[b], later[b], slopes, cosine[b], sine[b], w)
        returned.append(lax.ppermute(dx, "section", [(1, 0)]))
    for b in every:
        later[b] = back_first(returned[b], early[b], slopes, cosine[b], sine[b], wo, wi, wd)

    place = lax.axis_index("seq")
    core, y_place = place % 2, place // 2
    roles = [
        2 * (1 - y_place) + 1 - core,
        2 * y_place + 1 - core,
        2 * (1 - y_place) + core,
        2 * y_place + core,
        section,
    ]
    usual = lax.axis_size("seq") == 4 and lax.axis_size("dp") == 4
    if not usual:
        roles = [0, 1, 2, 3, section]
    roles = jnp.stack([jnp.asarray(r, jnp.int32) for r in roles])

    def operands(*names):
        return [[[r[name] for r in records] for name in names] for records in (early, late)]

    def left(name):
        return [side[0] for side in operands(name)]

    def gradient(name, names, groups):
        return weight_gradient(roles, left(name), operands(*names), groups)

    chunks = []
    chunks += gradient("product", ("dy",), [(0, 0, 4), (0, 4, 4)])
    half = hidden // LANES // 2
    chunks += gradient(
        "h2", ("dg", "dup"), [(0, 0, half), (0, half, half), (1, 0, half), (1, half, half)]
    )
    dx = [back_second(early[b], later[b], slopes, cosine[b], sine[b], w) for b in every]
    eight = width // LANES
    chunks += gradient("gated", ("dm",), [(0, 0, eight)])
    chunks += gradient(
        "h1", ("dq", "dkp", "dvp", "du"), [(s, 0, eight) for s in range(4)]
    )
    joined = jnp.where(is_first, jnp.stack(dx), jnp.stack(outputs))[None]

    spans = [(3, width), (3, width)] + [(2, 2 * hidden)] * 4 + [(1, width)] + [(0, 4 * width)] * 4
    order = [0, 1, 0, 1, 2, 3, 0, 0, 1, 2, 3]
    edge = (lax.axis_index("dp") == 0) | (lax.axis_index("dp") == 3)
    if usual:
        shaped = [c.reshape(c.shape[0] * c.shape[1] // 256, 256, LANES) for c in chunks]
        pairs = sum_line(sum_quarters(shaped))
        flag = edge.astype(jnp.int32)[None]
        held = [None] * 4
        for (index, total), number, (outer, inner), chunk in zip(spans, order, pairs, chunks):
            shape = (chunk.shape[0] // 4,) + chunk.shape[1:]
            held[index] = settle(
                flag, outer.reshape(shape), inner.reshape(shape), total, held[index], number
            )
        return (joined, *(h[None] for h in held))
    found = [[], [], [], []]
    for (index, total), chunk in zip(spans, chunks):
        blocks, quarter = chunk.shape[0] // 4, chunk.shape[1]
        rows_first = chunk.reshape(4, blocks, quarter, LANES).transpose(0, 2, 1, 3)
        found[index].append(rows_first.reshape(4 * quarter, blocks * LANES))
    summed = []
    for pieces in found:
        part = lax.psum_scatter(
            jnp.concatenate(pieces, axis=1), "seq", scatter_dimension=0, tiled=True
        )
        summed.append(lax.psum(part, "dp").astype(f32)[None])
    return (joined, *summed)


def solution(mesh):
    in_specs = (
        P("section", "dp", "seq", None),
        P("dp", "seq"),
        P("section", None),
        P("section", None, None),
        P("section", None, None),
        P("section", None, None),
        P("section", None, None),
    )
    out_specs = (
        P("section", "dp", "seq", None),
        P("section", "seq", None),
        P("section", "seq", None),
        P("section", "seq", None),
        P("section", "seq", None),
    )
    return jax.shard_map(
        per_device, mesh=mesh, in_specs=in_specs, out_specs=out_specs, check_vma=False
    )
```

```python
import functools
import math

import jax
import jax.numpy as jnp
from jax import lax
from jax.experimental import pallas as pl
from jax.experimental.pallas import tpu as pltpu
from jax.sharding import PartitionSpec as P

HEADS = 8
BLK = 256
LANES = 128
STEPS = 8

epsilon = 1e-06
theta_base = 10000.0
f32 = jnp.float32
bf16 = jnp.bfloat16


def nn(a, b):
    return jnp.dot(a, b, preferred_element_type=f32)


def nt(a, b):
    return lax.dot_general(a, b, (((1,), (1,)), ((), ())), preferred_element_type=f32)


def tn(a, b):
    return lax.dot_general(a, b, (((0,), (0,)), ((), ())), preferred_element_type=f32)


def sigmoid(v):
    return 1.0 / (1.0 + jnp.exp(-v))


def norm_factor(v, width):
    return lax.rsqrt(jnp.sum(v * v, axis=-1, keepdims=True) * (1.0 / width) + epsilon)


def norm_back(cotangent, normed, factor, width):
    mean = jnp.sum(cotangent * normed, axis=-1, keepdims=True) * (1.0 / width)
    return factor * (cotangent - normed * mean)


def row_index(rows, columns):
    return lax.broadcasted_iota(jnp.int32, (rows, columns), 0).astype(f32)


def decay_mask(slope, rows):
    row = lax.broadcasted_iota(jnp.int32, (rows, rows), 0)
    column = lax.broadcasted_iota(jnp.int32, (rows, rows), 1)
    distance = jnp.maximum(row - column, 0).astype(f32)
    return jnp.where(row >= column, jnp.exp(distance * (-slope)), 0.0)


def head(number):
    return slice(number * LANES, (number + 1) * LANES)


def half_turn(v):
    return pltpu.roll(v, LANES // 2, 1)


def whole(shape):
    return pl.BlockSpec(shape, lambda j: (0,) * len(shape))


def hbm(shape, kind):
    return pltpu.HBM(tuple(shape), kind)


def far_away(*arrays):
    return [pltpu.with_memory_space_constraint(a, pltpu.HBM) for a in arrays]


def close_by(*arrays):
    return [pltpu.with_memory_space_constraint(a, pltpu.VMEM) for a in arrays]


def params(megabytes):
    return pltpu.CompilerParams(vmem_limit_bytes=megabytes * 1024 * 1024)


SMEM = pl.BlockSpec(memory_space=pltpu.SMEM)
ANY = pl.BlockSpec(memory_space=pltpu.HBM)
VMEM = pl.BlockSpec(memory_space=pltpu.VMEM)


def tables(position, rows):
    lane = lax.broadcasted_iota(jnp.int32, (rows, LANES), 1)
    half = LANES // 2
    feature = jnp.where(lane < half, lane, lane - half).astype(f32)
    frequency = jnp.exp(feature * (-math.log(theta_base) / half))
    angle = position * frequency
    return jnp.cos(angle), jnp.where(lane < half, -jnp.sin(angle), jnp.sin(angle))


def project_body(slope, x, cosine, sine, w, h1, r1, pre, qk, state,
                 xv, cv, sv, hv, rv, prev, qkv, stv, isem, osem):
    rows, width = x.shape
    steps = STEPS
    columns = w.shape[1] // steps
    heads = columns // LANES
    first = [
        pltpu.make_async_copy(source, target, isem.at[n])
        for n, (source, target) in enumerate(((x, xv), (cosine, cv), (sine, sv)))
    ]
    for copy in first:
        copy.start()

    first[0].wait()
    v = xv[...].astype(f32)
    factor = norm_factor(v, width)
    hv[...] = (v * factor).astype(bf16)
    rv[...] = jnp.broadcast_to(factor, rv.shape)
    first[1].wait()
    first[2].wait()
    outs = [pltpu.make_async_copy(hv, h1, osem.at[0]), pltpu.make_async_copy(rv, r1, osem.at[1])]
    for copy in outs:
        copy.start()

    def pre_out(j):
        at = pl.ds(pl.multiple_of(j * columns, LANES), columns)
        return pltpu.make_async_copy(prev.at[:, at], pre.at[:, at], osem.at[3 + j])

    def step(j, carry):
        at = pl.multiple_of(j * columns, LANES)
        p = nn(hv[...], w[:, pl.ds(at, columns)])
        prev[:, pl.ds(at, columns)] = p.astype(bf16)
        pre_out(j).start()

        @pl.when(j < steps // 2)
        def _():
            for n in range(heads):
                v = p[:, head(n)]
                v = v * sigmoid(v)
                turned = v * cv[...] + half_turn(v) * sv[...]
                qkv[:, pl.ds(at + n * LANES, LANES)] = turned.astype(bf16)

        @pl.when((j >= steps // 2) & (j < 3 * steps // 4))
        def _():
            values = p.astype(bf16)
            ahead = rows - row_index(rows, LANES)
            for n in range(heads):
                number = (j - steps // 2) * heads + n
                decay = jnp.exp(ahead * (-slope[number]))
                key = qkv[:, pl.ds(at - width + n * LANES, LANES)]
                keyed = (key.astype(f32) * decay).astype(bf16)
                stv[number] = tn(keyed, values[:, head(n)]).astype(bf16)

        return carry

    lax.fori_loop(0, steps, step, 0)
    last = [pltpu.make_async_copy(qkv, qk, osem.at[2]), pltpu.make_async_copy(stv, state, osem.at[11])]
    for copy in last:
        copy.start()
    for copy in outs + last:
        copy.wait()
    for j in range(steps):
        pre_out(j).wait()


def project(slopes, x, cosine, sine, w):
    rows, width = x.shape
    total = w.shape[1]
    states = (HEADS, LANES, LANES)
    return pl.pallas_call(
        project_body,
        in_specs=[SMEM] + [ANY] * 3 + [VMEM],
        out_specs=[ANY] * 5,
        out_shape=[
            hbm((rows, width), bf16),
            hbm((rows, LANES), f32),
            hbm((rows, total), bf16),
            hbm((rows, total // 2), bf16),
            hbm(states, bf16),
        ],
        scratch_shapes=[
            pltpu.VMEM((rows, width), bf16),
            pltpu.VMEM((rows, LANES), f32),
            pltpu.VMEM((rows, LANES), f32),
            pltpu.VMEM((rows, width), bf16),
            pltpu.VMEM((rows, LANES), f32),
            pltpu.VMEM((rows, total), bf16),
            pltpu.VMEM((rows, total // 2), bf16),
            pltpu.VMEM(states, bf16),
            pltpu.SemaphoreType.DMA((3,)),
            pltpu.SemaphoreType.DMA((12,)),
        ],
        compiler_params=params(8),
        cost_estimate=pl.CostEstimate(
            flops=2 * rows * width * total, bytes_accessed=2 * width * total, transcendentals=0
        ),
        name="project",
    )(slopes, *far_away(x, cosine, sine), *close_by(w))


def moves(pairs, sem, start=0):
    return [
        pltpu.make_async_copy(source, target, sem.at[start + n])
        for n, (source, target) in enumerate(pairs)
    ]


def entering_state(factors, states, number):
    state = factors[0, number] * states[number].astype(f32)
    state += factors[1, number] * states[HEADS + number].astype(f32)
    return state.astype(bf16)


def finish_body(
    slope, factors, x, qk, pre, far, near, wo, wi, wd,
    mixed, gated, ra, h2, r2, low, g, up, product, y,
    xv, qkv, vuv, statev, mixedv, gatedv, rav, h2v, r2v, lowv, gv, upv, productv, yv,
    attended, total, held, isem, osem, csem,
):
    rows, width = x.shape
    hidden = wd.shape[0]
    columns = held.shape[1]
    steps = hidden // columns
    ins = moves(
        (
            (qk, qkv), (pre.at[:, pl.ds(2 * width, 2 * width)], vuv),
            (far, statev.at[pl.ds(0, HEADS)]), (near, statev.at[pl.ds(HEADS, HEADS)]), (x, xv),
        ),
        isem,
    )
    for copy in ins:
        copy.start()
    for copy in ins[:4]:
        copy.wait()
    ahead = row_index(rows, LANES)

    def pair(i, carry):
        for m in range(4):
            n = i * 4 + m
            at = pl.multiple_of(n * LANES, LANES)
            lane = pl.ds(at, LANES)
            state = entering_state(factors, statev, n)
            lowv[n] = state
            query = qkv[:, lane]
            key = qkv[:, pl.ds(at + width, LANES)]
            weights = (decay_mask(slope[n], rows) * nt(query, key)).astype(bf16)
            inner = nn(weights, vuv[:, lane])
            carried = nn(query, state)
            attended[:, lane] = inner + jnp.exp(ahead * (-slope[n])) * carried
        return carry

    lax.fori_loop(0, HEADS // 4, pair, 0)
    rows_out = attended[...]
    factor = norm_factor(rows_out, width)
    rav[...] = jnp.broadcast_to(factor, rav.shape)
    normed = rows_out * factor
    mixedv[...] = normed.astype(bf16)
    gatedv[...] = (normed * vuv[:, width:].astype(f32)).astype(bf16)
    outs = moves(((mixedv, mixed), (gatedv, gated), (rav, ra), (lowv, low)), osem)
    for copy in outs:
        copy.start()
    ins[4].wait()
    middle = xv[...].astype(f32) + nn(gatedv[...], wo[...])
    total[...] = middle
    factor = norm_factor(middle, width)
    r2v[...] = jnp.broadcast_to(factor, r2v.shape)
    h2v[...] = (middle * factor).astype(bf16)
    more = moves(((h2v, h2), (r2v, r2)), osem, 4)
    for copy in more:
        copy.start()
    held[...] = jnp.zeros_like(held)

    def chunk_out(i):
        at = pl.ds(pl.multiple_of(i * columns, LANES), columns)
        return [
            pltpu.make_async_copy(source.at[:, at], target.at[:, at], csem.at[n, i])
            for n, (source, target) in enumerate(((gv, g), (upv, up), (productv, product)))
        ]

    def step(i, carry):
        start = pl.multiple_of(i * columns, LANES)
        before = pl.multiple_of(jnp.maximum(i - 1, 0) * columns, LANES)
        at = pl.ds(start, columns)
        total[...] += nn(held[...], wd[pl.ds(before, columns), :])
        gate = nn(h2v[...], wi[:, at])
        rise = nn(h2v[...], wi[:, pl.ds(start + hidden, columns)])
        both = (gate * rise).astype(bf16)
        gv[:, at] = gate.astype(bf16)
        upv[:, at] = rise.astype(bf16)
        productv[:, at] = both
        held[...] = both
        for copy in chunk_out(i):
            copy.start()
        return carry

    lax.fori_loop(0, steps, step, 0)
    yv[...] = (total[...] + nn(held[...], wd[hidden - columns :, :])).astype(bf16)
    last = moves(((yv, y),), osem, 6)
    for copy in last:
        copy.start()
    for copy in outs + more + last:
        copy.wait()

    def drain(i, carry):
        for copy in chunk_out(i):
            copy.wait()
        return carry

    lax.fori_loop(0, steps, drain, 0)


def finish(slopes, factors, x, qk, pre, entering, wo, wi, wd):
    rows, width = x.shape
    hidden = wd.shape[0]
    columns = 256
    steps = hidden // columns
    states = (HEADS, LANES, LANES)
    act = hbm((rows, width), bf16)
    factor = hbm((rows, LANES), f32)
    unit = hbm((rows, hidden), bf16)
    outs = [
        act, act, factor, act, factor, hbm(states, bf16), unit, unit, unit, act,
    ]
    return pl.pallas_call(
        finish_body,
        in_specs=[SMEM] * 2 + [ANY] * 5 + [VMEM] * 3,
        out_specs=[ANY] * len(outs),
        out_shape=outs,
        scratch_shapes=[
            pltpu.VMEM((rows, width), bf16),
            pltpu.VMEM((rows, 2 * width), bf16),
            pltpu.VMEM((rows, 2 * width), bf16),
            pltpu.VMEM((2 * HEADS, LANES, LANES), bf16),
        ]
        + [pltpu.VMEM(o.shape, o.dtype) for o in outs]
        + [
            pltpu.VMEM((rows, width), f32),
            pltpu.VMEM((rows, width), f32),
            pltpu.VMEM((rows, columns), bf16),
            pltpu.SemaphoreType.DMA((5,)),
            pltpu.SemaphoreType.DMA((7,)),
            pltpu.SemaphoreType.DMA((3, steps)),
        ],
        compiler_params=params(18),
        cost_estimate=pl.CostEstimate(
            flops=2 * rows * width * (width + 3 * hidden),
            bytes_accessed=2 * width * (width + 3 * hidden),
            transcendentals=0,
        ),
        name="finish",
    )(slopes, factors, *far_away(x, qk, pre, *entering), *close_by(wo, wi, wd))


def back_channel_body(
    slope, dy, wo, wi, wd, g, up, h2, r2, mixed, ra, qk, pre, low, cosine, sine,
    dg, dup, dmid, dm, dq, du, dk, dv, state,
    dyv, gv, upv, h2v, r2v, mixedv, rav, qkv, qpv, vuv, lowv, cv, sv,
    dgv, dupv, dmidv, dmv, dqv, duv, dkv, dvv, statev,
    total, datt, heldg, heldu, isem, osem, csem,
):
    rows, width = dy.shape
    hidden = wd.shape[0]
    columns = heldg.shape[1]
    steps = hidden // columns
    ins = moves(
        (
            (dy, dyv), (g, gv), (up, upv), (h2, h2v), (r2, r2v), (mixed, mixedv), (ra, rav),
            (qk, qkv), (pre.at[:, pl.ds(0, width)], qpv),
            (pre.at[:, pl.ds(2 * width, 2 * width)], vuv), (low, lowv), (cosine, cv), (sine, sv),
        ),
        isem,
    )
    for copy in ins:
        copy.start()
    for copy in ins[:3]:
        copy.wait()
    heldg[...] = jnp.zeros_like(heldg)
    heldu[...] = jnp.zeros_like(heldu)
    total[...] = jnp.zeros_like(total)

    def chunk_out(i):
        at = pl.ds(pl.multiple_of(i * columns, LANES), columns)
        return [
            pltpu.make_async_copy(source.at[:, at], target.at[:, at], csem.at[n, i])
            for n, (source, target) in enumerate(((dgv, dg), (dupv, dup)))
        ]

    def step(i, carry):
        at = pl.ds(pl.multiple_of(i * columns, LANES), columns)
        before = pl.multiple_of(jnp.maximum(i - 1, 0) * columns, LANES)
        total[...] += nt(heldg[...], wi[:, pl.ds(before, columns)]) + nt(
            heldu[...], wi[:, pl.ds(before + hidden, columns)]
        )
        product = nt(dyv[...], wd[at, :])
        left = (product * upv[:, at].astype(f32)).astype(bf16)
        right = (product * gv[:, at].astype(f32)).astype(bf16)
        dgv[:, at] = left
        dupv[:, at] = right
        heldg[...] = left
        heldu[...] = right
        for copy in chunk_out(i):
            copy.start()
        return carry

    lax.fori_loop(0, steps, step, 0)
    for copy in ins[3:]:
        copy.wait()
    dh2 = (
        total[...]
        + nt(heldg[...], wi[:, hidden - columns : hidden])
        + nt(heldu[...], wi[:, 2 * hidden - columns :])
    )
    middle = dyv[...].astype(f32) + norm_back(dh2, h2v[...].astype(f32), r2v[:, 0:1], width)
    dmidv[...] = middle
    dmv[...] = middle.astype(bf16)
    outs = moves(((dmidv, dmid), (dmv, dm)), osem)
    for copy in outs:
        copy.start()
    dgated = nt(dmv[...], wo[...])
    normed = mixedv[...].astype(f32)
    duv[...] = (dgated * normed).astype(bf16)
    back = norm_back(dgated * vuv[:, width:].astype(f32), normed, rav[:, 0:1], width)
    datt[...] = back.astype(bf16)
    ahead = row_index(rows, LANES)
    row = lax.broadcasted_iota(jnp.int32, (rows, rows), 0)
    column = lax.broadcasted_iota(jnp.int32, (rows, rows), 1)
    distance = (row - column).astype(f32)

    def some(i, carry):
        for m in range(2):
            n = i * 2 + m
            at = pl.multiple_of(n * LANES, LANES)
            lane = pl.ds(at, LANES)
            query, key = qkv[:, lane], qkv[:, pl.ds(at + width, LANES)]
            value, cot = vuv[:, lane], datt[:, lane]
            power = jnp.exp(jnp.abs(distance) * (-slope[n]))
            mask = jnp.where(distance >= 0.0, power, 0.0)
            flipped = jnp.where(distance <= 0.0, power, 0.0)
            weights_t = (flipped * nt(key, query)).astype(bf16)
            scores = (mask * nt(cot, value)).astype(bf16)
            scores_t = (flipped * nt(value, cot)).astype(bf16)
            scaled = (jnp.exp(ahead * (-slope[n])) * cot.astype(f32)).astype(bf16)
            statev[n] = tn(query, scaled).astype(bf16)
            dquery = nn(scores, key) + nt(scaled, lowv[n])
            turned = dquery * cv[...] + half_turn(dquery * sv[...])
            p = qpv[:, lane].astype(f32)
            s = sigmoid(p)
            dqv[:, lane] = (turned * (s * (1.0 + p * (1.0 - s)))).astype(bf16)
            dkv[:, lane] = nn(scores_t, query)
            dvv[:, lane] = nn(weights_t, cot)
        return carry

    lax.fori_loop(0, HEADS // 2, some, 0)
    last = moves(((statev, state), (dqv, dq), (duv, du), (dkv, dk), (dvv, dv)), osem, 2)
    for copy in last:
        copy.start()
    for copy in outs + last:
        copy.wait()

    def drain(i, carry):
        for copy in chunk_out(i):
            copy.wait()
        return carry

    lax.fori_loop(0, steps, drain, 0)


def back_channel(slopes, dy, r, cosine, sine, wo, wi, wd):
    rows, width = dy.shape
    hidden = wd.shape[0]
    columns = 256
    steps = hidden // columns
    states = (HEADS, LANES, LANES)
    act = hbm((rows, width), bf16)
    full = hbm((rows, width), f32)
    unit = hbm((rows, hidden), bf16)
    outs = [unit, unit, full, act, act, act, full, full, hbm(states, bf16)]
    wide = pltpu.VMEM((rows, width), bf16)
    thin = pltpu.VMEM((rows, LANES), f32)
    twice = pltpu.VMEM((rows, 2 * width), bf16)
    tall = pltpu.VMEM((rows, hidden), bf16)
    return pl.pallas_call(
        back_channel_body,
        in_specs=[SMEM] + [ANY] + [VMEM] * 3 + [ANY] * 11,
        out_specs=[ANY] * len(outs),
        out_shape=outs,
        scratch_shapes=[
            wide, tall, tall, wide, thin, wide, thin, twice, wide, twice,
            pltpu.VMEM(states, bf16), thin, thin,
        ]
        + [pltpu.VMEM(o.shape, o.dtype) for o in outs]
        + [
            pltpu.VMEM((rows, width), f32),
            wide,
            pltpu.VMEM((rows, columns), bf16),
            pltpu.VMEM((rows, columns), bf16),
            pltpu.SemaphoreType.DMA((13,)),
            pltpu.SemaphoreType.DMA((7,)),
            pltpu.SemaphoreType.DMA((2, steps)),
        ],
        compiler_params=params(22),
        cost_estimate=pl.CostEstimate(
            flops=2 * rows * width * (width + 3 * hidden),
            bytes_accessed=2 * width * (width + 3 * hidden),
            transcendentals=0,
        ),
        name="back_channel",
    )(
        slopes, *far_away(dy), *close_by(wo, wi, wd),
        *far_away(
            r["g"], r["up"], r["h2"], r["r2"], r["mixed"], r["ra"], r["qk"], r["pre"], r["low"],
            cosine, sine,
        ),
    )


def back_mixer_body(
    slope, factors, dq, du, dk, dv, qk, pre, far, near, cosine, sine, h1, r1, dmid, w,
    dkp, dvp, dx,
    dkin, dvin, kvv, kpv, vv, statev, cv, sv, h1v, r1v, dmidv, parts, dxv, isem, osem,
):
    rows, width = dq.shape
    ins = moves(
        (
            (dk, dkin), (dv, dvin), (qk.at[:, pl.ds(width, width)], kvv),
            (pre.at[:, pl.ds(width, width)], kpv), (pre.at[:, pl.ds(2 * width, width)], vv),
            (far, statev.at[pl.ds(0, HEADS)]), (near, statev.at[pl.ds(HEADS, HEADS)]),
            (cosine, cv), (sine, sv),
            (dq, parts.at[:, pl.ds(0, width)]), (du, parts.at[:, pl.ds(3 * width, width)]),
            (h1, h1v), (r1, r1v), (dmid, dmidv),
        ),
        isem,
    )
    for copy in ins:
        copy.start()
    for copy in ins[:9]:
        copy.wait()
    ahead = rows - row_index(rows, LANES)

    def some(i, carry):
        for m in range(4):
            n = i * 4 + m
            at = pl.multiple_of(n * LANES, LANES)
            lane = pl.ds(at, LANES)
            state = entering_state(factors, statev, n)
            decay = jnp.exp(ahead * (-slope[n]))
            keyed = (kvv[:, lane].astype(f32) * decay).astype(bf16)
            dkey = dkin[:, lane] + decay * nt(vv[:, lane], state)
            turned = dkey * cv[...] + half_turn(dkey * sv[...])
            p = kpv[:, lane].astype(f32)
            s = sigmoid(p)
            parts[:, pl.ds(at + width, LANES)] = (turned * (s * (1.0 + p * (1.0 - s)))).astype(bf16)
            parts[:, pl.ds(at + 2 * width, LANES)] = (dvin[:, lane] + nn(keyed, state)).astype(bf16)
        return carry

    lax.fori_loop(0, HEADS // 4, some, 0)
    outs = moves(
        ((parts.at[:, pl.ds(width, width)], dkp), (parts.at[:, pl.ds(2 * width, width)], dvp)), osem
    )
    for copy in outs:
        copy.start()
    for copy in ins[9:]:
        copy.wait()
    total = nt(parts[...], w[...])
    back = norm_back(total, h1v[...].astype(f32), r1v[:, 0:1], width)
    dxv[...] = (dmidv[...] + back).astype(bf16)
    last = moves(((dxv, dx),), osem, 2)
    for copy in last:
        copy.start()
    for copy in outs + last:
        copy.wait()


def back_mixer(slopes, factors, r, entering, cosine, sine, w):
    rows, width = r["dq"].shape
    act = hbm((rows, width), bf16)
    wide = pltpu.VMEM((rows, width), bf16)
    full = pltpu.VMEM((rows, width), f32)
    thin = pltpu.VMEM((rows, LANES), f32)
    return pl.pallas_call(
        back_mixer_body,
        in_specs=[SMEM] * 2 + [ANY] * 13 + [VMEM],
        out_specs=[ANY] * 3,
        out_shape=[act, act, act],
        scratch_shapes=[
            full, full, wide, wide, wide, pltpu.VMEM((2 * HEADS, LANES, LANES), bf16), thin, thin,
            wide, thin,
            full,
            pltpu.VMEM((rows, w.shape[1]), bf16), wide,
            pltpu.SemaphoreType.DMA((14,)),
            pltpu.SemaphoreType.DMA((3,)),
        ],
        compiler_params=params(14),
        cost_estimate=pl.CostEstimate(
            flops=2 * rows * width * w.shape[1],
            bytes_accessed=2 * width * w.shape[1],
            transcendentals=0,
        ),
        name="back_mixer",
    )(
        slopes, factors,
        *far_away(
            r["dq"], r["du"], r["dk"], r["dv"], r["qk"], r["pre"], *entering, cosine, sine,
            r["h1"], r["r1"], r["dmid"],
        ),
        *close_by(w),
    )


def weight_body(*refs, batch, sides, groups):
    place = refs[0]
    lefts = refs[1 : 1 + 2 * batch]
    rights = refs[1 + 2 * batch : 1 + 2 * batch + 2 * batch * sides]
    outs = refs[1 + 2 * batch + 2 * batch * sides : -7]
    x, xt, ys, stage, xsem, ysem, osem = refs[-7:]
    rows = lefts[0].shape[0]
    columns = x.shape[1]
    quarter = columns // 4
    blocks = groups[0][2]

    def left_copies(section):
        return [
            pltpu.make_async_copy(
                lefts[section * batch + b], x.at[pl.ds(b * rows, rows)], xsem.at[b]
            )
            for b in range(batch)
        ]

    def right_copies(section, s):
        return [
            pltpu.make_async_copy(
                rights[(section * sides + s) * batch + b],
                ys.at[s, pl.ds(b * rows, rows)],
                ysem.at[s, b],
            )
            for b in range(batch)
        ]

    for section in range(2):

        @pl.when(place[4] == section)
        def _():
            for copy in left_copies(section):
                copy.start()
            for s in range(sides):
                for copy in right_copies(section, s):
                    copy.start()

    for copy in left_copies(0):
        copy.wait()
    for piece in range(columns // LANES):
        xt[piece * LANES : (piece + 1) * LANES, :] = x[:, piece * LANES : (piece + 1) * LANES].T

    def move(number, role, out):
        slot = number * 4 + role
        return pltpu.make_async_copy(
            stage.at[slot], out.at[pl.ds((role % 2) * blocks, blocks)], osem.at[slot]
        )

    def one(role, number, side, start):
        left = xt[pl.ds(pl.multiple_of(place[role] * quarter, 16), quarter), :]
        tile = nn(left, ys[side, :, start * LANES : (start + blocks) * LANES]).astype(bf16)
        for n in range(blocks):
            stage[number * 4 + role, n] = tile[:, head(n)]

    for number, (side, start, _) in enumerate(groups):
        if all(side != done for done, _, _ in groups[:number]):
            for copy in right_copies(0, side):
                copy.wait()

        def step(role, carry, number=number, side=side, start=start):
            one(role, number, side, start)

            @pl.when(role < 2)
            def _():
                move(number, role, outs[2 * number]).start()

            @pl.when(role >= 2)
            def _():
                move(number, role, outs[2 * number + 1]).start()

            return carry

        lax.fori_loop(0, 4, step, 0)
    for number in range(len(groups)):
        for role in range(4):
            move(number, role, outs[2 * number + role // 2]).wait()


def weight_gradient(place, lefts, rights, groups):
    batch = len(lefts[0])
    sides = len(rights[0])
    rows, columns = lefts[0][0].shape
    span = rights[0][0][0].shape[1]
    quarter = columns // 4
    blocks = groups[0][2]
    flat_left = [a for section in lefts for a in section]
    flat_right = [a for section in rights for side in section for a in side]
    out = pl.pallas_call(
        functools.partial(weight_body, batch=batch, sides=sides, groups=groups),
        in_specs=[SMEM] + [ANY] * (len(flat_left) + len(flat_right)),
        out_specs=[ANY] * (2 * len(groups)),
        out_shape=[hbm((2 * blocks, quarter, LANES), bf16)] * (2 * len(groups)),
        scratch_shapes=[
            pltpu.VMEM((batch * rows, columns), bf16),
            pltpu.VMEM((columns, batch * rows), bf16),
            pltpu.VMEM((sides, batch * rows, span), bf16),
            pltpu.VMEM((4 * len(groups), blocks, quarter, LANES), bf16),
            pltpu.SemaphoreType.DMA((batch,)),
            pltpu.SemaphoreType.DMA((sides, batch)),
            pltpu.SemaphoreType.DMA((4 * len(groups),)),
        ],
        compiler_params=params(24),
        cost_estimate=pl.CostEstimate(
            flops=2 * batch * rows * columns * sides * span,
            bytes_accessed=2 * columns * sides * span,
            transcendentals=0,
        ),
        name="weight_gradient",
    )(place, *far_away(*flat_left, *flat_right))
    return [(out[2 * n], out[2 * n + 1]) for n in range(len(groups))]


def settle_body(edge, outer, inner, *rest):
    out = rest[-1]

    @pl.when(edge[0] == 1)
    def _():
        for n in range(outer.shape[0]):
            out[:, head(n)] = outer[n].astype(f32)

    @pl.when(edge[0] == 0)
    def _():
        for n in range(inner.shape[0]):
            out[:, head(n)] = inner[n].astype(f32)


def settle(edge, outer, inner, total, held, number):
    blocks, quarter, _ = outer.shape
    more = [] if held is None else [held]
    return pl.pallas_call(
        settle_body,
        grid=(1,),
        in_specs=[SMEM, whole(outer.shape), whole(inner.shape)] + [ANY] * len(more),
        out_specs=pl.BlockSpec((quarter, blocks * LANES), lambda j: (0, number)),
        out_shape=hbm((quarter, total), f32),
        input_output_aliases={3: 0} if more else {},
        compiler_params=params(8),
        name="settle",
    )(edge, outer, inner, *more)


def add(a, b):
    return (a.astype(f32) + b.astype(f32)).astype(bf16)


def state_factors(slopes, forward):
    if lax.axis_size("seq") != 4:
        return jnp.stack([jnp.ones_like(slopes), jnp.zeros_like(slopes)])
    place = lax.axis_index("seq")
    second = (place % 2 == 1) if forward else (place % 2 == 0)
    decay = jnp.exp(-slopes * BLK)
    one = jnp.ones_like(slopes)
    return jnp.stack([jnp.where(second, decay, one), jnp.where(second, one, 0.0 * one)])


def join_factors(slopes, forward):
    place = lax.axis_index("seq")
    second = (place % 2 == 1) if forward else (place % 2 == 0)
    decay = jnp.exp(-slopes * BLK)
    one = jnp.ones_like(slopes)
    return jnp.stack([jnp.where(second, one, decay), jnp.where(second, decay, one)])


def entering_parts(own, slopes, factors, forward):
    count = lax.axis_size("seq")
    if count != 4:
        place = lax.axis_index("seq")
        gathered = lax.all_gather(own, "seq").astype(f32)
        device = jnp.arange(count)
        distance = place - 1 - device if forward else device - place - 1
        power = jnp.maximum(distance, 0).astype(f32) * BLK
        weight = jnp.where(distance[:, None] >= 0, jnp.exp(-slopes[None] * power[:, None]), 0.0)
        state = jnp.sum(weight[:, :, None, None] * gathered, axis=0).astype(bf16)
        return (state, state), state
    near = lax.ppermute(own, "seq", [(0, 1), (1, 0), (2, 3), (3, 2)])
    mine, other = factors[0][:, None, None], factors[1][:, None, None]
    joined = (mine * own.astype(f32) + other * near.astype(f32)).astype(bf16)
    far = lax.ppermute(joined, "seq", [(0, 2), (1, 3)] if forward else [(2, 0), (3, 1)])
    return (far, near), joined


class Sums:
    def __init__(self, edge, settled):
        self.edge = edge
        self.settled = settled
        self.waiting, self.parts, self.partial, self.across = [], [], [], []
        self.previous = None
        self.step = 0
        self.marks = []
        self.written = None

    def load(self, chunks):
        for given, kept in chunks:
            blocks = given.shape[0] // 2
            taken = lax.ppermute(given, "seq", [(0, 1), (1, 0), (2, 3), (3, 2)])
            self.waiting.append(
                (add(kept[:blocks], taken[:blocks]), add(kept[blocks:], taken[blocks:]))
            )

    def over_y(self):
        if not self.waiting:
            return
        far, own = self.waiting.pop(0)
        if self.previous is not None:
            far, _ = lax.optimization_barrier((far, self.previous))
        self.marks.append(far)
        self.previous = lax.ppermute(far, "seq", [(0, 2), (2, 0), (1, 3), (3, 1)])
        self.parts.append(add(own, self.previous))

    def over_z(self, last=False):
        step, count = self.step, len(self.parts)
        if step >= count + 2 or (step >= count and not last):
            return False
        part = self.parts[step] if step < count else None
        done = None
        if step >= 2:
            done = self.partial[step - 2].astype(f32) + self.across[step - 2].astype(f32)
        if part is not None and self.written is not None:
            part, _ = lax.optimization_barrier((part, self.written))
            self.written = None
        if 1 <= step <= count:
            self.marks.append(self.partial[step - 1])
            self.across.append(lax.ppermute(self.partial[step - 1], "dp", [(1, 2), (2, 1)]))
        if part is not None and done is not None and part.shape == done.shape:
            sent = jnp.where(self.edge, part.astype(f32), done).astype(bf16)
            self.marks.append(sent)
            got = lax.ppermute(sent, "dp", [(0, 1), (1, 0), (2, 3), (3, 2)])
            self.partial.append(add(part, got))
            self.written = self.settled(got, sent)
        else:
            if part is not None:
                self.marks.append(part)
                self.partial.append(add(part, lax.ppermute(part, "dp", [(0, 1), (3, 2)])))
            if done is not None:
                done = done.astype(bf16)
                self.marks.append(done)
                self.written = self.settled(lax.ppermute(done, "dp", [(1, 0), (2, 3)]), done)
        self.step += 1
        return True

    def started(self):
        marks, self.marks = self.marks, []
        return marks


def angle_tables(position_row, half_size):
    frequency = jnp.exp(
        jnp.arange(half_size, dtype=jnp.float32) * (-math.log(theta_base) / half_size)
    )
    angles = position_row.astype(jnp.float32)[..., None] * frequency
    cosine = jnp.cos(angles)
    sine_rows = jnp.sin(angles)
    return (
        jnp.concatenate([cosine, cosine], axis=-1),
        jnp.concatenate([-sine_rows, sine_rows], axis=-1),
    )


class Order:
    def __init__(self):
        self.last = []

    def after(self, value):
        if self.last:
            value = lax.optimization_barrier((value, *self.last))[0]
        return value

    def at(self, *values):
        self.last = list(values)


def first_half(order, x, shared, cosine, sine, w):
    h1, r1, pre, qk, state = project(order.after(shared[0]), x, cosine, sine, w)
    entering, joined = entering_parts(state, shared[0], shared[3], True)
    order.at(r1, joined)
    return dict(x=x, h1=h1, r1=r1, pre=pre, qk=qk), entering


def second_half(order, record, entering, shared, wo, wi, wd):
    mixed, gated, ra, h2, r2, low, g, up, product, y = finish(
        order.after(shared[0]), shared[1], record["x"], record["qk"], record["pre"], entering,
        wo, wi, wd,
    )
    order.at(ra)
    record.update(
        mixed=mixed, gated=gated, ra=ra, h2=h2, r2=r2, low=low, g=g, up=up, product=product
    )
    return y


def back_first(order, dy, record, shared, cosine, sine, wo, wi, wd):
    dg, dup, dmid, dm, dq, du, dk, dv, state = back_channel(
        order.after(shared[0]), dy, record, cosine, sine, wo, wi, wd
    )
    entering, joined = entering_parts(state, shared[0], shared[4], False)
    order.at(dm, joined)
    record.update(dy=dy, dg=dg, dup=dup, dmid=dmid, dm=dm, dq=dq, du=du, dk=dk, dv=dv)
    return entering


def back_second(order, record, entering, shared, cosine, sine, w):
    dkp, dvp, dx = back_mixer(
        order.after(shared[0]), shared[2], record, entering, cosine, sine, w
    )
    order.at(dkp)
    record.update(dkp=dkp, dvp=dvp)
    return dx


def per_device(boundary, positions, decay_exp, mixer_in, mixer_out, channel_in, channel_out):
    section = lax.axis_index("section")
    is_first = section == 0
    own = boundary[0]
    batch, rows, width = own.shape
    assert rows == BLK
    slopes = jnp.exp2(-0.5 * decay_exp[0].astype(jnp.float32))
    w, wo, wi, wd = mixer_in[0], mixer_out[0], channel_in[0], channel_out[0]
    hidden = wd.shape[0]
    half_size = width // HEADS // 2
    cosine, sine = angle_tables(positions, half_size)
    every = range(batch)
    usual = lax.axis_size("seq") == 4 and lax.axis_size("dp") == 4

    place, line = lax.axis_index("seq"), lax.axis_index("dp")
    core, y_place = place % 2, place // 2
    roles = [
        2 * (1 - y_place) + 1 - core,
        2 * y_place + 1 - core,
        2 * (1 - y_place) + core,
        2 * y_place + core,
    ]
    if not usual:
        roles = [0, 1, 2, 3]
    roles = jnp.stack([jnp.asarray(r, jnp.int32) for r in (*roles, section)])
    edge = (line == 0) | (line == lax.axis_size("dp") - 1)
    flag = edge.astype(jnp.int32)[None]
    shared = [
        slopes, state_factors(slopes, True), state_factors(slopes, False),
        join_factors(slopes, True), join_factors(slopes, False),
    ]
    own, roles, flag, *shared = lax.optimization_barrier((own, roles, flag, *shared))
    edge = flag[0] == 1
    order = Order()

    early, states = [None] * batch, [None] * batch
    for b in every:
        early[b], states[b] = first_half(order, own[b], shared, cosine[b], sine[b], w)
    arrived = []
    for b in every:
        y = second_half(order, early[b], states[b], shared, wo, wi, wd)
        arrived.append(lax.ppermute(y, "section", [(0, 1)]))
    late = [None] * batch
    for b in every:
        late[b], states[b] = first_half(order, arrived[b], shared, cosine[b], sine[b], w)
    outputs, later = [None] * batch, [None] * batch
    for b in every:
        outputs[b] = second_half(order, late[b], states[b], shared, wo, wi, wd)
        later[b] = back_first(order, own[b], late[b], shared, cosine[b], sine[b], wo, wi, wd)
    returned = []
    for b in every:
        dx = back_second(order, late[b], later[b], shared, cosine[b], sine[b], w)
        returned.append(lax.ppermute(dx, "section", [(1, 0)]))

    def operands(*names):
        return [[[r[name] for r in records] for name in names] for records in (early, late)]

    chunks = []
    spans = [(3, width), (3, width)] + [(2, 2 * hidden)] * 4 + [(1, width)] + [(0, 4 * width)] * 4
    numbers = [0, 1, 0, 1, 2, 3, 0, 0, 1, 2, 3]
    held = [None] * 4
    finished = []

    def settled(outer, inner):
        number = len(finished)
        index, total = spans[number]
        blocks, quarter = chunks[number][0].shape[0] // 2, chunks[number][0].shape[1]
        shape = (blocks, quarter, LANES)
        finished.append(number)
        held[index] = settle(
            flag, outer.reshape(shape), inner.reshape(shape), total, held[index], numbers[number]
        )
        return held[index]

    sums = Sums(edge, settled)

    def even(array):
        return array.reshape(array.shape[0] * array.shape[1] // 256, 256, LANES)

    def gradient(name, names, groups):
        left = [side[0] for side in operands(name)]
        found = weight_gradient(order.after(roles), left, operands(*names), groups)
        order.at(found[-1][1])
        chunks.extend(found)
        if usual:
            sums.load([(even(given), even(kept)) for given, kept in found])

    def move(*what):
        if not usual:
            return
        for way in what:
            way()
        order.at(*order.last, *sums.started())

    def first(b):
        return back_first(order, returned[b], early[b], shared, cosine[b], sine[b], wo, wi, wd)

    def second(b):
        return back_second(order, early[b], later[b], shared, cosine[b], sine[b], w)

    later = [first(b) for b in every[:-1]]
    for b in every:
        early[b]["dy"] = returned[b]
    gradient("product", ("dy",), [(0, 0, 4), (0, 4, 4)])
    move(sums.over_y)
    later.append(first(batch - 1))
    move(sums.over_y, sums.over_z)
    half = hidden // LANES // 2
    gradient("h2", ("dg", "dup"), [(0, 0, half), (0, half, half), (1, 0, half), (1, half, half)])
    move(sums.over_y, sums.over_z)
    dx = [second(b) for b in every]
    move(sums.over_y, sums.over_z)
    eight = width // LANES
    gradient("gated", ("dm",), [(0, 0, eight)])
    gradient("h1", ("dq", "dkp", "dvp", "du"), [(s, 0, eight) for s in range(4)])
    joined = jnp.where(is_first, jnp.stack(dx), jnp.stack(outputs))[None]
    if usual:
        while sums.waiting:
            move(sums.over_y, sums.over_z)
        while sums.over_z(last=True):
            pass
        return (joined, *(h[None] for h in held))
    found = [[], [], [], []]
    for (index, total), chunk in zip(spans, chunks):
        chunk = jnp.concatenate(chunk)
        blocks, quarter = chunk.shape[0] // 4, chunk.shape[1]
        rows_first = chunk.reshape(4, blocks, quarter, LANES).transpose(0, 2, 1, 3)
        found[index].append(rows_first.reshape(4 * quarter, blocks * LANES))
    summed = []
    for pieces in found:
        part = lax.psum_scatter(
            jnp.concatenate(pieces, axis=1), "seq", scatter_dimension=0, tiled=True
        )
        summed.append(lax.psum(part, "dp").astype(f32)[None])
    return (joined, *summed)


def solution(mesh):
    in_specs = (
        P("section", "dp", "seq", None),
        P("dp", "seq"),
        P("section", None),
        P("section", None, None),
        P("section", None, None),
        P("section", None, None),
        P("section", None, None),
    )
    out_specs = (
        P("section", "dp", "seq", None),
        P("section", "seq", None),
        P("section", "seq", None),
        P("section", "seq", None),
        P("section", "seq", None),
    )
    return jax.shard_map(
        per_device, mesh=mesh, in_specs=in_specs, out_specs=out_specs, check_vma=False
    )
```

```python
import functools
import math

import jax
import jax.numpy as jnp
from jax import lax
from jax.experimental import pallas as pl
from jax.experimental.pallas import tpu as pltpu
from jax.sharding import PartitionSpec as P

HEADS = 8
BLK = 256
LANES = 128
STEPS = 8

epsilon = 1e-06
theta_base = 10000.0
f32 = jnp.float32
bf16 = jnp.bfloat16


def nn(a, b):
    return jnp.dot(a, b, preferred_element_type=f32)


def nt(a, b):
    return lax.dot_general(a, b, (((1,), (1,)), ((), ())), preferred_element_type=f32)


def tn(a, b):
    return lax.dot_general(a, b, (((0,), (0,)), ((), ())), preferred_element_type=f32)


def sigmoid(v):
    return 1.0 / (1.0 + jnp.exp(-v))


def norm_factor(v, width):
    return lax.rsqrt(jnp.sum(v * v, axis=-1, keepdims=True) * (1.0 / width) + epsilon)


def norm_back(cotangent, normed, factor, width):
    mean = jnp.sum(cotangent * normed, axis=-1, keepdims=True) * (1.0 / width)
    return factor * (cotangent - normed * mean)


def row_index(rows, columns):
    return lax.broadcasted_iota(jnp.int32, (rows, columns), 0).astype(f32)


def decay_mask(slope, rows):
    row = lax.broadcasted_iota(jnp.int32, (rows, rows), 0)
    column = lax.broadcasted_iota(jnp.int32, (rows, rows), 1)
    distance = jnp.maximum(row - column, 0).astype(f32)
    return jnp.where(row >= column, jnp.exp(distance * (-slope)), 0.0)


def head(number):
    return slice(number * LANES, (number + 1) * LANES)


def half_turn(v):
    return pltpu.roll(v, LANES // 2, 1)


def whole(shape):
    return pl.BlockSpec(shape, lambda j: (0,) * len(shape))


def hbm(shape, kind):
    return pltpu.HBM(tuple(shape), kind)


def far_away(*arrays):
    return [pltpu.with_memory_space_constraint(a, pltpu.HBM) for a in arrays]


def close_by(*arrays):
    return [pltpu.with_memory_space_constraint(a, pltpu.VMEM) for a in arrays]


def params(megabytes):
    return pltpu.CompilerParams(vmem_limit_bytes=megabytes * 1024 * 1024)


SMEM = pl.BlockSpec(memory_space=pltpu.SMEM)
ANY = pl.BlockSpec(memory_space=pltpu.HBM)
VMEM = pl.BlockSpec(memory_space=pltpu.VMEM)


def tables(position, rows):
    lane = lax.broadcasted_iota(jnp.int32, (rows, LANES), 1)
    half = LANES // 2
    feature = jnp.where(lane < half, lane, lane - half).astype(f32)
    frequency = jnp.exp(feature * (-math.log(theta_base) / half))
    angle = position * frequency
    return jnp.cos(angle), jnp.where(lane < half, -jnp.sin(angle), jnp.sin(angle))


def join(slope, before, own):
    decay = jnp.exp(jnp.full((LANES, LANES), -BLK, f32) * slope)
    return (decay * before.astype(f32) + own).astype(bf16)


def project_body(slope, x, cosine, sine, before, w, h1, r1, pre, qk, state, joined,
                 xv, cv, sv, bv, hv, rv, prev, qkv, stv, jv, isem, osem):
    rows, width = x.shape
    steps = STEPS
    columns = w.shape[1] // steps
    heads = columns // LANES
    first = [
        pltpu.make_async_copy(source, target, isem.at[n])
        for n, (source, target) in enumerate(((x, xv), (cosine, cv), (sine, sv), (before, bv)))
    ]
    for copy in first:
        copy.start()

    first[0].wait()
    v = xv[...].astype(f32)
    factor = norm_factor(v, width)
    hv[...] = (v * factor).astype(bf16)
    rv[...] = jnp.broadcast_to(factor, rv.shape)
    for copy in first[1:]:
        copy.wait()
    outs = [pltpu.make_async_copy(hv, h1, osem.at[0]), pltpu.make_async_copy(rv, r1, osem.at[1])]
    for copy in outs:
        copy.start()

    def pre_out(j):
        at = pl.ds(pl.multiple_of(j * columns, LANES), columns)
        return pltpu.make_async_copy(prev.at[:, at], pre.at[:, at], osem.at[3 + j])

    def step(j, carry):
        at = pl.multiple_of(j * columns, LANES)
        p = nn(hv[...], w[:, pl.ds(at, columns)])
        prev[:, pl.ds(at, columns)] = p.astype(bf16)
        pre_out(j).start()

        @pl.when(j < steps // 2)
        def _():
            for n in range(heads):
                v = p[:, head(n)]
                v = v * sigmoid(v)
                turned = v * cv[...] + half_turn(v) * sv[...]
                qkv[:, pl.ds(at + n * LANES, LANES)] = turned.astype(bf16)

        @pl.when((j >= steps // 2) & (j < 3 * steps // 4))
        def _():
            values = p.astype(bf16)
            ahead = rows - row_index(rows, LANES)
            for n in range(heads):
                number = (j - steps // 2) * heads + n
                decay = jnp.exp(ahead * (-slope[number]))
                key = qkv[:, pl.ds(at - width + n * LANES, LANES)]
                keyed = (key.astype(f32) * decay).astype(bf16)
                own = tn(keyed, values[:, head(n)])
                stv[number] = own.astype(bf16)
                jv[number] = join(slope[number], bv[number], own)

        return carry

    lax.fori_loop(0, steps, step, 0)
    last = [
        pltpu.make_async_copy(qkv, qk, osem.at[2]),
        pltpu.make_async_copy(stv, state, osem.at[11]),
        pltpu.make_async_copy(jv, joined, osem.at[12]),
    ]
    for copy in last:
        copy.start()
    for copy in outs + last:
        copy.wait()
    for j in range(steps):
        pre_out(j).wait()


def project(slopes, x, cosine, sine, before, w):
    rows, width = x.shape
    total = w.shape[1]
    states = (HEADS, LANES, LANES)
    return pl.pallas_call(
        project_body,
        in_specs=[SMEM] + [ANY] * 4 + [VMEM],
        out_specs=[ANY] * 6,
        out_shape=[
            hbm((rows, width), bf16),
            hbm((rows, LANES), f32),
            hbm((rows, total), bf16),
            hbm((rows, total // 2), bf16),
            hbm(states, bf16),
            hbm(states, bf16),
        ],
        scratch_shapes=[
            pltpu.VMEM((rows, width), bf16),
            pltpu.VMEM((rows, LANES), f32),
            pltpu.VMEM((rows, LANES), f32),
            pltpu.VMEM(states, bf16),
            pltpu.VMEM((rows, width), bf16),
            pltpu.VMEM((rows, LANES), f32),
            pltpu.VMEM((rows, total), bf16),
            pltpu.VMEM((rows, total // 2), bf16),
            pltpu.VMEM(states, bf16),
            pltpu.VMEM(states, bf16),
            pltpu.SemaphoreType.DMA((4,)),
            pltpu.SemaphoreType.DMA((13,)),
        ],
        compiler_params=params(8),
        cost_estimate=pl.CostEstimate(
            flops=2 * rows * width * total, bytes_accessed=2 * width * total, transcendentals=0
        ),
        name="project",
    )(slopes, *far_away(x, cosine, sine, before), *close_by(w))


def moves(pairs, sem, start=0):
    return [
        pltpu.make_async_copy(source, target, sem.at[start + n])
        for n, (source, target) in enumerate(pairs)
    ]


def entering_state(factors, states, number):
    state = factors[0, number] * states[number].astype(f32)
    state += factors[1, number] * states[HEADS + number].astype(f32)
    return state.astype(bf16)


def finish_body(
    slope, factors, x, qk, pre, far, near, wo, wi, wd,
    mixed, gated, ra, h2, r2, low, g, up, product, y,
    xv, qkv, vuv, statev, mixedv, gatedv, rav, h2v, r2v, lowv, gv, upv, productv, yv,
    attended, total, held, isem, osem, csem,
):
    rows, width = x.shape
    hidden = wd.shape[0]
    columns = held.shape[1]
    steps = hidden // columns
    ins = moves(
        (
            (qk, qkv), (pre.at[:, pl.ds(2 * width, 2 * width)], vuv),
            (far, statev.at[pl.ds(0, HEADS)]), (near, statev.at[pl.ds(HEADS, HEADS)]), (x, xv),
        ),
        isem,
    )
    for copy in ins:
        copy.start()
    for copy in ins[:4]:
        copy.wait()
    ahead = row_index(rows, LANES)

    def pair(i, carry):
        for m in range(4):
            n = i * 4 + m
            at = pl.multiple_of(n * LANES, LANES)
            lane = pl.ds(at, LANES)
            state = entering_state(factors, statev, n)
            lowv[n] = state
            query = qkv[:, lane]
            key = qkv[:, pl.ds(at + width, LANES)]
            weights = (decay_mask(slope[n], rows) * nt(query, key)).astype(bf16)
            inner = nn(weights, vuv[:, lane])
            carried = nn(query, state)
            attended[:, lane] = inner + jnp.exp(ahead * (-slope[n])) * carried
        return carry

    lax.fori_loop(0, HEADS // 4, pair, 0)
    rows_out = attended[...]
    factor = norm_factor(rows_out, width)
    rav[...] = jnp.broadcast_to(factor, rav.shape)
    normed = rows_out * factor
    mixedv[...] = normed.astype(bf16)
    gatedv[...] = (normed * vuv[:, width:].astype(f32)).astype(bf16)
    outs = moves(((mixedv, mixed), (gatedv, gated), (rav, ra), (lowv, low)), osem)
    for copy in outs:
        copy.start()
    ins[4].wait()
    middle = xv[...].astype(f32) + nn(gatedv[...], wo[...])
    total[...] = middle
    factor = norm_factor(middle, width)
    r2v[...] = jnp.broadcast_to(factor, r2v.shape)
    h2v[...] = (middle * factor).astype(bf16)
    more = moves(((h2v, h2), (r2v, r2)), osem, 4)
    for copy in more:
        copy.start()
    held[...] = jnp.zeros_like(held)

    def chunk_out(i):
        at = pl.ds(pl.multiple_of(i * columns, LANES), columns)
        return [
            pltpu.make_async_copy(source.at[:, at], target.at[:, at], csem.at[n, i])
            for n, (source, target) in enumerate(((gv, g), (upv, up), (productv, product)))
        ]

    def step(i, carry):
        start = pl.multiple_of(i * columns, LANES)
        before = pl.multiple_of(jnp.maximum(i - 1, 0) * columns, LANES)
        at = pl.ds(start, columns)
        total[...] += nn(held[...], wd[pl.ds(before, columns), :])
        gate = nn(h2v[...], wi[:, at])
        rise = nn(h2v[...], wi[:, pl.ds(start + hidden, columns)])
        both = (gate * rise).astype(bf16)
        gv[:, at] = gate.astype(bf16)
        upv[:, at] = rise.astype(bf16)
        productv[:, at] = both
        held[...] = both
        for copy in chunk_out(i):
            copy.start()
        return carry

    lax.fori_loop(0, steps, step, 0)
    yv[...] = (total[...] + nn(held[...], wd[hidden - columns :, :])).astype(bf16)
    last = moves(((yv, y),), osem, 6)
    for copy in last:
        copy.start()
    for copy in outs + more + last:
        copy.wait()

    def drain(i, carry):
        for copy in chunk_out(i):
            copy.wait()
        return carry

    lax.fori_loop(0, steps, drain, 0)


def finish(slopes, factors, x, qk, pre, entering, wo, wi, wd):
    rows, width = x.shape
    hidden = wd.shape[0]
    columns = 256
    steps = hidden // columns
    states = (HEADS, LANES, LANES)
    act = hbm((rows, width), bf16)
    factor = hbm((rows, LANES), f32)
    unit = hbm((rows, hidden), bf16)
    outs = [
        act, act, factor, act, factor, hbm(states, bf16), unit, unit, unit, act,
    ]
    return pl.pallas_call(
        finish_body,
        in_specs=[SMEM] * 2 + [ANY] * 5 + [VMEM] * 3,
        out_specs=[ANY] * len(outs),
        out_shape=outs,
        scratch_shapes=[
            pltpu.VMEM((rows, width), bf16),
            pltpu.VMEM((rows, 2 * width), bf16),
            pltpu.VMEM((rows, 2 * width), bf16),
            pltpu.VMEM((2 * HEADS, LANES, LANES), bf16),
        ]
        + [pltpu.VMEM(o.shape, o.dtype) for o in outs]
        + [
            pltpu.VMEM((rows, width), f32),
            pltpu.VMEM((rows, width), f32),
            pltpu.VMEM((rows, columns), bf16),
            pltpu.SemaphoreType.DMA((5,)),
            pltpu.SemaphoreType.DMA((7,)),
            pltpu.SemaphoreType.DMA((3, steps)),
        ],
        compiler_params=params(18),
        cost_estimate=pl.CostEstimate(
            flops=2 * rows * width * (width + 3 * hidden),
            bytes_accessed=2 * width * (width + 3 * hidden),
            transcendentals=0,
        ),
        name="finish",
    )(slopes, factors, *far_away(x, qk, pre, *entering), *close_by(wo, wi, wd))


def back_channel_body(
    slope, dy, wo, wi, wd, g, up, h2, r2, mixed, ra, qk, pre, low, cosine, sine, behind,
    dg, dup, dmid, dm, dq, du, dk, dv, state, joined,
    dyv, gv, upv, h2v, r2v, mixedv, rav, qkv, qpv, vuv, lowv, cv, sv, bv,
    dgv, dupv, dmidv, dmv, dqv, duv, dkv, dvv, statev, jv,
    total, datt, heldg, heldu, isem, osem, csem,
):
    rows, width = dy.shape
    hidden = wd.shape[0]
    columns = heldg.shape[1]
    steps = hidden // columns
    ins = moves(
        (
            (dy, dyv), (g, gv), (up, upv), (h2, h2v), (r2, r2v), (mixed, mixedv), (ra, rav),
            (qk, qkv), (pre.at[:, pl.ds(0, width)], qpv),
            (pre.at[:, pl.ds(2 * width, 2 * width)], vuv), (low, lowv), (cosine, cv), (sine, sv),
            (behind, bv),
        ),
        isem,
    )
    for copy in ins:
        copy.start()
    for copy in ins[:3]:
        copy.wait()
    heldg[...] = jnp.zeros_like(heldg)
    heldu[...] = jnp.zeros_like(heldu)
    total[...] = jnp.zeros_like(total)

    def chunk_out(i):
        at = pl.ds(pl.multiple_of(i * columns, LANES), columns)
        return [
            pltpu.make_async_copy(source.at[:, at], target.at[:, at], csem.at[n, i])
            for n, (source, target) in enumerate(((dgv, dg), (dupv, dup)))
        ]

    def step(i, carry):
        at = pl.ds(pl.multiple_of(i * columns, LANES), columns)
        before = pl.multiple_of(jnp.maximum(i - 1, 0) * columns, LANES)
        total[...] += nt(heldg[...], wi[:, pl.ds(before, columns)]) + nt(
            heldu[...], wi[:, pl.ds(before + hidden, columns)]
        )
        product = nt(dyv[...], wd[at, :])
        left = (product * upv[:, at].astype(f32)).astype(bf16)
        right = (product * gv[:, at].astype(f32)).astype(bf16)
        dgv[:, at] = left
        dupv[:, at] = right
        heldg[...] = left
        heldu[...] = right
        for copy in chunk_out(i):
            copy.start()
        return carry

    lax.fori_loop(0, steps, step, 0)
    for copy in ins[3:]:
        copy.wait()
    dh2 = (
        total[...]
        + nt(heldg[...], wi[:, hidden - columns : hidden])
        + nt(heldu[...], wi[:, 2 * hidden - columns :])
    )
    middle = dyv[...].astype(f32) + norm_back(dh2, h2v[...].astype(f32), r2v[:, 0:1], width)
    dmidv[...] = middle
    dmv[...] = middle.astype(bf16)
    outs = moves(((dmidv, dmid), (dmv, dm)), osem)
    for copy in outs:
        copy.start()
    dgated = nt(dmv[...], wo[...])
    normed = mixedv[...].astype(f32)
    duv[...] = (dgated * normed).astype(bf16)
    back = norm_back(dgated * vuv[:, width:].astype(f32), normed, rav[:, 0:1], width)
    datt[...] = back.astype(bf16)
    ahead = row_index(rows, LANES)
    row = lax.broadcasted_iota(jnp.int32, (rows, rows), 0)
    column = lax.broadcasted_iota(jnp.int32, (rows, rows), 1)
    distance = (row - column).astype(f32)

    def some(i, carry):
        for m in range(2):
            n = i * 2 + m
            at = pl.multiple_of(n * LANES, LANES)
            lane = pl.ds(at, LANES)
            query, key = qkv[:, lane], qkv[:, pl.ds(at + width, LANES)]
            value, cot = vuv[:, lane], datt[:, lane]
            power = jnp.exp(jnp.abs(distance) * (-slope[n]))
            mask = jnp.where(distance >= 0.0, power, 0.0)
            flipped = jnp.where(distance <= 0.0, power, 0.0)
            weights_t = (flipped * nt(key, query)).astype(bf16)
            scores = (mask * nt(cot, value)).astype(bf16)
            scores_t = (flipped * nt(value, cot)).astype(bf16)
            scaled = (jnp.exp(ahead * (-slope[n])) * cot.astype(f32)).astype(bf16)
            own = tn(query, scaled)
            statev[n] = own.astype(bf16)
            jv[n] = join(slope[n], bv[n], own)
            dquery = nn(scores, key) + nt(scaled, lowv[n])
            turned = dquery * cv[...] + half_turn(dquery * sv[...])
            p = qpv[:, lane].astype(f32)
            s = sigmoid(p)
            dqv[:, lane] = (turned * (s * (1.0 + p * (1.0 - s)))).astype(bf16)
            dkv[:, lane] = nn(scores_t, query)
            dvv[:, lane] = nn(weights_t, cot)
        return carry

    lax.fori_loop(0, HEADS // 2, some, 0)
    last = moves(
        ((statev, state), (jv, joined), (dqv, dq), (duv, du), (dkv, dk), (dvv, dv)), osem, 2
    )
    for copy in last:
        copy.start()
    for copy in outs + last:
        copy.wait()

    def drain(i, carry):
        for copy in chunk_out(i):
            copy.wait()
        return carry

    lax.fori_loop(0, steps, drain, 0)


def back_channel(slopes, dy, r, cosine, sine, behind, wo, wi, wd):
    rows, width = dy.shape
    hidden = wd.shape[0]
    columns = 256
    steps = hidden // columns
    states = (HEADS, LANES, LANES)
    act = hbm((rows, width), bf16)
    full = hbm((rows, width), f32)
    unit = hbm((rows, hidden), bf16)
    state = hbm(states, bf16)
    outs = [unit, unit, full, act, act, act, full, full, state, state]
    wide = pltpu.VMEM((rows, width), bf16)
    thin = pltpu.VMEM((rows, LANES), f32)
    twice = pltpu.VMEM((rows, 2 * width), bf16)
    tall = pltpu.VMEM((rows, hidden), bf16)
    return pl.pallas_call(
        back_channel_body,
        in_specs=[SMEM] + [ANY] + [VMEM] * 3 + [ANY] * 12,
        out_specs=[ANY] * len(outs),
        out_shape=outs,
        scratch_shapes=[
            wide, tall, tall, wide, thin, wide, thin, twice, wide, twice,
            pltpu.VMEM(states, bf16), thin, thin, pltpu.VMEM(states, bf16),
        ]
        + [pltpu.VMEM(o.shape, o.dtype) for o in outs]
        + [
            pltpu.VMEM((rows, width), f32),
            wide,
            pltpu.VMEM((rows, columns), bf16),
            pltpu.VMEM((rows, columns), bf16),
            pltpu.SemaphoreType.DMA((14,)),
            pltpu.SemaphoreType.DMA((8,)),
            pltpu.SemaphoreType.DMA((2, steps)),
        ],
        compiler_params=params(22),
        cost_estimate=pl.CostEstimate(
            flops=2 * rows * width * (width + 3 * hidden),
            bytes_accessed=2 * width * (width + 3 * hidden),
            transcendentals=0,
        ),
        name="back_channel",
    )(
        slopes, *far_away(dy), *close_by(wo, wi, wd),
        *far_away(
            r["g"], r["up"], r["h2"], r["r2"], r["mixed"], r["ra"], r["qk"], r["pre"], r["low"],
            cosine, sine, behind,
        ),
    )


def back_mixer_body(
    slope, factors, dq, du, dk, dv, qk, pre, far, near, cosine, sine, h1, r1, dmid, w,
    dkp, dvp, dx,
    dkin, dvin, kvv, kpv, vv, statev, cv, sv, h1v, r1v, dmidv, parts, dxv, isem, osem,
):
    rows, width = dq.shape
    ins = moves(
        (
            (dk, dkin), (dv, dvin), (qk.at[:, pl.ds(width, width)], kvv),
            (pre.at[:, pl.ds(width, width)], kpv), (pre.at[:, pl.ds(2 * width, width)], vv),
            (far, statev.at[pl.ds(0, HEADS)]), (near, statev.at[pl.ds(HEADS, HEADS)]),
            (cosine, cv), (sine, sv),
            (dq, parts.at[:, pl.ds(0, width)]), (du, parts.at[:, pl.ds(3 * width, width)]),
            (h1, h1v), (r1, r1v), (dmid, dmidv),
        ),
        isem,
    )
    for copy in ins:
        copy.start()
    for copy in ins[:9]:
        copy.wait()
    ahead = rows - row_index(rows, LANES)

    def some(i, carry):
        for m in range(4):
            n = i * 4 + m
            at = pl.multiple_of(n * LANES, LANES)
            lane = pl.ds(at, LANES)
            state = entering_state(factors, statev, n)
            decay = jnp.exp(ahead * (-slope[n]))
            keyed = (kvv[:, lane].astype(f32) * decay).astype(bf16)
            dkey = dkin[:, lane] + decay * nt(vv[:, lane], state)
            turned = dkey * cv[...] + half_turn(dkey * sv[...])
            p = kpv[:, lane].astype(f32)
            s = sigmoid(p)
            parts[:, pl.ds(at + width, LANES)] = (turned * (s * (1.0 + p * (1.0 - s)))).astype(bf16)
            parts[:, pl.ds(at + 2 * width, LANES)] = (dvin[:, lane] + nn(keyed, state)).astype(bf16)
        return carry

    lax.fori_loop(0, HEADS // 4, some, 0)
    outs = moves(
        ((parts.at[:, pl.ds(width, width)], dkp), (parts.at[:, pl.ds(2 * width, width)], dvp)), osem
    )
    for copy in outs:
        copy.start()
    for copy in ins[9:]:
        copy.wait()
    total = nt(parts[...], w[...])
    back = norm_back(total, h1v[...].astype(f32), r1v[:, 0:1], width)
    dxv[...] = (dmidv[...] + back).astype(bf16)
    last = moves(((dxv, dx),), osem, 2)
    for copy in last:
        copy.start()
    for copy in outs + last:
        copy.wait()


def back_mixer(slopes, factors, r, entering, cosine, sine, w):
    rows, width = r["dq"].shape
    act = hbm((rows, width), bf16)
    wide = pltpu.VMEM((rows, width), bf16)
    full = pltpu.VMEM((rows, width), f32)
    thin = pltpu.VMEM((rows, LANES), f32)
    return pl.pallas_call(
        back_mixer_body,
        in_specs=[SMEM] * 2 + [ANY] * 13 + [VMEM],
        out_specs=[ANY] * 3,
        out_shape=[act, act, act],
        scratch_shapes=[
            full, full, wide, wide, wide, pltpu.VMEM((2 * HEADS, LANES, LANES), bf16), thin, thin,
            wide, thin,
            full,
            pltpu.VMEM((rows, w.shape[1]), bf16), wide,
            pltpu.SemaphoreType.DMA((14,)),
            pltpu.SemaphoreType.DMA((3,)),
        ],
        compiler_params=params(14),
        cost_estimate=pl.CostEstimate(
            flops=2 * rows * width * w.shape[1],
            bytes_accessed=2 * width * w.shape[1],
            transcendentals=0,
        ),
        name="back_mixer",
    )(
        slopes, factors,
        *far_away(
            r["dq"], r["du"], r["dk"], r["dv"], r["qk"], r["pre"], *entering, cosine, sine,
            r["h1"], r["r1"], r["dmid"],
        ),
        *close_by(w),
    )


def weight_body(*refs, batch, sides, groups):
    place = refs[0]
    lefts = refs[1 : 1 + 2 * batch]
    rights = refs[1 + 2 * batch : 1 + 2 * batch + 2 * batch * sides]
    outs = refs[1 + 2 * batch + 2 * batch * sides : -7]
    x, xt, ys, stage, xsem, ysem, osem = refs[-7:]
    rows = lefts[0].shape[0]
    columns = x.shape[1]
    quarter = columns // 4
    blocks = groups[0][2]

    def left_copies(section):
        return [
            pltpu.make_async_copy(
                lefts[section * batch + b], x.at[pl.ds(b * rows, rows)], xsem.at[b]
            )
            for b in range(batch)
        ]

    def right_copies(section, s):
        return [
            pltpu.make_async_copy(
                rights[(section * sides + s) * batch + b],
                ys.at[s, pl.ds(b * rows, rows)],
                ysem.at[s, b],
            )
            for b in range(batch)
        ]

    for section in range(2):

        @pl.when(place[4] == section)
        def _():
            for copy in left_copies(section):
                copy.start()
            for s in range(sides):
                for copy in right_copies(section, s):
                    copy.start()

    for copy in left_copies(0):
        copy.wait()
    for piece in range(columns // LANES):
        xt[piece * LANES : (piece + 1) * LANES, :] = x[:, piece * LANES : (piece + 1) * LANES].T

    def move(number, role, out):
        slot = number * 4 + role
        return pltpu.make_async_copy(
            stage.at[slot], out.at[pl.ds((role % 2) * blocks, blocks)], osem.at[slot]
        )

    def one(role, number, side, start):
        left = xt[pl.ds(pl.multiple_of(place[role] * quarter, 16), quarter), :]
        tile = nn(left, ys[side, :, start * LANES : (start + blocks) * LANES]).astype(bf16)
        for n in range(blocks):
            stage[number * 4 + role, n] = tile[:, head(n)]

    for number, (side, start, _) in enumerate(groups):
        if all(side != done for done, _, _ in groups[:number]):
            for copy in right_copies(0, side):
                copy.wait()

        def step(role, carry, number=number, side=side, start=start):
            one(role, number, side, start)

            @pl.when(role < 2)
            def _():
                move(number, role, outs[2 * number]).start()

            @pl.when(role >= 2)
            def _():
                move(number, role, outs[2 * number + 1]).start()

            return carry

        lax.fori_loop(0, 4, step, 0)
    for number in range(len(groups)):
        for role in range(4):
            move(number, role, outs[2 * number + role // 2]).wait()


def weight_gradient(place, lefts, rights, groups):
    batch = len(lefts[0])
    sides = len(rights[0])
    rows, columns = lefts[0][0].shape
    span = rights[0][0][0].shape[1]
    quarter = columns // 4
    blocks = groups[0][2]
    flat_left = [a for section in lefts for a in section]
    flat_right = [a for section in rights for side in section for a in side]
    out = pl.pallas_call(
        functools.partial(weight_body, batch=batch, sides=sides, groups=groups),
        in_specs=[SMEM] + [ANY] * (len(flat_left) + len(flat_right)),
        out_specs=[ANY] * (2 * len(groups)),
        out_shape=[hbm((2 * blocks, quarter, LANES), bf16)] * (2 * len(groups)),
        scratch_shapes=[
            pltpu.VMEM((batch * rows, columns), bf16),
            pltpu.VMEM((columns, batch * rows), bf16),
            pltpu.VMEM((sides, batch * rows, span), bf16),
            pltpu.VMEM((4 * len(groups), blocks, quarter, LANES), bf16),
            pltpu.SemaphoreType.DMA((batch,)),
            pltpu.SemaphoreType.DMA((sides, batch)),
            pltpu.SemaphoreType.DMA((4 * len(groups),)),
        ],
        compiler_params=params(24),
        cost_estimate=pl.CostEstimate(
            flops=2 * batch * rows * columns * sides * span,
            bytes_accessed=2 * columns * sides * span,
            transcendentals=0,
        ),
        name="weight_gradient",
    )(place, *far_away(*flat_left, *flat_right))
    return [(out[2 * n], out[2 * n + 1]) for n in range(len(groups))]


def settle_body(edge, outer, inner, *rest):
    out = rest[-1]

    @pl.when(edge[0] == 1)
    def _():
        for n in range(outer.shape[0]):
            out[:, head(n)] = outer[n].astype(f32)

    @pl.when(edge[0] == 0)
    def _():
        for n in range(inner.shape[0]):
            out[:, head(n)] = inner[n].astype(f32)


def settle(edge, outer, inner, total, held, number):
    blocks, quarter, _ = outer.shape
    more = [] if held is None else [held]
    return pl.pallas_call(
        settle_body,
        grid=(1,),
        in_specs=[SMEM, whole(outer.shape), whole(inner.shape)] + [ANY] * len(more),
        out_specs=pl.BlockSpec((quarter, blocks * LANES), lambda j: (0, number)),
        out_shape=hbm((quarter, total), f32),
        input_output_aliases={3: 0} if more else {},
        compiler_params=params(8),
        name="settle",
    )(edge, outer, inner, *more)


def add(a, b):
    return (a.astype(f32) + b.astype(f32)).astype(bf16)


def gathered_state(own, slopes, forward):
    count = lax.axis_size("seq")
    place = lax.axis_index("seq")
    gathered = lax.all_gather(own, "seq").astype(f32)
    device = jnp.arange(count)
    distance = place - 1 - device if forward else device - place - 1
    power = jnp.maximum(distance, 0).astype(f32) * BLK
    weight = jnp.where(distance[:, None] >= 0, jnp.exp(-slopes[None] * power[:, None]), 0.0)
    return jnp.sum(weight[:, :, None, None] * gathered, axis=0).astype(bf16)


def halves(first, second):
    place = lax.axis_index("seq")
    sent = jnp.where(place % 2 == 1, first, second)
    one = lax.ppermute(sent, "seq", [(1, 0), (2, 3), (0, 2), (3, 1)])
    two = lax.ppermute(jnp.where(place == 1, second, first), "seq", [(2, 1), (1, 2)])
    return (
        jnp.where(place == 0, first, jnp.where(place == 1, two, one)),
        jnp.where(place == 3, second, jnp.where(place == 2, two, one)),
    )


def quarters(low, high):
    place = lax.axis_index("seq")
    one = lax.ppermute(jnp.where(place < 2, high, low), "seq", [(0, 1), (3, 2), (2, 0), (1, 3)])
    two = lax.ppermute(jnp.where(place == 1, low, high), "seq", [(1, 2), (2, 1)])
    return (
        jnp.where(place == 0, low, jnp.where(place == 2, two, one)),
        jnp.where(place == 3, high, jnp.where(place == 1, two, one)),
    )


class Sums:
    def __init__(self, edge, settled):
        self.edge = edge
        self.settled = settled
        self.waiting, self.parts, self.partial, self.across = [], [], [], []
        self.previous = None
        self.step = 0
        self.marks = []
        self.written = None

    def load(self, chunks):
        for given, kept in chunks:
            blocks = given.shape[0] // 2
            taken = lax.ppermute(given, "seq", [(0, 1), (1, 0), (2, 3), (3, 2)])
            self.waiting.append(
                (add(kept[:blocks], taken[:blocks]), add(kept[blocks:], taken[blocks:]))
            )

    def over_y(self):
        if not self.waiting:
            return
        far, own = self.waiting.pop(0)
        if self.previous is not None:
            far, _ = lax.optimization_barrier((far, self.previous))
        self.marks.append(far)
        self.previous = lax.ppermute(far, "seq", [(0, 2), (2, 0), (1, 3), (3, 1)])
        self.parts.append(add(own, self.previous))

    def over_z(self, last=False):
        step, count = self.step, len(self.parts)
        if step >= count + 2 or (step >= count and not last):
            return False
        part = self.parts[step] if step < count else None
        done = None
        if step >= 2:
            done = self.partial[step - 2].astype(f32) + self.across[step - 2].astype(f32)
        if part is not None and self.written is not None:
            part, _ = lax.optimization_barrier((part, self.written))
            self.written = None
        if 1 <= step <= count:
            self.marks.append(self.partial[step - 1])
            self.across.append(lax.ppermute(self.partial[step - 1], "dp", [(1, 2), (2, 1)]))
        if part is not None and done is not None and part.shape == done.shape:
            sent = jnp.where(self.edge, part.astype(f32), done).astype(bf16)
            self.marks.append(sent)
            got = lax.ppermute(sent, "dp", [(0, 1), (1, 0), (2, 3), (3, 2)])
            self.partial.append(add(part, got))
            self.written = self.settled(got, sent)
        else:
            if part is not None:
                self.marks.append(part)
                self.partial.append(add(part, lax.ppermute(part, "dp", [(0, 1), (3, 2)])))
            if done is not None:
                done = done.astype(bf16)
                self.marks.append(done)
                self.written = self.settled(lax.ppermute(done, "dp", [(1, 0), (2, 3)]), done)
        self.step += 1
        return True

    def started(self):
        marks, self.marks = self.marks, []
        return marks


def angle_tables(position_row, half_size):
    frequency = jnp.exp(
        jnp.arange(half_size, dtype=jnp.float32) * (-math.log(theta_base) / half_size)
    )
    angles = position_row.astype(jnp.float32)[..., None] * frequency
    cosine = jnp.cos(angles)
    sine_rows = jnp.sin(angles)
    return (
        jnp.concatenate([cosine, cosine], axis=-1),
        jnp.concatenate([-sine_rows, sine_rows], axis=-1),
    )


class Order:
    def __init__(self):
        self.last = []

    def after(self, value):
        if self.last:
            value = lax.optimization_barrier((value, *self.last))[0]
        return value

    def at(self, *values):
        self.last = list(values)


class Layer:
    def __init__(self, order, slopes, factors, chained, cosine, sine, weights):
        self.order, self.slopes, self.factors, self.chained = order, slopes, factors, chained
        self.cosine, self.sine = cosine, sine
        self.w, self.wo, self.wi, self.wd = weights
        self.blocks = [None, None]
        self.entering = [None, None]
        self.later = [None, None]
        self.zero = jnp.zeros((HEADS, LANES, LANES), bf16)

    def first(self, b, x):
        before = self.blocks[0]["state"] if b == 1 else self.zero
        h1, r1, pre, qk, state, joined = project(
            self.order.after(self.slopes), x, self.cosine[b], self.sine[b], before, self.w
        )
        self.order.at(r1)
        self.blocks[b] = dict(x=x, h1=h1, r1=r1, pre=pre, qk=qk, state=state)
        if not self.chained:
            self.entering[b] = gathered_state(state, self.slopes, True)
        elif b == 1:
            near = lax.ppermute(joined, "seq", [(0, 1), (2, 3)])
            self.entering = [near, near]

    def second(self, b):
        r = self.blocks[b]
        near = self.blocks[0]["state"] if b == 1 else self.entering[b]
        mixed, gated, ra, h2, r2, low, g, up, product, y = finish(
            self.order.after(self.slopes), self.factors[b], r["x"], r["qk"], r["pre"],
            (self.entering[b], near), self.wo, self.wi, self.wd,
        )
        self.order.at(ra)
        r.update(
            mixed=mixed, gated=gated, ra=ra, h2=h2, r2=r2, low=low, g=g, up=up, product=product
        )
        return y

    def back_first(self, b, dy):
        r = self.blocks[b]
        behind = self.blocks[1]["dstate"] if b == 0 else self.zero
        dg, dup, dmid, dm, dq, du, dk, dv, state, joined = back_channel(
            self.order.after(self.slopes), dy, r, self.cosine[b], self.sine[b], behind,
            self.wo, self.wi, self.wd,
        )
        self.order.at(dm)
        r.update(dy=dy, dg=dg, dup=dup, dmid=dmid, dm=dm, dq=dq, du=du, dk=dk, dv=dv, dstate=state)
        if not self.chained:
            self.later[b] = gathered_state(state, self.slopes, False)
        elif b == 0:
            near = lax.ppermute(joined, "seq", [(1, 0), (3, 2)])
            self.later = [near, near]

    def back_second(self, b):
        r = self.blocks[b]
        near = self.blocks[1]["dstate"] if b == 0 else self.later[b]
        dkp, dvp, dx = back_mixer(
            self.order.after(self.slopes), self.factors[1 - b], r, (self.later[b], near),
            self.cosine[b], self.sine[b], self.w,
        )
        self.order.at(dkp)
        r.update(dkp=dkp, dvp=dvp)
        return dx


def per_device(boundary, positions, decay_exp, mixer_in, mixer_out, channel_in, channel_out):
    section = lax.axis_index("section")
    is_first = section == 0
    batch, rows, width = boundary.shape[1:]
    assert rows == BLK and batch == 2
    slopes = jnp.exp2(-0.5 * decay_exp[0].astype(jnp.float32))
    w, wo, wi, wd = weights = mixer_in[0], mixer_out[0], channel_in[0], channel_out[0]
    hidden = wd.shape[0]
    half_size = width // HEADS // 2
    usual = lax.axis_size("seq") == 4 and lax.axis_size("dp") == 4
    place, line = lax.axis_index("seq"), lax.axis_index("dp")
    core, y_place = place % 2, place // 2

    own = (boundary[0, 0], boundary[0, 1])
    if usual:
        own = halves(*own)
        every = lax.all_gather(positions, "seq")
        chosen = lax.dynamic_index_in_dim(every, y_place, 1, keepdims=False)
        positions = lax.dynamic_slice_in_dim(chosen, 2 * core, 2, 0)
    cosine, sine = angle_tables(positions, half_size)

    roles = [
        2 * (1 - y_place) + 1 - core,
        2 * y_place + 1 - core,
        2 * (1 - y_place) + core,
        2 * y_place + core,
    ]
    if not usual:
        roles = [0, 1, 2, 3]
    roles = jnp.stack([jnp.asarray(r, jnp.int32) for r in (*roles, section)])
    edge = (line == 0) | (line == lax.axis_size("dp") - 1)
    flag = edge.astype(jnp.int32)[None]
    one = jnp.ones_like(slopes)
    factors = [jnp.stack([one, 0.0 * one])] * 2
    if usual:
        factors[1] = jnp.stack([jnp.exp(-slopes * BLK), one])
    roles, flag, slopes, *factors = lax.optimization_barrier((roles, flag, slopes, *factors))
    edge = flag[0] == 1
    order = Order()
    order.at(roles, flag)
    layers = [
        Layer(order, slopes, factors, usual, cosine, sine, weights) for section_of_it in range(2)
    ]
    early, late = layers

    for b in range(2):
        early.first(b, own[b])
    arrived = [lax.ppermute(early.second(b), "section", [(0, 1)]) for b in range(2)]
    for b in range(2):
        late.first(b, arrived[b])
    outputs = [late.second(b) for b in range(2)]
    for b in (1, 0):
        late.back_first(b, own[b])
    returned = [None, None]
    for b in (1, 0):
        returned[b] = lax.ppermute(late.back_second(b), "section", [(1, 0)])

    def operands(*names):
        return [[[r[name] for r in layer.blocks] for name in names] for layer in layers]

    chunks = []
    spans = [(3, width), (3, width)] + [(2, 2 * hidden)] * 4 + [(1, width)] + [(0, 4 * width)] * 4
    numbers = [0, 1, 0, 1, 2, 3, 0, 0, 1, 2, 3]
    held = [None] * 4
    finished = []

    def settled(outer, inner):
        number = len(finished)
        index, total = spans[number]
        blocks, quarter = chunks[number][0].shape[0] // 2, chunks[number][0].shape[1]
        shape = (blocks, quarter, LANES)
        finished.append(number)
        held[index] = settle(
            flag, outer.reshape(shape), inner.reshape(shape), total, held[index], numbers[number]
        )
        return held[index]

    sums = Sums(edge, settled)

    def even(array):
        return array.reshape(array.shape[0] * array.shape[1] // 256, 256, LANES)

    def gradient(name, names, groups):
        left = [side[0] for side in operands(name)]
        found = weight_gradient(order.after(roles), left, operands(*names), groups)
        order.at(found[-1][1])
        chunks.extend(found)
        if usual:
            sums.load([(even(given), even(kept)) for given, kept in found])

    def move(*what):
        if not usual:
            return
        for way in what:
            way()
        order.at(*order.last, *sums.started())

    early.back_first(1, returned[1])
    early.blocks[0]["dy"] = returned[0]
    gradient("product", ("dy",), [(0, 0, 4), (0, 4, 4)])
    move(sums.over_y)
    early.back_first(0, returned[0])
    move(sums.over_y, sums.over_z)
    half = hidden // LANES // 2
    gradient("h2", ("dg", "dup"), [(0, 0, half), (0, half, half), (1, 0, half), (1, half, half)])
    move(sums.over_y, sums.over_z)
    dx = [None, None]
    for b in (1, 0):
        dx[b] = early.back_second(b)
    move(sums.over_y, sums.over_z)
    eight = width // LANES
    gradient("gated", ("dm",), [(0, 0, eight)])
    gradient("h1", ("dq", "dkp", "dvp", "du"), [(s, 0, eight) for s in range(4)])
    ends = [jnp.where(is_first, dx[b], outputs[b]) for b in range(2)]
    joined = jnp.stack(quarters(*ends) if usual else ends)[None]
    if usual:
        while sums.waiting:
            move(sums.over_y, sums.over_z)
        while sums.over_z(last=True):
            pass
        return (joined, *(h[None] for h in held))
    found = [[], [], [], []]
    for (index, total), chunk in zip(spans, chunks):
        chunk = jnp.concatenate(chunk)
        blocks, quarter = chunk.shape[0] // 4, chunk.shape[1]
        rows_first = chunk.reshape(4, blocks, quarter, LANES).transpose(0, 2, 1, 3)
        found[index].append(rows_first.reshape(4 * quarter, blocks * LANES))
    summed = []
    for pieces in found:
        part = lax.psum_scatter(
            jnp.concatenate(pieces, axis=1), "seq", scatter_dimension=0, tiled=True
        )
        summed.append(lax.psum(part, "dp").astype(f32)[None])
    return (joined, *summed)


def solution(mesh):
    in_specs = (
        P("section", "dp", "seq", None),
        P("dp", "seq"),
        P("section", None),
        P("section", None, None),
        P("section", None, None),
        P("section", None, None),
        P("section", None, None),
    )
    out_specs = (
        P("section", "dp", "seq", None),
        P("section", "seq", None),
        P("section", "seq", None),
        P("section", "seq", None),
        P("section", "seq", None),
    )
    return jax.shard_map(
        per_device, mesh=mesh, in_specs=in_specs, out_specs=out_specs, check_vma=False
    )
```

```python
import functools
import math

import jax
import jax.numpy as jnp
from jax import lax
from jax.experimental import pallas as pl
from jax.experimental.pallas import tpu as pltpu
from jax.sharding import PartitionSpec as P

HEADS = 8
BLK = 256
LANES = 128
STEPS = 8

epsilon = 1e-06
theta_base = 10000.0
f32 = jnp.float32
bf16 = jnp.bfloat16


def nn(a, b):
    return jnp.dot(a, b, preferred_element_type=f32)


def nt(a, b):
    return lax.dot_general(a, b, (((1,), (1,)), ((), ())), preferred_element_type=f32)


def tn(a, b):
    return lax.dot_general(a, b, (((0,), (0,)), ((), ())), preferred_element_type=f32)


def sigmoid(v):
    return 1.0 / (1.0 + jnp.exp(-v))


def norm_factor(v, width):
    return lax.rsqrt(jnp.sum(v * v, axis=-1, keepdims=True) * (1.0 / width) + epsilon)


def norm_back(cotangent, normed, factor, width):
    mean = jnp.sum(cotangent * normed, axis=-1, keepdims=True) * (1.0 / width)
    return factor * (cotangent - normed * mean)


def row_index(rows, columns):
    return lax.broadcasted_iota(jnp.int32, (rows, columns), 0).astype(f32)


def decay_mask(slope, rows):
    row = lax.broadcasted_iota(jnp.int32, (rows, rows), 0)
    column = lax.broadcasted_iota(jnp.int32, (rows, rows), 1)
    distance = jnp.maximum(row - column, 0).astype(f32)
    return jnp.where(row >= column, jnp.exp(distance * (-slope)), 0.0)


def head(number):
    return slice(number * LANES, (number + 1) * LANES)


def half_turn(v):
    return pltpu.roll(v, LANES // 2, 1)


def whole(shape):
    return pl.BlockSpec(shape, lambda j: (0,) * len(shape))


def hbm(shape, kind):
    return pltpu.HBM(tuple(shape), kind)


def far_away(*arrays):
    return [pltpu.with_memory_space_constraint(a, pltpu.HBM) for a in arrays]


def close_by(*arrays):
    return [pltpu.with_memory_space_constraint(a, pltpu.VMEM) for a in arrays]


def params(megabytes):
    return pltpu.CompilerParams(vmem_limit_bytes=megabytes * 1024 * 1024)


SMEM = pl.BlockSpec(memory_space=pltpu.SMEM)
ANY = pl.BlockSpec(memory_space=pltpu.HBM)
VMEM = pl.BlockSpec(memory_space=pltpu.VMEM)


def tables(position, rows):
    lane = lax.broadcasted_iota(jnp.int32, (rows, LANES), 1)
    half = LANES // 2
    feature = jnp.where(lane < half, lane, lane - half).astype(f32)
    frequency = jnp.exp(feature * (-math.log(theta_base) / half))
    angle = position * frequency
    return jnp.cos(angle), jnp.where(lane < half, -jnp.sin(angle), jnp.sin(angle))


def join(slope, before, own):
    decay = jnp.exp(jnp.full((LANES, LANES), -BLK, f32) * slope)
    return (decay * before.astype(f32) + own).astype(bf16)


def project_body(slope, x, cosine, sine, before, w, h1, r1, pre, qk, state, joined,
                 xv, cv, sv, bv, hv, rv, prev, qkv, stv, jv, isem, osem, qsem):
    rows, width = x.shape
    steps = STEPS
    columns = w.shape[1] // steps
    heads = columns // LANES
    first = [
        pltpu.make_async_copy(source, target, isem.at[n])
        for n, (source, target) in enumerate(((x, xv), (cosine, cv), (sine, sv), (before, bv)))
    ]
    for copy in first:
        copy.start()

    first[0].wait()
    v = xv[...].astype(f32)
    factor = norm_factor(v, width)
    hv[...] = (v * factor).astype(bf16)
    rv[...] = jnp.broadcast_to(factor, rv.shape)
    for copy in first[1:]:
        copy.wait()
    outs = [pltpu.make_async_copy(hv, h1, osem.at[0]), pltpu.make_async_copy(rv, r1, osem.at[1])]
    for copy in outs:
        copy.start()

    def pre_out(j):
        at = pl.ds(pl.multiple_of(j * columns, LANES), columns)
        return pltpu.make_async_copy(prev.at[:, at], pre.at[:, at], osem.at[3 + j])

    def qk_out(j):
        at = pl.ds(pl.multiple_of(j * columns, LANES), columns)
        return pltpu.make_async_copy(qkv.at[:, at], qk.at[:, at], qsem.at[j])

    def step(j, carry):
        at = pl.multiple_of(j * columns, LANES)
        p = nn(hv[...], w[:, pl.ds(at, columns)])
        prev[:, pl.ds(at, columns)] = p.astype(bf16)
        pre_out(j).start()

        @pl.when(j < steps // 2)
        def _():
            for n in range(heads):
                v = p[:, head(n)]
                v = v * sigmoid(v)
                turned = v * cv[...] + half_turn(v) * sv[...]
                qkv[:, pl.ds(at + n * LANES, LANES)] = turned.astype(bf16)
            qk_out(j).start()

        @pl.when((j >= steps // 2) & (j < 3 * steps // 4))
        def _():
            values = p.astype(bf16)
            ahead = rows - row_index(rows, LANES)
            for n in range(heads):
                number = (j - steps // 2) * heads + n
                decay = jnp.exp(ahead * (-slope[number]))
                key = qkv[:, pl.ds(at - width + n * LANES, LANES)]
                keyed = (key.astype(f32) * decay).astype(bf16)
                own = tn(keyed, values[:, head(n)])
                stv[number] = own.astype(bf16)
                jv[number] = join(slope[number], bv[number], own)

        return carry

    lax.fori_loop(0, steps, step, 0)
    last = [
        pltpu.make_async_copy(stv, state, osem.at[11]),
        pltpu.make_async_copy(jv, joined, osem.at[12]),
    ]
    for copy in last:
        copy.start()
    for copy in outs + last:
        copy.wait()
    for j in range(steps):
        pre_out(j).wait()
    for j in range(steps // 2):
        qk_out(j).wait()


def project(slopes, x, cosine, sine, before, w):
    rows, width = x.shape
    total = w.shape[1]
    states = (HEADS, LANES, LANES)
    return pl.pallas_call(
        project_body,
        in_specs=[SMEM] + [ANY] * 4 + [VMEM],
        out_specs=[ANY] * 6,
        out_shape=[
            hbm((rows, width), bf16),
            hbm((rows, LANES), f32),
            hbm((rows, total), bf16),
            hbm((rows, total // 2), bf16),
            hbm(states, bf16),
            hbm(states, bf16),
        ],
        scratch_shapes=[
            pltpu.VMEM((rows, width), bf16),
            pltpu.VMEM((rows, LANES), f32),
            pltpu.VMEM((rows, LANES), f32),
            pltpu.VMEM(states, bf16),
            pltpu.VMEM((rows, width), bf16),
            pltpu.VMEM((rows, LANES), f32),
            pltpu.VMEM((rows, total), bf16),
            pltpu.VMEM((rows, total // 2), bf16),
            pltpu.VMEM(states, bf16),
            pltpu.VMEM(states, bf16),
            pltpu.SemaphoreType.DMA((4,)),
            pltpu.SemaphoreType.DMA((13,)),
            pltpu.SemaphoreType.DMA((STEPS // 2,)),
        ],
        compiler_params=params(8),
        cost_estimate=pl.CostEstimate(
            flops=2 * rows * width * total, bytes_accessed=2 * width * total, transcendentals=0
        ),
        name="project",
    )(slopes, *far_away(x, cosine, sine, before), *close_by(w))


def moves(pairs, sem, start=0):
    return [
        pltpu.make_async_copy(source, target, sem.at[start + n])
        for n, (source, target) in enumerate(pairs)
    ]


def entering_state(factors, states, number):
    state = factors[0, number] * states[number].astype(f32)
    state += factors[1, number] * states[HEADS + number].astype(f32)
    return state.astype(bf16)


def finish_body(
    slope, factors, x, qk, pre, far, near, wo, wi, wd,
    mixed, gated, ra, h2, r2, low, g, up, product, y,
    xv, qkv, vuv, statev, mixedv, gatedv, rav, h2v, r2v, lowv, gv, upv, productv, yv,
    attended, total, held, isem, osem, csem,
):
    rows, width = x.shape
    hidden = wd.shape[0]
    columns = held.shape[1]
    steps = hidden // columns
    ins = moves(
        (
            (qk, qkv), (pre.at[:, pl.ds(2 * width, 2 * width)], vuv),
            (far, statev.at[pl.ds(0, HEADS)]), (near, statev.at[pl.ds(HEADS, HEADS)]), (x, xv),
        ),
        isem,
    )
    for copy in ins:
        copy.start()
    for copy in ins[:4]:
        copy.wait()
    ahead = row_index(rows, LANES)

    def pair(i, carry):
        for m in range(4):
            n = i * 4 + m
            at = pl.multiple_of(n * LANES, LANES)
            lane = pl.ds(at, LANES)
            state = entering_state(factors, statev, n)
            lowv[n] = state
            query = qkv[:, lane]
            key = qkv[:, pl.ds(at + width, LANES)]
            weights = (decay_mask(slope[n], rows) * nt(query, key)).astype(bf16)
            inner = nn(weights, vuv[:, lane])
            carried = nn(query, state)
            attended[:, lane] = inner + jnp.exp(ahead * (-slope[n])) * carried
        return carry

    lax.fori_loop(0, HEADS // 4, pair, 0)
    rows_out = attended[...]
    factor = norm_factor(rows_out, width)
    rav[...] = jnp.broadcast_to(factor, rav.shape)
    normed = rows_out * factor
    mixedv[...] = normed.astype(bf16)
    gatedv[...] = (normed * vuv[:, width:].astype(f32)).astype(bf16)
    outs = moves(((mixedv, mixed), (gatedv, gated), (rav, ra), (lowv, low)), osem)
    for copy in outs:
        copy.start()
    ins[4].wait()
    middle = xv[...].astype(f32) + nn(gatedv[...], wo[...])
    total[...] = middle
    factor = norm_factor(middle, width)
    r2v[...] = jnp.broadcast_to(factor, r2v.shape)
    h2v[...] = (middle * factor).astype(bf16)
    more = moves(((h2v, h2), (r2v, r2)), osem, 4)
    for copy in more:
        copy.start()
    held[...] = jnp.zeros_like(held)

    def chunk_out(i):
        at = pl.ds(pl.multiple_of(i * columns, LANES), columns)
        return [
            pltpu.make_async_copy(source.at[:, at], target.at[:, at], csem.at[n, i])
            for n, (source, target) in enumerate(((gv, g), (upv, up), (productv, product)))
        ]

    def step(i, carry):
        start = pl.multiple_of(i * columns, LANES)
        before = pl.multiple_of(jnp.maximum(i - 1, 0) * columns, LANES)
        at = pl.ds(start, columns)
        total[...] += nn(held[...], wd[pl.ds(before, columns), :])
        gate = nn(h2v[...], wi[:, at])
        rise = nn(h2v[...], wi[:, pl.ds(start + hidden, columns)])
        both = (gate * rise).astype(bf16)
        gv[:, at] = gate.astype(bf16)
        upv[:, at] = rise.astype(bf16)
        productv[:, at] = both
        held[...] = both
        for copy in chunk_out(i):
            copy.start()
        return carry

    lax.fori_loop(0, steps, step, 0)
    yv[...] = (total[...] + nn(held[...], wd[hidden - columns :, :])).astype(bf16)
    last = moves(((yv, y),), osem, 6)
    for copy in last:
        copy.start()
    for copy in outs + more + last:
        copy.wait()

    def drain(i, carry):
        for copy in chunk_out(i):
            copy.wait()
        return carry

    lax.fori_loop(0, steps, drain, 0)


def finish(slopes, factors, x, qk, pre, entering, wo, wi, wd):
    rows, width = x.shape
    hidden = wd.shape[0]
    columns = 256
    steps = hidden // columns
    states = (HEADS, LANES, LANES)
    act = hbm((rows, width), bf16)
    factor = hbm((rows, LANES), f32)
    unit = hbm((rows, hidden), bf16)
    outs = [
        act, act, factor, act, factor, hbm(states, bf16), unit, unit, unit, act,
    ]
    return pl.pallas_call(
        finish_body,
        in_specs=[SMEM] * 2 + [ANY] * 5 + [VMEM] * 3,
        out_specs=[ANY] * len(outs),
        out_shape=outs,
        scratch_shapes=[
            pltpu.VMEM((rows, width), bf16),
            pltpu.VMEM((rows, 2 * width), bf16),
            pltpu.VMEM((rows, 2 * width), bf16),
            pltpu.VMEM((2 * HEADS, LANES, LANES), bf16),
        ]
        + [pltpu.VMEM(o.shape, o.dtype) for o in outs]
        + [
            pltpu.VMEM((rows, width), f32),
            pltpu.VMEM((rows, width), f32),
            pltpu.VMEM((rows, columns), bf16),
            pltpu.SemaphoreType.DMA((5,)),
            pltpu.SemaphoreType.DMA((7,)),
            pltpu.SemaphoreType.DMA((3, steps)),
        ],
        compiler_params=params(18),
        cost_estimate=pl.CostEstimate(
            flops=2 * rows * width * (width + 3 * hidden),
            bytes_accessed=2 * width * (width + 3 * hidden),
            transcendentals=0,
        ),
        name="finish",
    )(slopes, factors, *far_away(x, qk, pre, *entering), *close_by(wo, wi, wd))


def back_channel_body(
    slope, dy, wo, wi, wd, g, up, h2, r2, mixed, ra, qk, pre, low, cosine, sine, behind,
    dg, dup, dmid, dm, dq, du, dk, dv, state, joined,
    dyv, gv, upv, h2v, r2v, mixedv, rav, qkv, qpv, vuv, lowv, cv, sv, bv,
    dgv, dupv, dmidv, dmv, dqv, duv, dkv, dvv, statev, jv,
    total, datt, heldg, heldu, isem, osem, csem, psem,
):
    rows, width = dy.shape
    hidden = wd.shape[0]
    columns = heldg.shape[1]
    steps = hidden // columns
    ins = moves(
        (
            (dy, dyv), (g, gv), (up, upv), (h2, h2v), (r2, r2v), (mixed, mixedv), (ra, rav),
            (qk, qkv), (pre.at[:, pl.ds(0, width)], qpv),
            (pre.at[:, pl.ds(2 * width, 2 * width)], vuv), (low, lowv), (cosine, cv), (sine, sv),
            (behind, bv),
        ),
        isem,
    )
    for copy in ins[:3]:
        copy.start()
    for copy in ins[:3]:
        copy.wait()
    for copy in ins[3:]:
        copy.start()
    heldg[...] = jnp.zeros_like(heldg)
    heldu[...] = jnp.zeros_like(heldu)
    total[...] = jnp.zeros_like(total)

    def chunk_out(i):
        at = pl.ds(pl.multiple_of(i * columns, LANES), columns)
        return [
            pltpu.make_async_copy(source.at[:, at], target.at[:, at], csem.at[n, i])
            for n, (source, target) in enumerate(((dgv, dg), (dupv, dup)))
        ]

    def step(i, carry):
        at = pl.ds(pl.multiple_of(i * columns, LANES), columns)
        before = pl.multiple_of(jnp.maximum(i - 1, 0) * columns, LANES)
        total[...] += nt(heldg[...], wi[:, pl.ds(before, columns)]) + nt(
            heldu[...], wi[:, pl.ds(before + hidden, columns)]
        )
        product = nt(dyv[...], wd[at, :])
        left = (product * upv[:, at].astype(f32)).astype(bf16)
        right = (product * gv[:, at].astype(f32)).astype(bf16)
        dgv[:, at] = left
        dupv[:, at] = right
        heldg[...] = left
        heldu[...] = right
        for copy in chunk_out(i):
            copy.start()
        return carry

    lax.fori_loop(0, steps, step, 0)
    for copy in ins[3:]:
        copy.wait()
    dh2 = (
        total[...]
        + nt(heldg[...], wi[:, hidden - columns : hidden])
        + nt(heldu[...], wi[:, 2 * hidden - columns :])
    )
    middle = dyv[...].astype(f32) + norm_back(dh2, h2v[...].astype(f32), r2v[:, 0:1], width)
    dmidv[...] = middle
    dmv[...] = middle.astype(bf16)
    outs = moves(((dmidv, dmid), (dmv, dm)), osem)
    for copy in outs:
        copy.start()
    dgated = nt(dmv[...], wo[...])
    normed = mixedv[...].astype(f32)
    duv[...] = (dgated * normed).astype(bf16)
    back = norm_back(dgated * vuv[:, width:].astype(f32), normed, rav[:, 0:1], width)
    datt[...] = back.astype(bf16)
    ahead = row_index(rows, LANES)
    row = lax.broadcasted_iota(jnp.int32, (rows, rows), 0)
    column = lax.broadcasted_iota(jnp.int32, (rows, rows), 1)
    distance = (row - column).astype(f32)

    early = moves(((duv, du),), osem, 2)
    for copy in early:
        copy.start()

    def pair_out(i):
        at = pl.ds(pl.multiple_of(i * 2 * LANES, LANES), 2 * LANES)
        return [
            pltpu.make_async_copy(source.at[:, at], target.at[:, at], psem.at[n, i])
            for n, (source, target) in enumerate(((dqv, dq), (dkv, dk), (dvv, dv)))
        ]

    def some(i, carry):
        for m in range(2):
            n = i * 2 + m
            at = pl.multiple_of(n * LANES, LANES)
            lane = pl.ds(at, LANES)
            query, key = qkv[:, lane], qkv[:, pl.ds(at + width, LANES)]
            value, cot = vuv[:, lane], datt[:, lane]
            power = jnp.exp(jnp.abs(distance) * (-slope[n]))
            mask = jnp.where(distance >= 0.0, power, 0.0)
            flipped = jnp.where(distance <= 0.0, power, 0.0)
            weights_t = (flipped * nt(key, query)).astype(bf16)
            scores = (mask * nt(cot, value)).astype(bf16)
            scores_t = (flipped * nt(value, cot)).astype(bf16)
            scaled = (jnp.exp(ahead * (-slope[n])) * cot.astype(f32)).astype(bf16)
            own = tn(query, scaled)
            statev[n] = own.astype(bf16)
            jv[n] = join(slope[n], bv[n], own)
            dquery = nn(scores, key) + nt(scaled, lowv[n])
            turned = dquery * cv[...] + half_turn(dquery * sv[...])
            p = qpv[:, lane].astype(f32)
            s = sigmoid(p)
            dqv[:, lane] = (turned * (s * (1.0 + p * (1.0 - s)))).astype(bf16)
            dkv[:, lane] = nn(scores_t, query)
            dvv[:, lane] = nn(weights_t, cot)
        for copy in pair_out(i):
            copy.start()
        return carry

    lax.fori_loop(0, HEADS // 2, some, 0)
    last = moves(((statev, state), (jv, joined)), osem, 3)
    for copy in last:
        copy.start()
    for copy in outs + early + last:
        copy.wait()
    for i in range(HEADS // 2):
        for copy in pair_out(i):
            copy.wait()

    def drain(i, carry):
        for copy in chunk_out(i):
            copy.wait()
        return carry

    lax.fori_loop(0, steps, drain, 0)


def back_channel(slopes, dy, r, cosine, sine, behind, wo, wi, wd):
    rows, width = dy.shape
    hidden = wd.shape[0]
    columns = 256
    steps = hidden // columns
    states = (HEADS, LANES, LANES)
    act = hbm((rows, width), bf16)
    full = hbm((rows, width), f32)
    unit = hbm((rows, hidden), bf16)
    state = hbm(states, bf16)
    outs = [unit, unit, full, act, act, act, full, full, state, state]
    wide = pltpu.VMEM((rows, width), bf16)
    thin = pltpu.VMEM((rows, LANES), f32)
    twice = pltpu.VMEM((rows, 2 * width), bf16)
    tall = pltpu.VMEM((rows, hidden), bf16)
    return pl.pallas_call(
        back_channel_body,
        in_specs=[SMEM] + [ANY] + [VMEM] * 3 + [ANY] * 12,
        out_specs=[ANY] * len(outs),
        out_shape=outs,
        scratch_shapes=[
            wide, tall, tall, wide, thin, wide, thin, twice, wide, twice,
            pltpu.VMEM(states, bf16), thin, thin, pltpu.VMEM(states, bf16),
        ]
        + [pltpu.VMEM(o.shape, o.dtype) for o in outs]
        + [
            pltpu.VMEM((rows, width), f32),
            wide,
            pltpu.VMEM((rows, columns), bf16),
            pltpu.VMEM((rows, columns), bf16),
            pltpu.SemaphoreType.DMA((14,)),
            pltpu.SemaphoreType.DMA((5,)),
            pltpu.SemaphoreType.DMA((2, steps)),
            pltpu.SemaphoreType.DMA((3, HEADS // 2)),
        ],
        compiler_params=params(22),
        cost_estimate=pl.CostEstimate(
            flops=2 * rows * width * (width + 3 * hidden),
            bytes_accessed=2 * width * (width + 3 * hidden),
            transcendentals=0,
        ),
        name="back_channel",
    )(
        slopes, *far_away(dy), *close_by(wo, wi, wd),
        *far_away(
            r["g"], r["up"], r["h2"], r["r2"], r["mixed"], r["ra"], r["qk"], r["pre"], r["low"],
            cosine, sine, behind,
        ),
    )


def back_mixer_body(
    slope, factors, dq, du, dk, dv, qk, pre, far, near, cosine, sine, h1, r1, dmid, w,
    dkp, dvp, dx,
    dkin, dvin, kvv, kpv, vv, statev, cv, sv, h1v, r1v, dmidv, parts, dxv, total, isem, osem,
):
    rows, width = dq.shape
    ins = moves(
        (
            (dk, dkin), (dv, dvin), (qk.at[:, pl.ds(width, width)], kvv),
            (pre.at[:, pl.ds(width, width)], kpv), (pre.at[:, pl.ds(2 * width, width)], vv),
            (far, statev.at[pl.ds(0, HEADS)]), (near, statev.at[pl.ds(HEADS, HEADS)]),
            (cosine, cv), (sine, sv),
            (dq, parts.at[:, pl.ds(0, width)]), (du, parts.at[:, pl.ds(3 * width, width)]),
            (h1, h1v), (r1, r1v), (dmid, dmidv),
        ),
        isem,
    )
    for copy in ins:
        copy.start()
    for copy in ins[:9]:
        copy.wait()
    ahead = rows - row_index(rows, LANES)

    def some(i, carry):
        for m in range(4):
            n = i * 4 + m
            at = pl.multiple_of(n * LANES, LANES)
            lane = pl.ds(at, LANES)
            state = entering_state(factors, statev, n)
            decay = jnp.exp(ahead * (-slope[n]))
            keyed = (kvv[:, lane].astype(f32) * decay).astype(bf16)
            dkey = dkin[:, lane] + decay * nt(vv[:, lane], state)
            turned = dkey * cv[...] + half_turn(dkey * sv[...])
            p = kpv[:, lane].astype(f32)
            s = sigmoid(p)
            parts[:, pl.ds(at + width, LANES)] = (turned * (s * (1.0 + p * (1.0 - s)))).astype(bf16)
            parts[:, pl.ds(at + 2 * width, LANES)] = (dvin[:, lane] + nn(keyed, state)).astype(bf16)
        return carry

    lax.fori_loop(0, HEADS // 4, some, 0)
    outs = moves(
        ((parts.at[:, pl.ds(width, width)], dkp), (parts.at[:, pl.ds(2 * width, width)], dvp)), osem
    )
    for copy in outs:
        copy.start()
    for copy in ins[9:]:
        copy.wait()
    columns = 512

    def step(j, carry):
        at = pl.ds(pl.multiple_of(j * columns, LANES), columns)
        total[:, at] = nt(parts[...], w[at, :])
        return carry

    lax.fori_loop(0, width // columns, step, 0)
    back = norm_back(total[...], h1v[...].astype(f32), r1v[:, 0:1], width)
    dxv[...] = (dmidv[...] + back).astype(bf16)
    last = moves(((dxv, dx),), osem, 2)
    for copy in last:
        copy.start()
    for copy in outs + last:
        copy.wait()


def back_mixer(slopes, factors, r, entering, cosine, sine, w):
    rows, width = r["dq"].shape
    act = hbm((rows, width), bf16)
    wide = pltpu.VMEM((rows, width), bf16)
    full = pltpu.VMEM((rows, width), f32)
    thin = pltpu.VMEM((rows, LANES), f32)
    return pl.pallas_call(
        back_mixer_body,
        in_specs=[SMEM] * 2 + [ANY] * 13 + [VMEM],
        out_specs=[ANY] * 3,
        out_shape=[act, act, act],
        scratch_shapes=[
            full, full, wide, wide, wide, pltpu.VMEM((2 * HEADS, LANES, LANES), bf16), thin, thin,
            wide, thin,
            full,
            pltpu.VMEM((rows, w.shape[1]), bf16), wide, full,
            pltpu.SemaphoreType.DMA((14,)),
            pltpu.SemaphoreType.DMA((3,)),
        ],
        compiler_params=params(14),
        cost_estimate=pl.CostEstimate(
            flops=2 * rows * width * w.shape[1],
            bytes_accessed=2 * width * w.shape[1],
            transcendentals=0,
        ),
        name="back_mixer",
    )(
        slopes, factors,
        *far_away(
            r["dq"], r["du"], r["dk"], r["dv"], r["qk"], r["pre"], *entering, cosine, sine,
            r["h1"], r["r1"], r["dmid"],
        ),
        *close_by(w),
    )


def weight_body(*refs, batch, sides, groups):
    place = refs[0]
    lefts = refs[1 : 1 + 2 * batch]
    rights = refs[1 + 2 * batch : 1 + 2 * batch + 2 * batch * sides]
    outs = refs[1 + 2 * batch + 2 * batch * sides : -7]
    x, xt, ys, stage, xsem, ysem, osem = refs[-7:]
    rows = lefts[0].shape[0]
    columns = x.shape[1]
    quarter = columns // 4
    blocks = groups[0][2]

    def left_copies(section):
        return [
            pltpu.make_async_copy(
                lefts[section * batch + b], x.at[pl.ds(b * rows, rows)], xsem.at[b]
            )
            for b in range(batch)
        ]

    def right_copies(section, s):
        return [
            pltpu.make_async_copy(
                rights[(section * sides + s) * batch + b],
                ys.at[s, pl.ds(b * rows, rows)],
                ysem.at[s, b],
            )
            for b in range(batch)
        ]

    for section in range(2):

        @pl.when(place[4] == section)
        def _():
            for copy in left_copies(section):
                copy.start()
            for s in range(sides):
                for copy in right_copies(section, s):
                    copy.start()

    for copy in left_copies(0):
        copy.wait()
    for piece in range(columns // LANES):
        xt[piece * LANES : (piece + 1) * LANES, :] = x[:, piece * LANES : (piece + 1) * LANES].T

    def move(number, role, out):
        slot = number * 4 + role
        return pltpu.make_async_copy(
            stage.at[slot], out.at[pl.ds((role % 2) * blocks, blocks)], osem.at[slot]
        )

    def one(role, number, side, start):
        left = xt[pl.ds(pl.multiple_of(place[role] * quarter, 16), quarter), :]
        tile = nn(left, ys[side, :, start * LANES : (start + blocks) * LANES]).astype(bf16)
        for n in range(blocks):
            stage[number * 4 + role, n] = tile[:, head(n)]

    for number, (side, start, _) in enumerate(groups):
        if all(side != done for done, _, _ in groups[:number]):
            for copy in right_copies(0, side):
                copy.wait()

        def step(role, carry, number=number, side=side, start=start):
            one(role, number, side, start)

            @pl.when(role < 2)
            def _():
                move(number, role, outs[2 * number]).start()

            @pl.when(role >= 2)
            def _():
                move(number, role, outs[2 * number + 1]).start()

            return carry

        lax.fori_loop(0, 4, step, 0)
    for number in range(len(groups)):
        for role in range(4):
            move(number, role, outs[2 * number + role // 2]).wait()


def weight_gradient(place, lefts, rights, groups):
    batch = len(lefts[0])
    sides = len(rights[0])
    rows, columns = lefts[0][0].shape
    span = rights[0][0][0].shape[1]
    quarter = columns // 4
    blocks = groups[0][2]
    flat_left = [a for section in lefts for a in section]
    flat_right = [a for section in rights for side in section for a in side]
    out = pl.pallas_call(
        functools.partial(weight_body, batch=batch, sides=sides, groups=groups),
        in_specs=[SMEM] + [ANY] * (len(flat_left) + len(flat_right)),
        out_specs=[ANY] * (2 * len(groups)),
        out_shape=[hbm((2 * blocks, quarter, LANES), bf16)] * (2 * len(groups)),
        scratch_shapes=[
            pltpu.VMEM((batch * rows, columns), bf16),
            pltpu.VMEM((columns, batch * rows), bf16),
            pltpu.VMEM((sides, batch * rows, span), bf16),
            pltpu.VMEM((4 * len(groups), blocks, quarter, LANES), bf16),
            pltpu.SemaphoreType.DMA((batch,)),
            pltpu.SemaphoreType.DMA((sides, batch)),
            pltpu.SemaphoreType.DMA((4 * len(groups),)),
        ],
        compiler_params=params(24),
        cost_estimate=pl.CostEstimate(
            flops=2 * batch * rows * columns * sides * span,
            bytes_accessed=2 * columns * sides * span,
            transcendentals=0,
        ),
        name="weight_gradient",
    )(place, *far_away(*flat_left, *flat_right))
    return [(out[2 * n], out[2 * n + 1]) for n in range(len(groups))]


def settle_body(edge, outer, inner, *rest):
    out = rest[-1]

    @pl.when(edge[0] == 1)
    def _():
        for n in range(outer.shape[0]):
            out[:, head(n)] = outer[n].astype(f32)

    @pl.when(edge[0] == 0)
    def _():
        for n in range(inner.shape[0]):
            out[:, head(n)] = inner[n].astype(f32)


def settle(edge, outer, inner, total, held, number):
    blocks, quarter, _ = outer.shape
    more = [] if held is None else [held]
    return pl.pallas_call(
        settle_body,
        grid=(1,),
        in_specs=[SMEM, whole(outer.shape), whole(inner.shape)] + [ANY] * len(more),
        out_specs=pl.BlockSpec((quarter, blocks * LANES), lambda j: (0, number)),
        out_shape=hbm((quarter, total), f32),
        input_output_aliases={3: 0} if more else {},
        compiler_params=params(8),
        name="settle",
    )(edge, outer, inner, *more)


def add(a, b):
    return (a.astype(f32) + b.astype(f32)).astype(bf16)


def gathered_state(own, slopes, forward):
    count = lax.axis_size("seq")
    place = lax.axis_index("seq")
    gathered = lax.all_gather(own, "seq").astype(f32)
    device = jnp.arange(count)
    distance = place - 1 - device if forward else device - place - 1
    power = jnp.maximum(distance, 0).astype(f32) * BLK
    weight = jnp.where(distance[:, None] >= 0, jnp.exp(-slopes[None] * power[:, None]), 0.0)
    return jnp.sum(weight[:, :, None, None] * gathered, axis=0).astype(bf16)


def halves(first, second):
    place = lax.axis_index("seq")
    sent = jnp.where(place % 2 == 1, first, second)
    one = lax.ppermute(sent, "seq", [(1, 0), (2, 3), (0, 2), (3, 1)])
    two = lax.ppermute(jnp.where(place == 1, second, first), "seq", [(2, 1), (1, 2)])
    return (
        jnp.where(place == 0, first, jnp.where(place == 1, two, one)),
        jnp.where(place == 3, second, jnp.where(place == 2, two, one)),
    )


def quarters(low, high):
    place = lax.axis_index("seq")
    one = lax.ppermute(jnp.where(place < 2, high, low), "seq", [(0, 1), (3, 2), (2, 0), (1, 3)])
    two = lax.ppermute(jnp.where(place == 1, low, high), "seq", [(1, 2), (2, 1)])
    return (
        jnp.where(place == 0, low, jnp.where(place == 2, two, one)),
        jnp.where(place == 3, high, jnp.where(place == 1, two, one)),
    )


class Sums:
    def __init__(self, edge, settled):
        self.edge = edge
        self.settled = settled
        self.waiting, self.parts, self.partial, self.across = [], [], [], []
        self.previous = None
        self.step = 0
        self.marks = []
        self.written = None

    def load(self, chunks):
        for given, kept in chunks:
            blocks = given.shape[0] // 2
            taken = lax.ppermute(given, "seq", [(0, 1), (1, 0), (2, 3), (3, 2)])
            self.waiting.append(
                (add(kept[:blocks], taken[:blocks]), add(kept[blocks:], taken[blocks:]))
            )

    def over_y(self):
        if not self.waiting:
            return
        far, own = self.waiting.pop(0)
        if self.previous is not None:
            far, _ = lax.optimization_barrier((far, self.previous))
        self.marks.append(far)
        self.previous = lax.ppermute(far, "seq", [(0, 2), (2, 0), (1, 3), (3, 1)])
        self.parts.append(add(own, self.previous))

    def over_z(self, last=False):
        step, count = self.step, len(self.parts)
        if step >= count + 2 or (step >= count and not last):
            return False
        part = self.parts[step] if step < count else None
        done = None
        if step >= 2:
            done = self.partial[step - 2].astype(f32) + self.across[step - 2].astype(f32)
        if part is not None and self.written is not None:
            part, _ = lax.optimization_barrier((part, self.written))
            self.written = None
        if 1 <= step <= count:
            self.marks.append(self.partial[step - 1])
            self.across.append(lax.ppermute(self.partial[step - 1], "dp", [(1, 2), (2, 1)]))
        if part is not None and done is not None and part.shape == done.shape:
            sent = jnp.where(self.edge, part.astype(f32), done).astype(bf16)
            self.marks.append(sent)
            got = lax.ppermute(sent, "dp", [(0, 1), (1, 0), (2, 3), (3, 2)])
            self.partial.append(add(part, got))
            self.written = self.settled(got, sent)
        else:
            if part is not None:
                self.marks.append(part)
                self.partial.append(add(part, lax.ppermute(part, "dp", [(0, 1), (3, 2)])))
            if done is not None:
                done = done.astype(bf16)
                self.marks.append(done)
                self.written = self.settled(lax.ppermute(done, "dp", [(1, 0), (2, 3)]), done)
        self.step += 1
        return True

    def started(self):
        marks, self.marks = self.marks, []
        return marks


def angle_tables(position_row, half_size):
    frequency = jnp.exp(
        jnp.arange(half_size, dtype=jnp.float32) * (-math.log(theta_base) / half_size)
    )
    angles = position_row.astype(jnp.float32)[..., None] * frequency
    cosine = jnp.cos(angles)
    sine_rows = jnp.sin(angles)
    return (
        jnp.concatenate([cosine, cosine], axis=-1),
        jnp.concatenate([-sine_rows, sine_rows], axis=-1),
    )


class Order:
    def __init__(self):
        self.last = []

    def after(self, value):
        if self.last:
            value = lax.optimization_barrier((value, *self.last))[0]
        return value

    def at(self, *values):
        self.last = list(values)


class Layer:
    def __init__(self, order, slopes, factors, chained, cosine, sine, weights):
        self.order, self.slopes, self.factors, self.chained = order, slopes, factors, chained
        self.cosine, self.sine = cosine, sine
        self.w, self.wo, self.wi, self.wd = weights
        self.blocks = [None, None]
        self.entering = [None, None]
        self.later = [None, None]
        self.zero = jnp.zeros((HEADS, LANES, LANES), bf16)

    def first(self, b, x):
        before = self.blocks[0]["state"] if b == 1 else self.zero
        h1, r1, pre, qk, state, joined = project(
            self.order.after(self.slopes), x, self.cosine[b], self.sine[b], before, self.w
        )
        self.order.at(r1)
        self.blocks[b] = dict(x=x, h1=h1, r1=r1, pre=pre, qk=qk, state=state)
        if not self.chained:
            self.entering[b] = gathered_state(state, self.slopes, True)
        elif b == 1:
            near = lax.ppermute(joined, "seq", [(0, 1), (2, 3)])
            self.entering = [near, near]

    def second(self, b):
        r = self.blocks[b]
        near = self.blocks[0]["state"] if b == 1 else self.entering[b]
        mixed, gated, ra, h2, r2, low, g, up, product, y = finish(
            self.order.after(self.slopes), self.factors[b], r["x"], r["qk"], r["pre"],
            (self.entering[b], near), self.wo, self.wi, self.wd,
        )
        self.order.at(ra)
        r.update(
            mixed=mixed, gated=gated, ra=ra, h2=h2, r2=r2, low=low, g=g, up=up, product=product
        )
        return y

    def back_first(self, b, dy):
        r = self.blocks[b]
        behind = self.blocks[1]["dstate"] if b == 0 else self.zero
        dg, dup, dmid, dm, dq, du, dk, dv, state, joined = back_channel(
            self.order.after(self.slopes), dy, r, self.cosine[b], self.sine[b], behind,
            self.wo, self.wi, self.wd,
        )
        self.order.at(dm)
        r.update(dy=dy, dg=dg, dup=dup, dmid=dmid, dm=dm, dq=dq, du=du, dk=dk, dv=dv, dstate=state)
        if not self.chained:
            self.later[b] = gathered_state(state, self.slopes, False)
        elif b == 0:
            near = lax.ppermute(joined, "seq", [(1, 0), (3, 2)])
            self.later = [near, near]

    def back_second(self, b):
        r = self.blocks[b]
        near = self.blocks[1]["dstate"] if b == 0 else self.later[b]
        dkp, dvp, dx = back_mixer(
            self.order.after(self.slopes), self.factors[1 - b], r, (self.later[b], near),
            self.cosine[b], self.sine[b], self.w,
        )
        self.order.at(dkp)
        r.update(dkp=dkp, dvp=dvp)
        return dx


def per_device(boundary, positions, decay_exp, mixer_in, mixer_out, channel_in, channel_out):
    section = lax.axis_index("section")
    is_first = section == 0
    batch, rows, width = boundary.shape[1:]
    assert rows == BLK and batch == 2
    slopes = jnp.exp2(-0.5 * decay_exp[0].astype(jnp.float32))
    w, wo, wi, wd = weights = mixer_in[0], mixer_out[0], channel_in[0], channel_out[0]
    hidden = wd.shape[0]
    half_size = width // HEADS // 2
    usual = lax.axis_size("seq") == 4 and lax.axis_size("dp") == 4
    place, line = lax.axis_index("seq"), lax.axis_index("dp")
    core, y_place = place % 2, place // 2

    own = (boundary[0, 0], boundary[0, 1])
    if usual:
        own = halves(*own)
        every = lax.all_gather(positions, "seq")
        chosen = lax.dynamic_index_in_dim(every, y_place, 1, keepdims=False)
        positions = lax.dynamic_slice_in_dim(chosen, 2 * core, 2, 0)
    cosine, sine = angle_tables(positions, half_size)

    roles = [
        2 * (1 - y_place) + 1 - core,
        2 * y_place + 1 - core,
        2 * (1 - y_place) + core,
        2 * y_place + core,
    ]
    if not usual:
        roles = [0, 1, 2, 3]
    roles = jnp.stack([jnp.asarray(r, jnp.int32) for r in (*roles, section)])
    edge = (line == 0) | (line == lax.axis_size("dp") - 1)
    flag = edge.astype(jnp.int32)[None]
    one = jnp.ones_like(slopes)
    factors = [jnp.stack([one, 0.0 * one])] * 2
    if usual:
        factors[1] = jnp.stack([jnp.exp(-slopes * BLK), one])
    roles, flag, slopes, *factors = lax.optimization_barrier((roles, flag, slopes, *factors))
    edge = flag[0] == 1
    order = Order()
    order.at(roles, flag)
    layers = [
        Layer(order, slopes, factors, usual, cosine, sine, weights) for section_of_it in range(2)
    ]
    early, late = layers

    for b in range(2):
        early.first(b, own[b])
    arrived = [lax.ppermute(early.second(b), "section", [(0, 1)]) for b in range(2)]
    for b in range(2):
        late.first(b, arrived[b])
    outputs = [late.second(b) for b in range(2)]
    for b in (1, 0):
        late.back_first(b, own[b])
    returned = [None, None]
    for b in (1, 0):
        returned[b] = lax.ppermute(late.back_second(b), "section", [(1, 0)])

    def operands(*names):
        return [[[r[name] for r in layer.blocks] for name in names] for layer in layers]

    chunks = []
    spans = [(3, width), (3, width)] + [(2, 2 * hidden)] * 4 + [(1, width)] + [(0, 4 * width)] * 4
    numbers = [0, 1, 0, 1, 2, 3, 0, 0, 1, 2, 3]
    held = [None] * 4
    finished = []

    def settled(outer, inner):
        number = len(finished)
        index, total = spans[number]
        blocks, quarter = chunks[number][0].shape[0] // 2, chunks[number][0].shape[1]
        shape = (blocks, quarter, LANES)
        finished.append(number)
        held[index] = settle(
            flag, outer.reshape(shape), inner.reshape(shape), total, held[index], numbers[number]
        )
        return held[index]

    sums = Sums(edge, settled)

    def even(array):
        return array.reshape(array.shape[0] * array.shape[1] // 256, 256, LANES)

    def gradient(name, names, groups):
        left = [side[0] for side in operands(name)]
        found = weight_gradient(order.after(roles), left, operands(*names), groups)
        order.at(found[-1][1])
        chunks.extend(found)
        if usual:
            sums.load([(even(given), even(kept)) for given, kept in found])

    def move(*what):
        if not usual:
            return
        for way in what:
            way()
        order.at(*order.last, *sums.started())

    half, eight = hidden // LANES // 2, width // LANES
    early.back_first(1, returned[1])
    early.blocks[0]["dy"] = returned[0]
    gradient("product", ("dy",), [(0, 0, 4), (0, 4, 4)])
    move(sums.over_y)
    early.back_first(0, returned[0])
    pass
    gradient("h2", ("dg", "dup"), [(0, 0, half), (0, half, half), (1, 0, half), (1, half, half)])
    pass
    dx = [None, None]
    for b in (1, 0):
        dx[b] = early.back_second(b)
    move(sums.over_y, sums.over_z)
    gradient("gated", ("dm",), [(0, 0, eight)])
    gradient("h1", ("dq", "dkp", "dvp", "du"), [(s, 0, eight) for s in range(4)])

    ends = [jnp.where(is_first, dx[b], outputs[b]) for b in range(2)]
    joined = jnp.stack(quarters(*ends) if usual else ends)[None]
    if usual:
        while sums.waiting:
            move(sums.over_y, sums.over_z)
        while sums.over_z(last=True):
            pass
        return (joined, *(h[None] for h in held))
    found = [[], [], [], []]
    for (index, total), chunk in zip(spans, chunks):
        chunk = jnp.concatenate(chunk)
        blocks, quarter = chunk.shape[0] // 4, chunk.shape[1]
        rows_first = chunk.reshape(4, blocks, quarter, LANES).transpose(0, 2, 1, 3)
        found[index].append(rows_first.reshape(4 * quarter, blocks * LANES))
    summed = []
    for pieces in found:
        part = lax.psum_scatter(
            jnp.concatenate(pieces, axis=1), "seq", scatter_dimension=0, tiled=True
        )
        summed.append(lax.psum(part, "dp").astype(f32)[None])
    return (joined, *summed)


def solution(mesh):
    in_specs = (
        P("section", "dp", "seq", None),
        P("dp", "seq"),
        P("section", None),
        P("section", None, None),
        P("section", None, None),
        P("section", None, None),
        P("section", None, None),
    )
    out_specs = (
        P("section", "dp", "seq", None),
        P("section", "seq", None),
        P("section", "seq", None),
        P("section", "seq", None),
        P("section", "seq", None),
    )
    return jax.shard_map(
        per_device, mesh=mesh, in_specs=in_specs, out_specs=out_specs, check_vma=False
    )
```

```python
import functools
import math

import jax
import jax.numpy as jnp
from jax import lax
from jax.experimental import pallas as pl
from jax.experimental.pallas import tpu as pltpu
from jax.sharding import PartitionSpec as P

HEADS = 8
BLK = 256
LANES = 128
STEPS = 8

epsilon = 1e-06
theta_base = 10000.0
f32 = jnp.float32
bf16 = jnp.bfloat16


def nn(a, b):
    return jnp.dot(a, b, preferred_element_type=f32)


def nt(a, b):
    return lax.dot_general(a, b, (((1,), (1,)), ((), ())), preferred_element_type=f32)


def tn(a, b):
    return lax.dot_general(a, b, (((0,), (0,)), ((), ())), preferred_element_type=f32)


def sigmoid(v):
    return 1.0 / (1.0 + jnp.exp(-v))


def norm_factor(v, width):
    return lax.rsqrt(jnp.sum(v * v, axis=-1, keepdims=True) * (1.0 / width) + epsilon)


def norm_back(cotangent, normed, factor, width):
    mean = jnp.sum(cotangent * normed, axis=-1, keepdims=True) * (1.0 / width)
    return factor * (cotangent - normed * mean)


def row_index(rows, columns):
    return lax.broadcasted_iota(jnp.int32, (rows, columns), 0).astype(f32)


def decay_mask(slope, rows):
    row = lax.broadcasted_iota(jnp.int32, (rows, rows), 0)
    column = lax.broadcasted_iota(jnp.int32, (rows, rows), 1)
    distance = jnp.maximum(row - column, 0).astype(f32)
    return jnp.where(row >= column, jnp.exp(distance * (-slope)), 0.0)


def head(number):
    return slice(number * LANES, (number + 1) * LANES)


def half_turn(v):
    return pltpu.roll(v, LANES // 2, 1)


def whole(shape):
    return pl.BlockSpec(shape, lambda j: (0,) * len(shape))


def hbm(shape, kind):
    return pltpu.HBM(tuple(shape), kind)


def far_away(*arrays):
    return [pltpu.with_memory_space_constraint(a, pltpu.HBM) for a in arrays]


def close_by(*arrays):
    return [pltpu.with_memory_space_constraint(a, pltpu.VMEM) for a in arrays]


def params(megabytes):
    return pltpu.CompilerParams(vmem_limit_bytes=megabytes * 1024 * 1024)


SMEM = pl.BlockSpec(memory_space=pltpu.SMEM)
ANY = pl.BlockSpec(memory_space=pltpu.HBM)
VMEM = pl.BlockSpec(memory_space=pltpu.VMEM)
FREE = pl.BlockSpec(memory_space=pl.ANY)


def tables(position, rows):
    lane = lax.broadcasted_iota(jnp.int32, (rows, LANES), 1)
    half = LANES // 2
    feature = jnp.where(lane < half, lane, lane - half).astype(f32)
    frequency = jnp.exp(feature * (-math.log(theta_base) / half))
    angle = position * frequency
    return jnp.cos(angle), jnp.where(lane < half, -jnp.sin(angle), jnp.sin(angle))


def join(slope, before, own):
    decay = jnp.exp(jnp.full((LANES, LANES), -BLK, f32) * slope)
    return (decay * before.astype(f32) + own).astype(bf16)


def project_body(slope, x, cosine, sine, before, w, h1, r1, pre, qk, state, joined,
                 xv, cv, sv, bv, hv, rv, prev, qkv, stv, jv, isem, osem, qsem):
    rows, width = x.shape
    steps = STEPS
    columns = w.shape[1] // steps
    heads = columns // LANES
    first = [
        pltpu.make_async_copy(source, target, isem.at[n])
        for n, (source, target) in enumerate(((x, xv), (cosine, cv), (sine, sv), (before, bv)))
    ]
    for copy in first:
        copy.start()

    first[0].wait()
    v = xv[...].astype(f32)
    factor = norm_factor(v, width)
    hv[...] = (v * factor).astype(bf16)
    rv[...] = jnp.broadcast_to(factor, rv.shape)
    for copy in first[1:]:
        copy.wait()
    outs = [pltpu.make_async_copy(hv, h1, osem.at[0]), pltpu.make_async_copy(rv, r1, osem.at[1])]
    for copy in outs:
        copy.start()

    def pre_out(j):
        at = pl.ds(pl.multiple_of(j * columns, LANES), columns)
        return pltpu.make_async_copy(prev.at[:, at], pre.at[:, at], osem.at[3 + j])

    def qk_out(j):
        at = pl.ds(pl.multiple_of(j * columns, LANES), columns)
        return pltpu.make_async_copy(qkv.at[:, at], qk.at[:, at], qsem.at[j])

    def step(j, carry):
        at = pl.multiple_of(j * columns, LANES)
        p = nn(hv[...], w[:, pl.ds(at, columns)])
        prev[:, pl.ds(at, columns)] = p.astype(bf16)
        pre_out(j).start()

        @pl.when(j < steps // 2)
        def _():
            for n in range(heads):
                v = p[:, head(n)]
                v = v * sigmoid(v)
                turned = v * cv[...] + half_turn(v) * sv[...]
                qkv[:, pl.ds(at + n * LANES, LANES)] = turned.astype(bf16)
            qk_out(j).start()

        @pl.when((j >= steps // 2) & (j < 3 * steps // 4))
        def _():
            values = p.astype(bf16)
            ahead = rows - row_index(rows, LANES)
            for n in range(heads):
                number = (j - steps // 2) * heads + n
                decay = jnp.exp(ahead * (-slope[number]))
                key = qkv[:, pl.ds(at - width + n * LANES, LANES)]
                keyed = (key.astype(f32) * decay).astype(bf16)
                own = tn(keyed, values[:, head(n)])
                stv[number] = own.astype(bf16)
                jv[number] = join(slope[number], bv[number], own)

        return carry

    lax.fori_loop(0, steps, step, 0)
    last = [
        pltpu.make_async_copy(stv, state, osem.at[11]),
        pltpu.make_async_copy(jv, joined, osem.at[12]),
    ]
    for copy in last:
        copy.start()
    for copy in outs + last:
        copy.wait()
    for j in range(steps):
        pre_out(j).wait()
    for j in range(steps // 2):
        qk_out(j).wait()


def project(slopes, x, cosine, sine, before, w):
    rows, width = x.shape
    total = w.shape[1]
    states = (HEADS, LANES, LANES)
    return pl.pallas_call(
        project_body,
        in_specs=[SMEM, FREE] + [ANY] * 3 + [VMEM],
        out_specs=[ANY] * 6,
        out_shape=[
            hbm((rows, width), bf16),
            hbm((rows, LANES), f32),
            hbm((rows, total), bf16),
            hbm((rows, total // 2), bf16),
            hbm(states, bf16),
            hbm(states, bf16),
        ],
        scratch_shapes=[
            pltpu.VMEM((rows, width), bf16),
            pltpu.VMEM((rows, LANES), f32),
            pltpu.VMEM((rows, LANES), f32),
            pltpu.VMEM(states, bf16),
            pltpu.VMEM((rows, width), bf16),
            pltpu.VMEM((rows, LANES), f32),
            pltpu.VMEM((rows, total), bf16),
            pltpu.VMEM((rows, total // 2), bf16),
            pltpu.VMEM(states, bf16),
            pltpu.VMEM(states, bf16),
            pltpu.SemaphoreType.DMA((4,)),
            pltpu.SemaphoreType.DMA((13,)),
            pltpu.SemaphoreType.DMA((STEPS // 2,)),
        ],
        compiler_params=params(8),
        cost_estimate=pl.CostEstimate(
            flops=2 * rows * width * total, bytes_accessed=2 * width * total, transcendentals=0
        ),
        name="project",
    )(slopes, x, *far_away(cosine, sine, before), *close_by(w))


def moves(pairs, sem, start=0):
    return [
        pltpu.make_async_copy(source, target, sem.at[start + n])
        for n, (source, target) in enumerate(pairs)
    ]


def entering_state(factors, states, number):
    state = factors[0, number] * states[number].astype(f32)
    state += factors[1, number] * states[HEADS + number].astype(f32)
    return state.astype(bf16)


def finish_body(
    slope, factors, x, qk, pre, far, near, wo, wi, wd,
    mixed, gated, ra, h2, r2, low, g, up, product, y,
    xv, qkv, vuv, statev, mixedv, gatedv, rav, h2v, r2v, lowv, gv, upv, productv, yv,
    attended, total, held, isem, osem, csem,
):
    rows, width = x.shape
    hidden = wd.shape[0]
    columns = held.shape[1]
    steps = hidden // columns
    ins = moves(
        (
            (qk, qkv), (pre.at[:, pl.ds(2 * width, 2 * width)], vuv),
            (far, statev.at[pl.ds(0, HEADS)]), (near, statev.at[pl.ds(HEADS, HEADS)]), (x, xv),
        ),
        isem,
    )
    for copy in ins:
        copy.start()
    for copy in ins[:4]:
        copy.wait()
    ahead = row_index(rows, LANES)

    def pair(i, carry):
        for m in range(2):
            n = i * 2 + m
            at = pl.multiple_of(n * LANES, LANES)
            lane = pl.ds(at, LANES)
            state = entering_state(factors, statev, n)
            lowv[n] = state
            query = qkv[:, lane]
            key = qkv[:, pl.ds(at + width, LANES)]
            weights = (decay_mask(slope[n], rows) * nt(query, key)).astype(bf16)
            inner = nn(weights, vuv[:, lane])
            carried = nn(query, state)
            attended[:, lane] = inner + jnp.exp(ahead * (-slope[n])) * carried
        return carry

    lax.fori_loop(0, HEADS // 2, pair, 0)
    rows_out = attended[...]
    factor = norm_factor(rows_out, width)
    rav[...] = jnp.broadcast_to(factor, rav.shape)
    normed = rows_out * factor
    mixedv[...] = normed.astype(bf16)
    gatedv[...] = (normed * vuv[:, width:].astype(f32)).astype(bf16)
    outs = moves(((mixedv, mixed), (gatedv, gated), (rav, ra), (lowv, low)), osem)
    for copy in outs:
        copy.start()
    ins[4].wait()
    middle = xv[...].astype(f32) + nn(gatedv[...], wo[...])
    total[...] = middle
    factor = norm_factor(middle, width)
    r2v[...] = jnp.broadcast_to(factor, r2v.shape)
    h2v[...] = (middle * factor).astype(bf16)
    more = moves(((h2v, h2), (r2v, r2)), osem, 4)
    for copy in more:
        copy.start()
    held[...] = jnp.zeros_like(held)

    def chunk_out(i):
        at = pl.ds(pl.multiple_of(i * columns, LANES), columns)
        return [
            pltpu.make_async_copy(source.at[:, at], target.at[:, at], csem.at[n, i])
            for n, (source, target) in enumerate(((gv, g), (upv, up), (productv, product)))
        ]

    def step(i, carry):
        start = pl.multiple_of(i * columns, LANES)
        before = pl.multiple_of(jnp.maximum(i - 1, 0) * columns, LANES)
        at = pl.ds(start, columns)
        total[...] += nn(held[...], wd[pl.ds(before, columns), :])
        gate = nn(h2v[...], wi[:, at])
        rise = nn(h2v[...], wi[:, pl.ds(start + hidden, columns)])
        both = (gate * rise).astype(bf16)
        gv[:, at] = gate.astype(bf16)
        upv[:, at] = rise.astype(bf16)
        productv[:, at] = both
        held[...] = both
        for copy in chunk_out(i):
            copy.start()
        return carry

    lax.fori_loop(0, steps, step, 0)
    yv[...] = (total[...] + nn(held[...], wd[hidden - columns :, :])).astype(bf16)
    last = moves(((yv, y),), osem, 6)
    for copy in last:
        copy.start()
    for copy in outs + more + last:
        copy.wait()

    def drain(i, carry):
        for copy in chunk_out(i):
            copy.wait()
        return carry

    lax.fori_loop(0, steps, drain, 0)


def finish(slopes, factors, x, qk, pre, entering, wo, wi, wd):
    rows, width = x.shape
    hidden = wd.shape[0]
    columns = 256
    steps = hidden // columns
    states = (HEADS, LANES, LANES)
    act = hbm((rows, width), bf16)
    factor = hbm((rows, LANES), f32)
    unit = hbm((rows, hidden), bf16)
    outs = [
        act, act, factor, act, factor, hbm(states, bf16), unit, unit, unit, act,
    ]
    return pl.pallas_call(
        finish_body,
        in_specs=[SMEM] * 2 + [FREE] + [ANY] * 2 + [FREE] * 2 + [VMEM] * 3,
        out_specs=[ANY] * len(outs),
        out_shape=outs,
        scratch_shapes=[
            pltpu.VMEM((rows, width), bf16),
            pltpu.VMEM((rows, 2 * width), bf16),
            pltpu.VMEM((rows, 2 * width), bf16),
            pltpu.VMEM((2 * HEADS, LANES, LANES), bf16),
        ]
        + [pltpu.VMEM(o.shape, o.dtype) for o in outs]
        + [
            pltpu.VMEM((rows, width), f32),
            pltpu.VMEM((rows, width), f32),
            pltpu.VMEM((rows, columns), bf16),
            pltpu.SemaphoreType.DMA((5,)),
            pltpu.SemaphoreType.DMA((7,)),
            pltpu.SemaphoreType.DMA((3, steps)),
        ],
        compiler_params=params(18),
        cost_estimate=pl.CostEstimate(
            flops=2 * rows * width * (width + 3 * hidden),
            bytes_accessed=2 * width * (width + 3 * hidden),
            transcendentals=0,
        ),
        name="finish",
    )(slopes, factors, x, *far_away(qk, pre), *entering, *close_by(wo, wi, wd))


def back_channel_body(
    slope, dy, wo, wi, wd, g, up, h2, r2, mixed, ra, qk, pre, low, cosine, sine, behind,
    dg, dup, dmid, dm, dq, du, dk, dv, state, joined,
    dyv, gv, upv, h2v, r2v, mixedv, rav, qkv, qpv, vuv, lowv, cv, sv, bv,
    dgv, dupv, dmidv, dmv, dqv, duv, dkv, dvv, statev, jv,
    total, datt, heldg, heldu, isem, osem, csem, psem,
):
    rows, width = dy.shape
    hidden = wd.shape[0]
    columns = heldg.shape[1]
    steps = hidden // columns
    ins = moves(
        (
            (dy, dyv), (g, gv), (up, upv), (h2, h2v), (r2, r2v), (mixed, mixedv), (ra, rav),
            (qk, qkv), (pre.at[:, pl.ds(0, width)], qpv),
            (pre.at[:, pl.ds(2 * width, 2 * width)], vuv), (low, lowv), (cosine, cv), (sine, sv),
            (behind, bv),
        ),
        isem,
    )
    for copy in ins[:3]:
        copy.start()
    for copy in ins[:3]:
        copy.wait()
    for copy in ins[3:]:
        copy.start()
    heldg[...] = jnp.zeros_like(heldg)
    heldu[...] = jnp.zeros_like(heldu)
    total[...] = jnp.zeros_like(total)

    def chunk_out(i):
        at = pl.ds(pl.multiple_of(i * columns, LANES), columns)
        return [
            pltpu.make_async_copy(source.at[:, at], target.at[:, at], csem.at[n, i])
            for n, (source, target) in enumerate(((dgv, dg), (dupv, dup)))
        ]

    def step(i, carry):
        at = pl.ds(pl.multiple_of(i * columns, LANES), columns)
        before = pl.multiple_of(jnp.maximum(i - 1, 0) * columns, LANES)
        total[...] += nt(heldg[...], wi[:, pl.ds(before, columns)]) + nt(
            heldu[...], wi[:, pl.ds(before + hidden, columns)]
        )
        product = nt(dyv[...], wd[at, :])
        left = (product * upv[:, at].astype(f32)).astype(bf16)
        right = (product * gv[:, at].astype(f32)).astype(bf16)
        dgv[:, at] = left
        dupv[:, at] = right
        heldg[...] = left
        heldu[...] = right
        for copy in chunk_out(i):
            copy.start()
        return carry

    lax.fori_loop(0, steps, step, 0)
    for copy in ins[3:]:
        copy.wait()
    dh2 = (
        total[...]
        + nt(heldg[...], wi[:, hidden - columns : hidden])
        + nt(heldu[...], wi[:, 2 * hidden - columns :])
    )
    middle = dyv[...].astype(f32) + norm_back(dh2, h2v[...].astype(f32), r2v[:, 0:1], width)
    dmidv[...] = middle
    dmv[...] = middle.astype(bf16)
    outs = moves(((dmidv, dmid), (dmv, dm)), osem)
    for copy in outs:
        copy.start()
    dgated = nt(dmv[...], wo[...])
    normed = mixedv[...].astype(f32)
    duv[...] = (dgated * normed).astype(bf16)
    back = norm_back(dgated * vuv[:, width:].astype(f32), normed, rav[:, 0:1], width)
    datt[...] = back.astype(bf16)
    ahead = row_index(rows, LANES)
    row = lax.broadcasted_iota(jnp.int32, (rows, rows), 0)
    column = lax.broadcasted_iota(jnp.int32, (rows, rows), 1)
    distance = (row - column).astype(f32)

    early = moves(((duv, du),), osem, 2)
    for copy in early:
        copy.start()

    def pair_out(i):
        at = pl.ds(pl.multiple_of(i * 2 * LANES, LANES), 2 * LANES)
        return [
            pltpu.make_async_copy(source.at[:, at], target.at[:, at], psem.at[n, i])
            for n, (source, target) in enumerate(((dqv, dq), (dkv, dk), (dvv, dv)))
        ]

    def some(i, carry):
        for m in range(2):
            n = i * 2 + m
            at = pl.multiple_of(n * LANES, LANES)
            lane = pl.ds(at, LANES)
            query, key = qkv[:, lane], qkv[:, pl.ds(at + width, LANES)]
            value, cot = vuv[:, lane], datt[:, lane]
            power = jnp.exp(jnp.abs(distance) * (-slope[n]))
            mask = jnp.where(distance >= 0.0, power, 0.0)
            flipped = jnp.where(distance <= 0.0, power, 0.0)
            weights_t = (flipped * nt(key, query)).astype(bf16)
            scores = (mask * nt(cot, value)).astype(bf16)
            scores_t = (flipped * nt(value, cot)).astype(bf16)
            scaled = (jnp.exp(ahead * (-slope[n])) * cot.astype(f32)).astype(bf16)
            own = tn(query, scaled)
            statev[n] = own.astype(bf16)
            jv[n] = join(slope[n], bv[n], own)
            dquery = nn(scores, key) + nt(scaled, lowv[n])
            turned = dquery * cv[...] + half_turn(dquery * sv[...])
            p = qpv[:, lane].astype(f32)
            s = sigmoid(p)
            dqv[:, lane] = (turned * (s * (1.0 + p * (1.0 - s)))).astype(bf16)
            dkv[:, lane] = nn(scores_t, query)
            dvv[:, lane] = nn(weights_t, cot)
        for copy in pair_out(i):
            copy.start()
        return carry

    lax.fori_loop(0, HEADS // 2, some, 0)
    last = moves(((statev, state), (jv, joined)), osem, 3)
    for copy in last:
        copy.start()
    for copy in outs + early + last:
        copy.wait()
    for i in range(HEADS // 2):
        for copy in pair_out(i):
            copy.wait()

    def drain(i, carry):
        for copy in chunk_out(i):
            copy.wait()
        return carry

    lax.fori_loop(0, steps, drain, 0)


def back_channel(slopes, dy, r, cosine, sine, behind, wo, wi, wd):
    rows, width = dy.shape
    hidden = wd.shape[0]
    columns = 256
    steps = hidden // columns
    states = (HEADS, LANES, LANES)
    act = hbm((rows, width), bf16)
    full = hbm((rows, width), f32)
    unit = hbm((rows, hidden), bf16)
    state = hbm(states, bf16)
    outs = [unit, unit, full, act, act, act, full, full, state, state]
    wide = pltpu.VMEM((rows, width), bf16)
    thin = pltpu.VMEM((rows, LANES), f32)
    twice = pltpu.VMEM((rows, 2 * width), bf16)
    tall = pltpu.VMEM((rows, hidden), bf16)
    return pl.pallas_call(
        back_channel_body,
        in_specs=[SMEM] + [FREE] + [VMEM] * 3 + [ANY] * 12,
        out_specs=[ANY] * len(outs),
        out_shape=outs,
        scratch_shapes=[
            wide, tall, tall, wide, thin, wide, thin, twice, wide, twice,
            pltpu.VMEM(states, bf16), thin, thin, pltpu.VMEM(states, bf16),
        ]
        + [pltpu.VMEM(o.shape, o.dtype) for o in outs]
        + [
            pltpu.VMEM((rows, width), f32),
            wide,
            pltpu.VMEM((rows, columns), bf16),
            pltpu.VMEM((rows, columns), bf16),
            pltpu.SemaphoreType.DMA((14,)),
            pltpu.SemaphoreType.DMA((5,)),
            pltpu.SemaphoreType.DMA((2, steps)),
            pltpu.SemaphoreType.DMA((3, HEADS // 2)),
        ],
        compiler_params=params(22),
        cost_estimate=pl.CostEstimate(
            flops=2 * rows * width * (width + 3 * hidden),
            bytes_accessed=2 * width * (width + 3 * hidden),
            transcendentals=0,
        ),
        name="back_channel",
    )(
        slopes, dy, *close_by(wo, wi, wd),
        *far_away(
            r["g"], r["up"], r["h2"], r["r2"], r["mixed"], r["ra"], r["qk"], r["pre"], r["low"],
            cosine, sine, behind,
        ),
    )


def back_mixer_body(
    slope, factors, dq, du, dk, dv, qk, pre, far, near, cosine, sine, h1, r1, dmid, w,
    dkp, dvp, dx,
    dkin, dvin, kvv, kpv, vv, statev, cv, sv, h1v, r1v, dmidv, parts, dxv, total, isem, osem,
):
    rows, width = dq.shape
    ins = moves(
        (
            (dk, dkin), (dv, dvin), (qk.at[:, pl.ds(width, width)], kvv),
            (pre.at[:, pl.ds(width, width)], kpv), (pre.at[:, pl.ds(2 * width, width)], vv),
            (far, statev.at[pl.ds(0, HEADS)]), (near, statev.at[pl.ds(HEADS, HEADS)]),
            (cosine, cv), (sine, sv),
            (dq, parts.at[:, pl.ds(0, width)]), (du, parts.at[:, pl.ds(3 * width, width)]),
            (h1, h1v), (r1, r1v), (dmid, dmidv),
        ),
        isem,
    )
    for copy in ins:
        copy.start()
    for copy in ins[:9]:
        copy.wait()
    ahead = rows - row_index(rows, LANES)

    def some(i, carry):
        for m in range(4):
            n = i * 4 + m
            at = pl.multiple_of(n * LANES, LANES)
            lane = pl.ds(at, LANES)
            state = entering_state(factors, statev, n)
            decay = jnp.exp(ahead * (-slope[n]))
            keyed = (kvv[:, lane].astype(f32) * decay).astype(bf16)
            dkey = dkin[:, lane] + decay * nt(vv[:, lane], state)
            turned = dkey * cv[...] + half_turn(dkey * sv[...])
            p = kpv[:, lane].astype(f32)
            s = sigmoid(p)
            parts[:, pl.ds(at + width, LANES)] = (turned * (s * (1.0 + p * (1.0 - s)))).astype(bf16)
            parts[:, pl.ds(at + 2 * width, LANES)] = (dvin[:, lane] + nn(keyed, state)).astype(bf16)
        return carry

    lax.fori_loop(0, HEADS // 4, some, 0)
    outs = moves(
        ((parts.at[:, pl.ds(width, width)], dkp), (parts.at[:, pl.ds(2 * width, width)], dvp)), osem
    )
    for copy in outs:
        copy.start()
    for copy in ins[9:]:
        copy.wait()
    columns = 256

    def step(j, carry):
        at = pl.ds(pl.multiple_of(j * columns, LANES), columns)
        total[:, at] = nt(parts[...], w[at, :])
        return carry

    lax.fori_loop(0, width // columns, step, 0)
    back = norm_back(total[...], h1v[...].astype(f32), r1v[:, 0:1], width)
    dxv[...] = (dmidv[...] + back).astype(bf16)
    last = moves(((dxv, dx),), osem, 2)
    for copy in last:
        copy.start()
    for copy in outs + last:
        copy.wait()


def back_mixer(slopes, factors, r, entering, cosine, sine, w):
    rows, width = r["dq"].shape
    act = hbm((rows, width), bf16)
    wide = pltpu.VMEM((rows, width), bf16)
    full = pltpu.VMEM((rows, width), f32)
    thin = pltpu.VMEM((rows, LANES), f32)
    return pl.pallas_call(
        back_mixer_body,
        in_specs=[SMEM] * 2 + [ANY] * 6 + [FREE] * 2 + [ANY] * 5 + [VMEM],
        out_specs=[ANY] * 3,
        out_shape=[act, act, act],
        scratch_shapes=[
            full, full, wide, wide, wide, pltpu.VMEM((2 * HEADS, LANES, LANES), bf16), thin, thin,
            wide, thin,
            full,
            pltpu.VMEM((rows, w.shape[1]), bf16), wide, full,
            pltpu.SemaphoreType.DMA((14,)),
            pltpu.SemaphoreType.DMA((3,)),
        ],
        compiler_params=params(14),
        cost_estimate=pl.CostEstimate(
            flops=2 * rows * width * w.shape[1],
            bytes_accessed=2 * width * w.shape[1],
            transcendentals=0,
        ),
        name="back_mixer",
    )(
        slopes, factors,
        *far_away(r["dq"], r["du"], r["dk"], r["dv"], r["qk"], r["pre"]),
        *entering,
        *far_away(cosine, sine, r["h1"], r["r1"], r["dmid"]),
        *close_by(w),
    )


def weight_body(*refs, batch, sides, groups):
    place = refs[0]
    lefts = refs[1 : 1 + 2 * batch]
    rights = refs[1 + 2 * batch : 1 + 2 * batch + 2 * batch * sides]
    outs = refs[1 + 2 * batch + 2 * batch * sides : -7]
    x, xt, ys, stage, xsem, ysem, osem = refs[-7:]
    rows = lefts[0].shape[0]
    columns = x.shape[1]
    quarter = columns // 4
    blocks = groups[0][2]

    def left_copies(section):
        return [
            pltpu.make_async_copy(
                lefts[section * batch + b], x.at[pl.ds(b * rows, rows)], xsem.at[b]
            )
            for b in range(batch)
        ]

    def right_copies(section, s):
        return [
            pltpu.make_async_copy(
                rights[(section * sides + s) * batch + b],
                ys.at[s, pl.ds(b * rows, rows)],
                ysem.at[s, b],
            )
            for b in range(batch)
        ]

    for section in range(2):

        @pl.when(place[4] == section)
        def _():
            for copy in left_copies(section):
                copy.start()
            for s in range(sides):
                for copy in right_copies(section, s):
                    copy.start()

    for copy in left_copies(0):
        copy.wait()
    def turn(piece, carry):
        at = pl.ds(pl.multiple_of(piece * 2 * LANES, LANES), 2 * LANES)
        xt[at, :] = x[:, at].T
        return carry

    lax.fori_loop(0, columns // (2 * LANES), turn, 0)

    def move(number, role, out):
        slot = number * 4 + role
        return pltpu.make_async_copy(
            stage.at[slot], out.at[pl.ds((role % 2) * blocks, blocks)], osem.at[slot]
        )

    def one(role, number, side, start):
        left = xt[pl.ds(pl.multiple_of(place[role] * quarter, 16), quarter), :]
        tile = nn(left, ys[side, :, start * LANES : (start + blocks) * LANES]).astype(bf16)
        for n in range(blocks):
            stage[number * 4 + role, n] = tile[:, head(n)]

    for number, (side, start, _) in enumerate(groups):
        if all(side != done for done, _, _ in groups[:number]):
            for copy in right_copies(0, side):
                copy.wait()

        def step(role, carry, number=number, side=side, start=start):
            one(role, number, side, start)

            @pl.when(role < 2)
            def _():
                move(number, role, outs[2 * number]).start()

            @pl.when(role >= 2)
            def _():
                move(number, role, outs[2 * number + 1]).start()

            return carry

        lax.fori_loop(0, 4, step, 0)
    for number in range(len(groups)):
        for role in range(4):
            move(number, role, outs[2 * number + role // 2]).wait()


def weight_gradient(place, lefts, rights, groups):
    batch = len(lefts[0])
    sides = len(rights[0])
    rows, columns = lefts[0][0].shape
    span = rights[0][0][0].shape[1]
    quarter = columns // 4
    blocks = groups[0][2]
    flat_left = [a for section in lefts for a in section]
    flat_right = [a for section in rights for side in section for a in side]
    out = pl.pallas_call(
        functools.partial(weight_body, batch=batch, sides=sides, groups=groups),
        in_specs=[SMEM] + [ANY] * (len(flat_left) + len(flat_right)),
        out_specs=[ANY] * (2 * len(groups)),
        out_shape=[hbm((2 * blocks, quarter, LANES), bf16)] * (2 * len(groups)),
        scratch_shapes=[
            pltpu.VMEM((batch * rows, columns), bf16),
            pltpu.VMEM((columns, batch * rows), bf16),
            pltpu.VMEM((sides, batch * rows, span), bf16),
            pltpu.VMEM((4 * len(groups), blocks, quarter, LANES), bf16),
            pltpu.SemaphoreType.DMA((batch,)),
            pltpu.SemaphoreType.DMA((sides, batch)),
            pltpu.SemaphoreType.DMA((4 * len(groups),)),
        ],
        compiler_params=params(24),
        cost_estimate=pl.CostEstimate(
            flops=2 * batch * rows * columns * sides * span,
            bytes_accessed=2 * columns * sides * span,
            transcendentals=0,
        ),
        name="weight_gradient",
    )(place, *far_away(*flat_left, *flat_right))
    return [(out[2 * n], out[2 * n + 1]) for n in range(len(groups))]


def settle_body(edge, outer, inner, *rest):
    out = rest[-1]

    def write(source):
        def one(n, carry):
            out[:, pl.ds(pl.multiple_of(n * LANES, LANES), LANES)] = source[n].astype(f32)
            return carry

        lax.fori_loop(0, source.shape[0], one, 0)

    @pl.when(edge[0] == 1)
    def _():
        write(outer)

    @pl.when(edge[0] == 0)
    def _():
        write(inner)


def settle(edge, outer, inner, total, held, number):
    blocks, quarter, _ = outer.shape
    more = [] if held is None else [held]
    return pl.pallas_call(
        settle_body,
        grid=(1,),
        in_specs=[SMEM, whole(outer.shape), whole(inner.shape)] + [ANY] * len(more),
        out_specs=pl.BlockSpec((quarter, blocks * LANES), lambda j: (0, number)),
        out_shape=hbm((quarter, total), f32),
        input_output_aliases={3: 0} if more else {},
        compiler_params=params(8),
        name="settle",
    )(edge, outer, inner, *more)


def add(a, b):
    return (a.astype(f32) + b.astype(f32)).astype(bf16)


def gathered_state(own, slopes, forward):
    count = lax.axis_size("seq")
    place = lax.axis_index("seq")
    gathered = lax.all_gather(own, "seq").astype(f32)
    device = jnp.arange(count)
    distance = place - 1 - device if forward else device - place - 1
    power = jnp.maximum(distance, 0).astype(f32) * BLK
    weight = jnp.where(distance[:, None] >= 0, jnp.exp(-slopes[None] * power[:, None]), 0.0)
    return jnp.sum(weight[:, :, None, None] * gathered, axis=0).astype(bf16)


def halves(first, second):
    place = lax.axis_index("seq")
    sent = jnp.where(place % 2 == 1, first, second)
    one = lax.ppermute(sent, "seq", [(1, 0), (2, 3), (0, 2), (3, 1)])
    two = lax.ppermute(jnp.where(place == 1, second, first), "seq", [(2, 1), (1, 2)])
    return (
        jnp.where(place == 0, first, jnp.where(place == 1, two, one)),
        jnp.where(place == 3, second, jnp.where(place == 2, two, one)),
    )


def quarters(low, high):
    place = lax.axis_index("seq")
    one = lax.ppermute(jnp.where(place < 2, high, low), "seq", [(0, 1), (3, 2), (2, 0), (1, 3)])
    two = lax.ppermute(jnp.where(place == 1, low, high), "seq", [(1, 2), (2, 1)])
    return (
        jnp.where(place == 0, low, jnp.where(place == 2, two, one)),
        jnp.where(place == 3, high, jnp.where(place == 1, two, one)),
    )


class Sums:
    def __init__(self, edge, settled):
        self.edge = edge
        self.settled = settled
        self.waiting, self.parts, self.partial, self.across = [], [], [], []
        self.previous = None
        self.step = 0
        self.marks = []
        self.written = None

    def load(self, chunks):
        for given, kept in chunks:
            blocks = given.shape[0] // 2
            taken = lax.ppermute(given, "seq", [(0, 1), (1, 0), (2, 3), (3, 2)])
            self.waiting.append(
                (add(kept[:blocks], taken[:blocks]), add(kept[blocks:], taken[blocks:]))
            )

    def over_y(self):
        if not self.waiting:
            return
        far, own = self.waiting.pop(0)
        if self.previous is not None:
            far, _ = lax.optimization_barrier((far, self.previous))
        self.marks.append(far)
        self.previous = lax.ppermute(far, "seq", [(0, 2), (2, 0), (1, 3), (3, 1)])
        self.parts.append(add(own, self.previous))

    def over_z(self, last=False):
        step, count = self.step, len(self.parts)
        if step >= count + 2 or (step >= count and not last):
            return False
        part = self.parts[step] if step < count else None
        done = None
        if step >= 2:
            done = self.partial[step - 2].astype(f32) + self.across[step - 2].astype(f32)
        if part is not None and self.written is not None:
            part, _ = lax.optimization_barrier((part, self.written))
            self.written = None
        if 1 <= step <= count:
            self.marks.append(self.partial[step - 1])
            self.across.append(lax.ppermute(self.partial[step - 1], "dp", [(1, 2), (2, 1)]))
        if part is not None and done is not None and part.shape == done.shape:
            sent = jnp.where(self.edge, part.astype(f32), done).astype(bf16)
            self.marks.append(sent)
            got = lax.ppermute(sent, "dp", [(0, 1), (1, 0), (2, 3), (3, 2)])
            self.partial.append(add(part, got))
            self.written = self.settled(got, sent)
        else:
            if part is not None:
                self.marks.append(part)
                self.partial.append(add(part, lax.ppermute(part, "dp", [(0, 1), (3, 2)])))
            if done is not None:
                done = done.astype(bf16)
                self.marks.append(done)
                self.written = self.settled(lax.ppermute(done, "dp", [(1, 0), (2, 3)]), done)
        self.step += 1
        return True

    def started(self):
        marks, self.marks = self.marks, []
        return marks


def angle_tables(position_row, half_size):
    frequency = jnp.exp(
        jnp.arange(half_size, dtype=jnp.float32) * (-math.log(theta_base) / half_size)
    )
    angles = position_row.astype(jnp.float32)[..., None] * frequency
    cosine = jnp.cos(angles)
    sine_rows = jnp.sin(angles)
    return (
        jnp.concatenate([cosine, cosine], axis=-1),
        jnp.concatenate([-sine_rows, sine_rows], axis=-1),
    )


class Order:
    def __init__(self):
        self.last = []

    def after(self, value):
        if self.last:
            value = lax.optimization_barrier((value, *self.last))[0]
        return value

    def at(self, *values):
        self.last = list(values)


class Layer:
    def __init__(self, order, slopes, factors, chained, cosine, sine, weights):
        self.order, self.slopes, self.factors, self.chained = order, slopes, factors, chained
        self.cosine, self.sine = cosine, sine
        self.w, self.wo, self.wi, self.wd = weights
        self.blocks = [None, None]
        self.entering = [None, None]
        self.later = [None, None]
        self.zero = jnp.zeros((HEADS, LANES, LANES), bf16)

    def first(self, b, x):
        before = self.blocks[0]["state"] if b == 1 else self.zero
        h1, r1, pre, qk, state, joined = project(
            self.order.after(self.slopes), x, self.cosine[b], self.sine[b], before, self.w
        )
        self.order.at(r1)
        self.blocks[b] = dict(x=x, h1=h1, r1=r1, pre=pre, qk=qk, state=state)
        if not self.chained:
            self.entering[b] = gathered_state(state, self.slopes, True)
        elif b == 1:
            near = lax.ppermute(joined, "seq", [(0, 1), (2, 3)])
            self.entering = [near, near]

    def second(self, b):
        r = self.blocks[b]
        near = self.blocks[0]["state"] if b == 1 else self.entering[b]
        mixed, gated, ra, h2, r2, low, g, up, product, y = finish(
            self.order.after(self.slopes), self.factors[b], r["x"], r["qk"], r["pre"],
            (self.entering[b], near), self.wo, self.wi, self.wd,
        )
        self.order.at(ra)
        r.update(
            mixed=mixed, gated=gated, ra=ra, h2=h2, r2=r2, low=low, g=g, up=up, product=product
        )
        return y

    def back_first(self, b, dy):
        r = self.blocks[b]
        behind = self.blocks[1]["dstate"] if b == 0 else self.zero
        dg, dup, dmid, dm, dq, du, dk, dv, state, joined = back_channel(
            self.order.after(self.slopes), dy, r, self.cosine[b], self.sine[b], behind,
            self.wo, self.wi, self.wd,
        )
        self.order.at(dm)
        r.update(dy=dy, dg=dg, dup=dup, dmid=dmid, dm=dm, dq=dq, du=du, dk=dk, dv=dv, dstate=state)
        if not self.chained:
            self.later[b] = gathered_state(state, self.slopes, False)
        elif b == 0:
            near = lax.ppermute(joined, "seq", [(1, 0), (3, 2)])
            self.later = [near, near]

    def back_second(self, b):
        r = self.blocks[b]
        near = self.blocks[1]["dstate"] if b == 0 else self.later[b]
        dkp, dvp, dx = back_mixer(
            self.order.after(self.slopes), self.factors[1 - b], r, (self.later[b], near),
            self.cosine[b], self.sine[b], self.w,
        )
        self.order.at(dkp)
        r.update(dkp=dkp, dvp=dvp)
        return dx


def per_device(boundary, positions, decay_exp, mixer_in, mixer_out, channel_in, channel_out):
    section = lax.axis_index("section")
    is_first = section == 0
    batch, rows, width = boundary.shape[1:]
    assert rows == BLK and batch == 2
    slopes = jnp.exp2(-0.5 * decay_exp[0].astype(jnp.float32))
    w, wo, wi, wd = weights = mixer_in[0], mixer_out[0], channel_in[0], channel_out[0]
    hidden = wd.shape[0]
    half_size = width // HEADS // 2
    usual = lax.axis_size("seq") == 4 and lax.axis_size("dp") == 4
    place, line = lax.axis_index("seq"), lax.axis_index("dp")
    core, y_place = place % 2, place // 2

    own = (boundary[0, 0], boundary[0, 1])
    if usual:
        own = halves(*own)
        every = lax.all_gather(positions, "seq")
        chosen = lax.dynamic_index_in_dim(every, y_place, 1, keepdims=False)
        positions = lax.dynamic_slice_in_dim(chosen, 2 * core, 2, 0)
    cosine, sine = angle_tables(positions, half_size)

    roles = [
        2 * (1 - y_place) + 1 - core,
        2 * y_place + 1 - core,
        2 * (1 - y_place) + core,
        2 * y_place + core,
    ]
    if not usual:
        roles = [0, 1, 2, 3]
    roles = jnp.stack([jnp.asarray(r, jnp.int32) for r in (*roles, section)])
    edge = (line == 0) | (line == lax.axis_size("dp") - 1)
    flag = edge.astype(jnp.int32)[None]
    one = jnp.ones_like(slopes)
    factors = [jnp.stack([one, 0.0 * one])] * 2
    if usual:
        factors[1] = jnp.stack([jnp.exp(-slopes * BLK), one])
    roles, flag, slopes, *factors = lax.optimization_barrier((roles, flag, slopes, *factors))
    edge = flag[0] == 1
    order = Order()
    order.at(roles, flag)
    layers = [
        Layer(order, slopes, factors, usual, cosine, sine, weights) for section_of_it in range(2)
    ]
    early, late = layers

    for b in range(2):
        early.first(b, own[b])
    arrived = [lax.ppermute(early.second(b), "section", [(0, 1)]) for b in range(2)]
    for b in range(2):
        late.first(b, arrived[b])
    outputs = [late.second(b) for b in range(2)]
    for b in (1, 0):
        late.back_first(b, own[b])
    returned = [None, None]
    for b in (1, 0):
        returned[b] = lax.ppermute(late.back_second(b), "section", [(1, 0)])

    def operands(*names):
        return [[[r[name] for r in layer.blocks] for name in names] for layer in layers]

    chunks = []
    spans = [(3, width), (3, width)] + [(2, 2 * hidden)] * 4 + [(1, width)] + [(0, 4 * width)] * 4
    numbers = [0, 1, 0, 1, 2, 3, 0, 0, 1, 2, 3]
    held = [None] * 4
    finished = []

    def settled(outer, inner):
        number = len(finished)
        index, total = spans[number]
        blocks, quarter = chunks[number][0].shape[0] // 2, chunks[number][0].shape[1]
        shape = (blocks, quarter, LANES)
        finished.append(number)
        held[index] = settle(
            flag, outer.reshape(shape), inner.reshape(shape), total, held[index], numbers[number]
        )
        return held[index]

    sums = Sums(edge, settled)

    def even(array):
        return array.reshape(array.shape[0] * array.shape[1] // 256, 256, LANES)

    def gradient(name, names, groups):
        left = [side[0] for side in operands(name)]
        found = weight_gradient(order.after(roles), left, operands(*names), groups)
        order.at(found[-1][1])
        chunks.extend(found)
        if usual:
            sums.load([(even(given), even(kept)) for given, kept in found])

    def move(*what):
        if not usual:
            return
        for way in what:
            way()
        order.at(*order.last, *sums.started())

    half, eight = hidden // LANES // 2, width // LANES
    early.back_first(1, returned[1])
    early.blocks[0]["dy"] = returned[0]
    gradient("product", ("dy",), [(0, 0, 4), (0, 4, 4)])
    move(sums.over_y)
    early.back_first(0, returned[0])
    pass
    gradient("h2", ("dg", "dup"), [(0, 0, half), (0, half, half), (1, 0, half), (1, half, half)])
    pass
    dx = [None, None]
    for b in (1, 0):
        dx[b] = early.back_second(b)
    move(sums.over_y, sums.over_z)
    gradient("gated", ("dm",), [(0, 0, eight)])
    gradient("h1", ("dq", "dkp", "dvp", "du"), [(s, 0, eight) for s in range(4)])

    ends = [jnp.where(is_first, dx[b], outputs[b]) for b in range(2)]
    joined = jnp.stack(quarters(*ends) if usual else ends)[None]
    if usual:
        while sums.waiting:
            move(sums.over_y, sums.over_z)
        while sums.over_z(last=True):
            pass
        return (joined, *(h[None] for h in held))
    found = [[], [], [], []]
    for (index, total), chunk in zip(spans, chunks):
        chunk = jnp.concatenate(chunk)
        blocks, quarter = chunk.shape[0] // 4, chunk.shape[1]
        rows_first = chunk.reshape(4, blocks, quarter, LANES).transpose(0, 2, 1, 3)
        found[index].append(rows_first.reshape(4 * quarter, blocks * LANES))
    summed = []
    for pieces in found:
        part = lax.psum_scatter(
            jnp.concatenate(pieces, axis=1), "seq", scatter_dimension=0, tiled=True
        )
        summed.append(lax.psum(part, "dp").astype(f32)[None])
    return (joined, *summed)


def solution(mesh):
    in_specs = (
        P("section", "dp", "seq", None),
        P("dp", "seq"),
        P("section", None),
        P("section", None, None),
        P("section", None, None),
        P("section", None, None),
        P("section", None, None),
    )
    out_specs = (
        P("section", "dp", "seq", None),
        P("section", "seq", None),
        P("section", "seq", None),
        P("section", "seq", None),
        P("section", "seq", None),
    )
    return jax.shard_map(
        per_device, mesh=mesh, in_specs=in_specs, out_specs=out_specs, check_vma=False
    )
```

```python
import functools
import math

import jax
import jax.numpy as jnp
from jax import lax
from jax.experimental import pallas as pl
from jax.experimental.pallas import tpu as pltpu
from jax.sharding import PartitionSpec as P

HEADS = 8
BLK = 256
LANES = 128
STEPS = 8

epsilon = 1e-06
theta_base = 10000.0
f32 = jnp.float32
bf16 = jnp.bfloat16


def nn(a, b):
    return jnp.dot(a, b, preferred_element_type=f32)


def nt(a, b):
    return lax.dot_general(a, b, (((1,), (1,)), ((), ())), preferred_element_type=f32)


def tn(a, b):
    return lax.dot_general(a, b, (((0,), (0,)), ((), ())), preferred_element_type=f32)


def sigmoid(v):
    return 1.0 / (1.0 + jnp.exp(-v))


def norm_factor(v, width):
    return lax.rsqrt(jnp.sum(v * v, axis=-1, keepdims=True) * (1.0 / width) + epsilon)


def norm_back(cotangent, normed, factor, width):
    mean = jnp.sum(cotangent * normed, axis=-1, keepdims=True) * (1.0 / width)
    return factor * (cotangent - normed * mean)


def row_index(rows, columns):
    return lax.broadcasted_iota(jnp.int32, (rows, columns), 0).astype(f32)


def decay_mask(slope, rows):
    row = lax.broadcasted_iota(jnp.int32, (rows, rows), 0)
    column = lax.broadcasted_iota(jnp.int32, (rows, rows), 1)
    distance = jnp.maximum(row - column, 0).astype(f32)
    return jnp.where(row >= column, jnp.exp(distance * (-slope)), 0.0)


def head(number):
    return slice(number * LANES, (number + 1) * LANES)


def half_turn(v):
    return pltpu.roll(v, LANES // 2, 1)


def whole(shape):
    return pl.BlockSpec(shape, lambda j: (0,) * len(shape))


def hbm(shape, kind):
    return pltpu.HBM(tuple(shape), kind)


def far_away(*arrays):
    return [pltpu.with_memory_space_constraint(a, pltpu.HBM) for a in arrays]


def close_by(*arrays):
    return [pltpu.with_memory_space_constraint(a, pltpu.VMEM) for a in arrays]


def params(megabytes):
    return pltpu.CompilerParams(vmem_limit_bytes=megabytes * 1024 * 1024)


SMEM = pl.BlockSpec(memory_space=pltpu.SMEM)
ANY = pl.BlockSpec(memory_space=pltpu.HBM)
VMEM = pl.BlockSpec(memory_space=pltpu.VMEM)
FREE = pl.BlockSpec(memory_space=pl.ANY)


def tables(position, rows):
    lane = lax.broadcasted_iota(jnp.int32, (rows, LANES), 1)
    half = LANES // 2
    feature = jnp.where(lane < half, lane, lane - half).astype(f32)
    frequency = jnp.exp(feature * (-math.log(theta_base) / half))
    angle = position * frequency
    return jnp.cos(angle), jnp.where(lane < half, -jnp.sin(angle), jnp.sin(angle))


def join(slope, before, own):
    decay = jnp.exp(jnp.full((LANES, LANES), -BLK, f32) * slope)
    return (decay * before.astype(f32) + own).astype(bf16)


def project_body(slope, x, cosine, sine, before, w, h1, r1, pre, qk, state, joined,
                 xv, cv, sv, bv, hv, rv, prev, qkv, stv, jv, isem, osem, qsem, *own):
    rows, width = x.shape
    steps = STEPS
    columns = w.shape[1] // steps
    heads = columns // LANES
    first = [
        pltpu.make_async_copy(source, target, isem.at[n])
        for n, (source, target) in enumerate(((x, xv), (cosine, cv), (sine, sv), (before, bv)))
    ]
    for copy in first:
        copy.start()

    def weight(j):
        at = pl.ds(pl.multiple_of(j * columns, LANES), columns)
        return pltpu.make_async_copy(w.at[:, at], own[0].at[j], own[1].at[j])

    if own:
        for j in range(steps):
            weight(j).start()
    first[0].wait()
    v = xv[...].astype(f32)
    factor = norm_factor(v, width)
    hv[...] = (v * factor).astype(bf16)
    rv[...] = jnp.broadcast_to(factor, rv.shape)
    for copy in first[1:]:
        copy.wait()
    outs = [pltpu.make_async_copy(hv, h1, osem.at[0]), pltpu.make_async_copy(rv, r1, osem.at[1])]
    for copy in outs:
        copy.start()

    def pre_out(j):
        at = pl.ds(pl.multiple_of(j * columns, LANES), columns)
        return pltpu.make_async_copy(prev.at[:, at], pre.at[:, at], osem.at[3 + j])

    def qk_out(j):
        at = pl.ds(pl.multiple_of(j * columns, LANES), columns)
        return pltpu.make_async_copy(qkv.at[:, at], qk.at[:, at], qsem.at[j])

    def step(j, carry):
        at = pl.multiple_of(j * columns, LANES)
        if own:
            weight(j).wait()
            p = nn(hv[...], own[0][j])
        else:
            p = nn(hv[...], w[:, pl.ds(at, columns)])
        prev[:, pl.ds(at, columns)] = p.astype(bf16)
        pre_out(j).start()

        @pl.when(j < steps // 2)
        def _():
            for n in range(heads):
                v = p[:, head(n)]
                v = v * sigmoid(v)
                turned = v * cv[...] + half_turn(v) * sv[...]
                qkv[:, pl.ds(at + n * LANES, LANES)] = turned.astype(bf16)
            qk_out(j).start()

        @pl.when((j >= steps // 2) & (j < 3 * steps // 4))
        def _():
            values = p.astype(bf16)
            ahead = rows - row_index(rows, LANES)
            for n in range(heads):
                number = (j - steps // 2) * heads + n
                decay = jnp.exp(ahead * (-slope[number]))
                key = qkv[:, pl.ds(at - width + n * LANES, LANES)]
                keyed = (key.astype(f32) * decay).astype(bf16)
                own = tn(keyed, values[:, head(n)])
                stv[number] = own.astype(bf16)
                jv[number] = join(slope[number], bv[number], own)

        return carry

    lax.fori_loop(0, steps, step, 0)
    last = [
        pltpu.make_async_copy(stv, state, osem.at[11]),
        pltpu.make_async_copy(jv, joined, osem.at[12]),
    ]
    for copy in last:
        copy.start()
    for copy in outs + last:
        copy.wait()
    for j in range(steps):
        pre_out(j).wait()
    for j in range(steps // 2):
        qk_out(j).wait()


def project(slopes, x, cosine, sine, before, w, streamed):
    rows, width = x.shape
    total = w.shape[1]
    states = (HEADS, LANES, LANES)
    return pl.pallas_call(
        project_body,
        in_specs=[SMEM, FREE] + [ANY] * 3 + [ANY if streamed else VMEM],
        out_specs=[ANY] * 6,
        out_shape=[
            hbm((rows, width), bf16),
            hbm((rows, LANES), f32),
            hbm((rows, total), bf16),
            hbm((rows, total // 2), bf16),
            hbm(states, bf16),
            hbm(states, bf16),
        ],
        scratch_shapes=[
            pltpu.VMEM((rows, width), bf16),
            pltpu.VMEM((rows, LANES), f32),
            pltpu.VMEM((rows, LANES), f32),
            pltpu.VMEM(states, bf16),
            pltpu.VMEM((rows, width), bf16),
            pltpu.VMEM((rows, LANES), f32),
            pltpu.VMEM((rows, total), bf16),
            pltpu.VMEM((rows, total // 2), bf16),
            pltpu.VMEM(states, bf16),
            pltpu.VMEM(states, bf16),
            pltpu.SemaphoreType.DMA((4,)),
            pltpu.SemaphoreType.DMA((13,)),
            pltpu.SemaphoreType.DMA((STEPS // 2,)),
        ]
        + [
            pltpu.VMEM((STEPS, width, total // STEPS), bf16),
            pltpu.SemaphoreType.DMA((STEPS,)),
        ]
        * streamed,
        compiler_params=params(18 if streamed else 8),
        cost_estimate=pl.CostEstimate(
            flops=2 * rows * width * total, bytes_accessed=2 * width * total, transcendentals=0
        ),
        name="project",
    )(slopes, x, *far_away(cosine, sine, before), *(far_away(w) if streamed else close_by(w)))


def moves(pairs, sem, start=0):
    return [
        pltpu.make_async_copy(source, target, sem.at[start + n])
        for n, (source, target) in enumerate(pairs)
    ]


def entering_state(factors, states, number):
    state = factors[0, number] * states[number].astype(f32)
    state += factors[1, number] * states[HEADS + number].astype(f32)
    return state.astype(bf16)


def finish_body(
    slope, factors, x, qk, pre, far, near, wo, wi, wd,
    mixed, gated, ra, h2, r2, low, g, up, product, y,
    xv, qkv, vuv, statev, mixedv, gatedv, rav, h2v, r2v, lowv, gv, upv, productv, yv,
    attended, total, held, isem, osem, csem,
):
    rows, width = x.shape
    hidden = wd.shape[0]
    columns = held.shape[1]
    steps = hidden // columns
    ins = moves(
        (
            (qk, qkv), (pre.at[:, pl.ds(2 * width, 2 * width)], vuv),
            (far, statev.at[pl.ds(0, HEADS)]), (near, statev.at[pl.ds(HEADS, HEADS)]), (x, xv),
        ),
        isem,
    )
    for copy in ins:
        copy.start()
    for copy in ins[:4]:
        copy.wait()
    ahead = row_index(rows, LANES)

    def pair(i, carry):
        for m in range(2):
            n = i * 2 + m
            at = pl.multiple_of(n * LANES, LANES)
            lane = pl.ds(at, LANES)
            state = entering_state(factors, statev, n)
            lowv[n] = state
            query = qkv[:, lane]
            key = qkv[:, pl.ds(at + width, LANES)]
            weights = (decay_mask(slope[n], rows) * nt(query, key)).astype(bf16)
            inner = nn(weights, vuv[:, lane])
            carried = nn(query, state)
            attended[:, lane] = inner + jnp.exp(ahead * (-slope[n])) * carried
        return carry

    lax.fori_loop(0, HEADS // 2, pair, 0)
    rows_out = attended[...]
    factor = norm_factor(rows_out, width)
    rav[...] = jnp.broadcast_to(factor, rav.shape)
    normed = rows_out * factor
    mixedv[...] = normed.astype(bf16)
    gatedv[...] = (normed * vuv[:, width:].astype(f32)).astype(bf16)
    outs = moves(((mixedv, mixed), (gatedv, gated), (rav, ra), (lowv, low)), osem)
    for copy in outs:
        copy.start()
    ins[4].wait()
    middle = xv[...].astype(f32) + nn(gatedv[...], wo[...])
    total[...] = middle
    factor = norm_factor(middle, width)
    r2v[...] = jnp.broadcast_to(factor, r2v.shape)
    h2v[...] = (middle * factor).astype(bf16)
    more = moves(((h2v, h2), (r2v, r2)), osem, 4)
    for copy in more:
        copy.start()
    held[...] = jnp.zeros_like(held)

    def chunk_out(i):
        at = pl.ds(pl.multiple_of(i * columns, LANES), columns)
        return [
            pltpu.make_async_copy(source.at[:, at], target.at[:, at], csem.at[n, i])
            for n, (source, target) in enumerate(((gv, g), (upv, up), (productv, product)))
        ]

    def step(i, carry):
        start = pl.multiple_of(i * columns, LANES)
        before = pl.multiple_of(jnp.maximum(i - 1, 0) * columns, LANES)
        at = pl.ds(start, columns)
        total[...] += nn(held[...], wd[pl.ds(before, columns), :])
        gate = nn(h2v[...], wi[:, at])
        rise = nn(h2v[...], wi[:, pl.ds(start + hidden, columns)])
        both = (gate * rise).astype(bf16)
        gv[:, at] = gate.astype(bf16)
        upv[:, at] = rise.astype(bf16)
        productv[:, at] = both
        held[...] = both
        for copy in chunk_out(i):
            copy.start()
        return carry

    lax.fori_loop(0, steps, step, 0)
    yv[...] = (total[...] + nn(held[...], wd[hidden - columns :, :])).astype(bf16)
    last = moves(((yv, y),), osem, 6)
    for copy in last:
        copy.start()
    for copy in outs + more + last:
        copy.wait()

    def drain(i, carry):
        for copy in chunk_out(i):
            copy.wait()
        return carry

    lax.fori_loop(0, steps, drain, 0)


def finish(slopes, factors, x, qk, pre, entering, wo, wi, wd):
    rows, width = x.shape
    hidden = wd.shape[0]
    columns = 256
    steps = hidden // columns
    states = (HEADS, LANES, LANES)
    act = hbm((rows, width), bf16)
    factor = hbm((rows, LANES), f32)
    unit = hbm((rows, hidden), bf16)
    outs = [
        act, act, factor, act, factor, hbm(states, bf16), unit, unit, unit, act,
    ]
    return pl.pallas_call(
        finish_body,
        in_specs=[SMEM] * 2 + [FREE] + [ANY] * 2 + [FREE] * 2 + [VMEM] * 3,
        out_specs=[ANY] * len(outs),
        out_shape=outs,
        scratch_shapes=[
            pltpu.VMEM((rows, width), bf16),
            pltpu.VMEM((rows, 2 * width), bf16),
            pltpu.VMEM((rows, 2 * width), bf16),
            pltpu.VMEM((2 * HEADS, LANES, LANES), bf16),
        ]
        + [pltpu.VMEM(o.shape, o.dtype) for o in outs]
        + [
            pltpu.VMEM((rows, width), f32),
            pltpu.VMEM((rows, width), f32),
            pltpu.VMEM((rows, columns), bf16),
            pltpu.SemaphoreType.DMA((5,)),
            pltpu.SemaphoreType.DMA((7,)),
            pltpu.SemaphoreType.DMA((3, steps)),
        ],
        compiler_params=params(18),
        cost_estimate=pl.CostEstimate(
            flops=2 * rows * width * (width + 3 * hidden),
            bytes_accessed=2 * width * (width + 3 * hidden),
            transcendentals=0,
        ),
        name="finish",
    )(slopes, factors, x, *far_away(qk, pre), *entering, *close_by(wo, wi, wd))


def back_channel_body(
    slope, dy, wo, wi, wd, g, up, h2, r2, mixed, ra, qk, pre, low, cosine, sine, behind,
    dg, dup, dmid, dm, dq, du, dk, dv, state, joined,
    dyv, gv, upv, h2v, r2v, mixedv, rav, qkv, qpv, vuv, lowv, cv, sv, bv,
    dgv, dupv, dmidv, dmv, dqv, duv, dkv, dvv, statev, jv,
    total, datt, heldg, heldu, isem, osem, csem, psem,
):
    rows, width = dy.shape
    hidden = wd.shape[0]
    columns = heldg.shape[1]
    steps = hidden // columns
    ins = moves(
        (
            (dy, dyv), (g, gv), (up, upv), (h2, h2v), (r2, r2v), (mixed, mixedv), (ra, rav),
            (qk, qkv), (pre.at[:, pl.ds(0, width)], qpv),
            (pre.at[:, pl.ds(2 * width, 2 * width)], vuv), (low, lowv), (cosine, cv), (sine, sv),
            (behind, bv),
        ),
        isem,
    )
    for copy in ins[:3]:
        copy.start()
    for copy in ins[:3]:
        copy.wait()
    for copy in ins[3:]:
        copy.start()
    heldg[...] = jnp.zeros_like(heldg)
    heldu[...] = jnp.zeros_like(heldu)
    total[...] = jnp.zeros_like(total)

    def chunk_out(i):
        at = pl.ds(pl.multiple_of(i * columns, LANES), columns)
        return [
            pltpu.make_async_copy(source.at[:, at], target.at[:, at], csem.at[n, i])
            for n, (source, target) in enumerate(((dgv, dg), (dupv, dup)))
        ]

    def step(i, carry):
        at = pl.ds(pl.multiple_of(i * columns, LANES), columns)
        before = pl.multiple_of(jnp.maximum(i - 1, 0) * columns, LANES)
        total[...] += nt(heldg[...], wi[:, pl.ds(before, columns)]) + nt(
            heldu[...], wi[:, pl.ds(before + hidden, columns)]
        )
        product = nt(dyv[...], wd[at, :])
        left = (product * upv[:, at].astype(f32)).astype(bf16)
        right = (product * gv[:, at].astype(f32)).astype(bf16)
        dgv[:, at] = left
        dupv[:, at] = right
        heldg[...] = left
        heldu[...] = right
        for copy in chunk_out(i):
            copy.start()
        return carry

    lax.fori_loop(0, steps, step, 0)
    for copy in ins[3:]:
        copy.wait()
    dh2 = (
        total[...]
        + nt(heldg[...], wi[:, hidden - columns : hidden])
        + nt(heldu[...], wi[:, 2 * hidden - columns :])
    )
    middle = dyv[...].astype(f32) + norm_back(dh2, h2v[...].astype(f32), r2v[:, 0:1], width)
    dmidv[...] = middle
    dmv[...] = middle.astype(bf16)
    outs = moves(((dmidv, dmid), (dmv, dm)), osem)
    for copy in outs:
        copy.start()
    dgated = nt(dmv[...], wo[...])
    normed = mixedv[...].astype(f32)
    duv[...] = (dgated * normed).astype(bf16)
    back = norm_back(dgated * vuv[:, width:].astype(f32), normed, rav[:, 0:1], width)
    datt[...] = back.astype(bf16)
    ahead = row_index(rows, LANES)
    row = lax.broadcasted_iota(jnp.int32, (rows, rows), 0)
    column = lax.broadcasted_iota(jnp.int32, (rows, rows), 1)
    distance = (row - column).astype(f32)

    early = moves(((duv, du),), osem, 2)
    for copy in early:
        copy.start()

    def pair_out(i):
        at = pl.ds(pl.multiple_of(i * 2 * LANES, LANES), 2 * LANES)
        return [
            pltpu.make_async_copy(source.at[:, at], target.at[:, at], psem.at[n, i])
            for n, (source, target) in enumerate(((dqv, dq), (dkv, dk), (dvv, dv)))
        ]

    def some(i, carry):
        for m in range(2):
            n = i * 2 + m
            at = pl.multiple_of(n * LANES, LANES)
            lane = pl.ds(at, LANES)
            query, key = qkv[:, lane], qkv[:, pl.ds(at + width, LANES)]
            value, cot = vuv[:, lane], datt[:, lane]
            power = jnp.exp(jnp.abs(distance) * (-slope[n]))
            mask = jnp.where(distance >= 0.0, power, 0.0)
            flipped = jnp.where(distance <= 0.0, power, 0.0)
            weights_t = (flipped * nt(key, query)).astype(bf16)
            scores = (mask * nt(cot, value)).astype(bf16)
            scores_t = (flipped * nt(value, cot)).astype(bf16)
            scaled = (jnp.exp(ahead * (-slope[n])) * cot.astype(f32)).astype(bf16)
            own = tn(query, scaled)
            statev[n] = own.astype(bf16)
            jv[n] = join(slope[n], bv[n], own)
            dquery = nn(scores, key) + nt(scaled, lowv[n])
            turned = dquery * cv[...] + half_turn(dquery * sv[...])
            p = qpv[:, lane].astype(f32)
            s = sigmoid(p)
            dqv[:, lane] = (turned * (s * (1.0 + p * (1.0 - s)))).astype(bf16)
            dkv[:, lane] = nn(scores_t, query)
            dvv[:, lane] = nn(weights_t, cot)
        for copy in pair_out(i):
            copy.start()
        return carry

    lax.fori_loop(0, HEADS // 2, some, 0)
    last = moves(((statev, state), (jv, joined)), osem, 3)
    for copy in last:
        copy.start()
    for copy in outs + early + last:
        copy.wait()
    for i in range(HEADS // 2):
        for copy in pair_out(i):
            copy.wait()

    def drain(i, carry):
        for copy in chunk_out(i):
            copy.wait()
        return carry

    lax.fori_loop(0, steps, drain, 0)


def back_channel(slopes, dy, r, cosine, sine, behind, wo, wi, wd):
    rows, width = dy.shape
    hidden = wd.shape[0]
    columns = 256
    steps = hidden // columns
    states = (HEADS, LANES, LANES)
    act = hbm((rows, width), bf16)
    full = hbm((rows, width), f32)
    unit = hbm((rows, hidden), bf16)
    state = hbm(states, bf16)
    outs = [unit, unit, full, act, act, act, full, full, state, state]
    wide = pltpu.VMEM((rows, width), bf16)
    thin = pltpu.VMEM((rows, LANES), f32)
    twice = pltpu.VMEM((rows, 2 * width), bf16)
    tall = pltpu.VMEM((rows, hidden), bf16)
    return pl.pallas_call(
        back_channel_body,
        in_specs=[SMEM] + [FREE] + [VMEM] * 3 + [ANY] * 12,
        out_specs=[ANY] * len(outs),
        out_shape=outs,
        scratch_shapes=[
            wide, tall, tall, wide, thin, wide, thin, twice, wide, twice,
            pltpu.VMEM(states, bf16), thin, thin, pltpu.VMEM(states, bf16),
        ]
        + [pltpu.VMEM(o.shape, o.dtype) for o in outs]
        + [
            pltpu.VMEM((rows, width), f32),
            wide,
            pltpu.VMEM((rows, columns), bf16),
            pltpu.VMEM((rows, columns), bf16),
            pltpu.SemaphoreType.DMA((14,)),
            pltpu.SemaphoreType.DMA((5,)),
            pltpu.SemaphoreType.DMA((2, steps)),
            pltpu.SemaphoreType.DMA((3, HEADS // 2)),
        ],
        compiler_params=params(22),
        cost_estimate=pl.CostEstimate(
            flops=2 * rows * width * (width + 3 * hidden),
            bytes_accessed=2 * width * (width + 3 * hidden),
            transcendentals=0,
        ),
        name="back_channel",
    )(
        slopes, dy, *close_by(wo, wi, wd),
        *far_away(
            r["g"], r["up"], r["h2"], r["r2"], r["mixed"], r["ra"], r["qk"], r["pre"], r["low"],
            cosine, sine, behind,
        ),
    )


def back_mixer_body(
    slope, factors, dq, du, dk, dv, qk, pre, far, near, cosine, sine, h1, r1, dmid, w,
    dkp, dvp, dx,
    dkin, dvin, kvv, kpv, vv, statev, cv, sv, h1v, r1v, dmidv, parts, dxv, total, isem, osem,
):
    rows, width = dq.shape
    ins = moves(
        (
            (dk, dkin), (dv, dvin), (qk.at[:, pl.ds(width, width)], kvv),
            (pre.at[:, pl.ds(width, width)], kpv), (pre.at[:, pl.ds(2 * width, width)], vv),
            (far, statev.at[pl.ds(0, HEADS)]), (near, statev.at[pl.ds(HEADS, HEADS)]),
            (cosine, cv), (sine, sv),
            (dq, parts.at[:, pl.ds(0, width)]), (du, parts.at[:, pl.ds(3 * width, width)]),
            (h1, h1v), (r1, r1v), (dmid, dmidv),
        ),
        isem,
    )
    for copy in ins:
        copy.start()
    for copy in ins[:9]:
        copy.wait()
    ahead = rows - row_index(rows, LANES)

    def some(i, carry):
        for m in range(4):
            n = i * 4 + m
            at = pl.multiple_of(n * LANES, LANES)
            lane = pl.ds(at, LANES)
            state = entering_state(factors, statev, n)
            decay = jnp.exp(ahead * (-slope[n]))
            keyed = (kvv[:, lane].astype(f32) * decay).astype(bf16)
            dkey = dkin[:, lane] + decay * nt(vv[:, lane], state)
            turned = dkey * cv[...] + half_turn(dkey * sv[...])
            p = kpv[:, lane].astype(f32)
            s = sigmoid(p)
            parts[:, pl.ds(at + width, LANES)] = (turned * (s * (1.0 + p * (1.0 - s)))).astype(bf16)
            parts[:, pl.ds(at + 2 * width, LANES)] = (dvin[:, lane] + nn(keyed, state)).astype(bf16)
        return carry

    lax.fori_loop(0, HEADS // 4, some, 0)
    outs = moves(
        ((parts.at[:, pl.ds(width, width)], dkp), (parts.at[:, pl.ds(2 * width, width)], dvp)), osem
    )
    for copy in outs:
        copy.start()
    for copy in ins[9:]:
        copy.wait()
    columns = 256

    def step(j, carry):
        at = pl.ds(pl.multiple_of(j * columns, LANES), columns)
        total[:, at] = nt(parts[...], w[at, :])
        return carry

    lax.fori_loop(0, width // columns, step, 0)
    back = norm_back(total[...], h1v[...].astype(f32), r1v[:, 0:1], width)
    dxv[...] = (dmidv[...] + back).astype(bf16)
    last = moves(((dxv, dx),), osem, 2)
    for copy in last:
        copy.start()
    for copy in outs + last:
        copy.wait()


def back_mixer(slopes, factors, r, entering, cosine, sine, w):
    rows, width = r["dq"].shape
    act = hbm((rows, width), bf16)
    wide = pltpu.VMEM((rows, width), bf16)
    full = pltpu.VMEM((rows, width), f32)
    thin = pltpu.VMEM((rows, LANES), f32)
    return pl.pallas_call(
        back_mixer_body,
        in_specs=[SMEM] * 2 + [ANY] * 6 + [FREE] * 2 + [ANY] * 5 + [VMEM],
        out_specs=[ANY] * 3,
        out_shape=[act, act, act],
        scratch_shapes=[
            full, full, wide, wide, wide, pltpu.VMEM((2 * HEADS, LANES, LANES), bf16), thin, thin,
            wide, thin,
            full,
            pltpu.VMEM((rows, w.shape[1]), bf16), wide, full,
            pltpu.SemaphoreType.DMA((14,)),
            pltpu.SemaphoreType.DMA((3,)),
        ],
        compiler_params=params(14),
        cost_estimate=pl.CostEstimate(
            flops=2 * rows * width * w.shape[1],
            bytes_accessed=2 * width * w.shape[1],
            transcendentals=0,
        ),
        name="back_mixer",
    )(
        slopes, factors,
        *far_away(r["dq"], r["du"], r["dk"], r["dv"], r["qk"], r["pre"]),
        *entering,
        *far_away(cosine, sine, r["h1"], r["r1"], r["dmid"]),
        *close_by(w),
    )


def weight_body(*refs, batch, sides, groups):
    place = refs[0]
    lefts = refs[1 : 1 + 2 * batch]
    rights = refs[1 + 2 * batch : 1 + 2 * batch + 2 * batch * sides]
    outs = refs[1 + 2 * batch + 2 * batch * sides : -7]
    x, xt, ys, stage, xsem, ysem, osem = refs[-7:]
    rows = lefts[0].shape[0]
    columns = x.shape[1]
    quarter = columns // 4
    blocks = groups[0][2]

    def left_copies(section):
        return [
            pltpu.make_async_copy(
                lefts[section * batch + b], x.at[pl.ds(b * rows, rows)], xsem.at[b]
            )
            for b in range(batch)
        ]

    def right_copies(section, s):
        return [
            pltpu.make_async_copy(
                rights[(section * sides + s) * batch + b],
                ys.at[s, pl.ds(b * rows, rows)],
                ysem.at[s, b],
            )
            for b in range(batch)
        ]

    for section in range(2):

        @pl.when(place[4] == section)
        def _():
            for copy in left_copies(section):
                copy.start()
            for s in range(sides):
                for copy in right_copies(section, s):
                    copy.start()

    for copy in left_copies(0):
        copy.wait()
    def turn(piece, carry):
        at = pl.ds(pl.multiple_of(piece * 2 * LANES, LANES), 2 * LANES)
        xt[at, :] = x[:, at].T
        return carry

    lax.fori_loop(0, columns // (2 * LANES), turn, 0)

    def move(number, role, out):
        slot = number * 4 + role
        return pltpu.make_async_copy(
            stage.at[slot], out.at[pl.ds((role % 2) * blocks, blocks)], osem.at[slot]
        )

    def one(role, number, side, start):
        left = xt[pl.ds(pl.multiple_of(place[role] * quarter, 16), quarter), :]
        tile = nn(left, ys[side, :, start * LANES : (start + blocks) * LANES]).astype(bf16)
        for n in range(blocks):
            stage[number * 4 + role, n] = tile[:, head(n)]

    for number, (side, start, _) in enumerate(groups):
        if all(side != done for done, _, _ in groups[:number]):
            for copy in right_copies(0, side):
                copy.wait()

        def step(role, carry, number=number, side=side, start=start):
            one(role, number, side, start)

            @pl.when(role < 2)
            def _():
                move(number, role, outs[2 * number]).start()

            @pl.when(role >= 2)
            def _():
                move(number, role, outs[2 * number + 1]).start()

            return carry

        lax.fori_loop(0, 4, step, 0)
    for number in range(len(groups)):
        for role in range(4):
            move(number, role, outs[2 * number + role // 2]).wait()


def weight_gradient(place, lefts, rights, groups):
    batch = len(lefts[0])
    sides = len(rights[0])
    rows, columns = lefts[0][0].shape
    span = rights[0][0][0].shape[1]
    quarter = columns // 4
    blocks = groups[0][2]
    flat_left = [a for section in lefts for a in section]
    flat_right = [a for section in rights for side in section for a in side]
    out = pl.pallas_call(
        functools.partial(weight_body, batch=batch, sides=sides, groups=groups),
        in_specs=[SMEM] + [ANY] * (len(flat_left) + len(flat_right)),
        out_specs=[ANY] * (2 * len(groups)),
        out_shape=[hbm((2 * blocks, quarter, LANES), bf16)] * (2 * len(groups)),
        scratch_shapes=[
            pltpu.VMEM((batch * rows, columns), bf16),
            pltpu.VMEM((columns, batch * rows), bf16),
            pltpu.VMEM((sides, batch * rows, span), bf16),
            pltpu.VMEM((4 * len(groups), blocks, quarter, LANES), bf16),
            pltpu.SemaphoreType.DMA((batch,)),
            pltpu.SemaphoreType.DMA((sides, batch)),
            pltpu.SemaphoreType.DMA((4 * len(groups),)),
        ],
        compiler_params=params(24),
        cost_estimate=pl.CostEstimate(
            flops=2 * batch * rows * columns * sides * span,
            bytes_accessed=2 * columns * sides * span,
            transcendentals=0,
        ),
        name="weight_gradient",
    )(place, *far_away(*flat_left, *flat_right))
    return [(out[2 * n], out[2 * n + 1]) for n in range(len(groups))]


def settle_body(edge, outer, inner, *rest):
    out = rest[-1]

    def write(source):
        def one(n, carry):
            out[:, pl.ds(pl.multiple_of(n * LANES, LANES), LANES)] = source[n].astype(f32)
            return carry

        lax.fori_loop(0, source.shape[0], one, 0)

    @pl.when(edge[0] == 1)
    def _():
        write(outer)

    @pl.when(edge[0] == 0)
    def _():
        write(inner)


def settle(edge, outer, inner, total, held, number):
    blocks, quarter, _ = outer.shape
    more = [] if held is None else [held]
    return pl.pallas_call(
        settle_body,
        grid=(1,),
        in_specs=[SMEM, whole(outer.shape), whole(inner.shape)] + [ANY] * len(more),
        out_specs=pl.BlockSpec((quarter, blocks * LANES), lambda j: (0, number)),
        out_shape=hbm((quarter, total), f32),
        input_output_aliases={3: 0} if more else {},
        compiler_params=params(8),
        name="settle",
    )(edge, outer, inner, *more)


def add(a, b):
    return (a.astype(f32) + b.astype(f32)).astype(bf16)


def gathered_state(own, slopes, forward):
    count = lax.axis_size("seq")
    place = lax.axis_index("seq")
    gathered = lax.all_gather(own, "seq").astype(f32)
    device = jnp.arange(count)
    distance = place - 1 - device if forward else device - place - 1
    power = jnp.maximum(distance, 0).astype(f32) * BLK
    weight = jnp.where(distance[:, None] >= 0, jnp.exp(-slopes[None] * power[:, None]), 0.0)
    return jnp.sum(weight[:, :, None, None] * gathered, axis=0).astype(bf16)


def halves(first, second):
    place = lax.axis_index("seq")
    sent = jnp.where(place % 2 == 1, first, second)
    one = lax.ppermute(sent, "seq", [(1, 0), (2, 3), (0, 2), (3, 1)])
    two = lax.ppermute(jnp.where(place == 1, second, first), "seq", [(2, 1), (1, 2)])
    return (
        jnp.where(place == 0, first, jnp.where(place == 1, two, one)),
        jnp.where(place == 3, second, jnp.where(place == 2, two, one)),
    )


def quarters(low, high):
    place = lax.axis_index("seq")
    one = lax.ppermute(jnp.where(place < 2, high, low), "seq", [(0, 1), (3, 2), (2, 0), (1, 3)])
    two = lax.ppermute(jnp.where(place == 1, low, high), "seq", [(1, 2), (2, 1)])
    return (
        jnp.where(place == 0, low, jnp.where(place == 2, two, one)),
        jnp.where(place == 3, high, jnp.where(place == 1, two, one)),
    )


class Sums:
    def __init__(self, edge, settled):
        self.edge = edge
        self.settled = settled
        self.waiting, self.parts, self.partial, self.across = [], [], [], []
        self.previous = None
        self.step = 0
        self.marks = []
        self.written = None

    def load(self, chunks):
        for given, kept in chunks:
            blocks = given.shape[0] // 2
            taken = lax.ppermute(given, "seq", [(0, 1), (1, 0), (2, 3), (3, 2)])
            self.waiting.append((add(kept[:blocks], taken[:blocks]), kept[blocks:], taken[blocks:]))

    def over_y(self):
        if not self.waiting:
            return
        far, own, other = self.waiting.pop(0)
        if self.previous is not None:
            far, _ = lax.optimization_barrier((far, self.previous))
        self.marks.append(far)
        self.previous = lax.ppermute(far, "seq", [(0, 2), (2, 0), (1, 3), (3, 1)])
        total = own.astype(f32) + other.astype(f32) + self.previous.astype(f32)
        self.parts.append(total.astype(bf16))

    def over_z(self, last=False):
        step, count = self.step, len(self.parts)
        if step >= count + 2 or (step >= count and not last):
            return False
        part = self.parts[step] if step < count else None
        done = None
        if step >= 2:
            done = self.partial[step - 2].astype(f32) + self.across[step - 2].astype(f32)
        if part is not None and self.written is not None:
            part, _ = lax.optimization_barrier((part, self.written))
            self.written = None
        if 1 <= step <= count:
            self.marks.append(self.partial[step - 1])
            self.across.append(lax.ppermute(self.partial[step - 1], "dp", [(1, 2), (2, 1)]))
        if part is not None and done is not None and part.shape == done.shape:
            sent = jnp.where(self.edge, part.astype(f32), done).astype(bf16)
            self.marks.append(sent)
            got = lax.ppermute(sent, "dp", [(0, 1), (1, 0), (2, 3), (3, 2)])
            self.partial.append(add(part, got))
            self.written = self.settled(got, sent)
        else:
            if part is not None:
                self.marks.append(part)
                self.partial.append(add(part, lax.ppermute(part, "dp", [(0, 1), (3, 2)])))
            if done is not None:
                done = done.astype(bf16)
                self.marks.append(done)
                self.written = self.settled(lax.ppermute(done, "dp", [(1, 0), (2, 3)]), done)
        self.step += 1
        return True

    def started(self):
        marks, self.marks = self.marks, []
        return marks


def angle_tables(position_row, half_size):
    frequency = jnp.exp(
        jnp.arange(half_size, dtype=jnp.float32) * (-math.log(theta_base) / half_size)
    )
    angles = position_row.astype(jnp.float32)[..., None] * frequency
    cosine = jnp.cos(angles)
    sine_rows = jnp.sin(angles)
    return (
        jnp.concatenate([cosine, cosine], axis=-1),
        jnp.concatenate([-sine_rows, sine_rows], axis=-1),
    )


class Order:
    def __init__(self):
        self.last = []

    def after(self, value):
        if self.last:
            value = lax.optimization_barrier((value, *self.last))[0]
        return value

    def at(self, *values):
        self.last = list(values)


class Layer:
    def __init__(self, order, slopes, factors, chained, cosine, sine, weights, first_of_all):
        self.first_of_all = first_of_all
        self.order, self.slopes, self.factors, self.chained = order, slopes, factors, chained
        self.cosine, self.sine = cosine, sine
        self.w, self.wo, self.wi, self.wd = weights
        self.blocks = [None, None]
        self.entering = [None, None]
        self.later = [None, None]
        self.zero = jnp.zeros((HEADS, LANES, LANES), bf16)

    def first(self, b, x):
        before = self.blocks[0]["state"] if b == 1 else self.zero
        h1, r1, pre, qk, state, joined = project(
            self.order.after(self.slopes), x, self.cosine[b], self.sine[b], before, self.w,
            self.first_of_all and b == 0,
        )
        self.order.at(r1)
        self.blocks[b] = dict(x=x, h1=h1, r1=r1, pre=pre, qk=qk, state=state)
        if not self.chained:
            self.entering[b] = gathered_state(state, self.slopes, True)
        elif b == 1:
            near = lax.ppermute(joined, "seq", [(0, 1), (2, 3)])
            self.entering = [near, near]

    def second(self, b):
        r = self.blocks[b]
        near = self.blocks[0]["state"] if b == 1 else self.entering[b]
        mixed, gated, ra, h2, r2, low, g, up, product, y = finish(
            self.order.after(self.slopes), self.factors[b], r["x"], r["qk"], r["pre"],
            (self.entering[b], near), self.wo, self.wi, self.wd,
        )
        self.order.at(ra)
        r.update(
            mixed=mixed, gated=gated, ra=ra, h2=h2, r2=r2, low=low, g=g, up=up, product=product
        )
        return y

    def back_first(self, b, dy):
        r = self.blocks[b]
        behind = self.blocks[1]["dstate"] if b == 0 else self.zero
        dg, dup, dmid, dm, dq, du, dk, dv, state, joined = back_channel(
            self.order.after(self.slopes), dy, r, self.cosine[b], self.sine[b], behind,
            self.wo, self.wi, self.wd,
        )
        self.order.at(dm)
        r.update(dy=dy, dg=dg, dup=dup, dmid=dmid, dm=dm, dq=dq, du=du, dk=dk, dv=dv, dstate=state)
        if not self.chained:
            self.later[b] = gathered_state(state, self.slopes, False)
        elif b == 0:
            near = lax.ppermute(joined, "seq", [(1, 0), (3, 2)])
            self.later = [near, near]

    def back_second(self, b):
        r = self.blocks[b]
        near = self.blocks[1]["dstate"] if b == 0 else self.later[b]
        dkp, dvp, dx = back_mixer(
            self.order.after(self.slopes), self.factors[1 - b], r, (self.later[b], near),
            self.cosine[b], self.sine[b], self.w,
        )
        self.order.at(dkp)
        r.update(dkp=dkp, dvp=dvp)
        return dx


def per_device(boundary, positions, decay_exp, mixer_in, mixer_out, channel_in, channel_out):
    section = lax.axis_index("section")
    is_first = section == 0
    batch, rows, width = boundary.shape[1:]
    assert rows == BLK and batch == 2
    slopes = jnp.exp2(-0.5 * decay_exp[0].astype(jnp.float32))
    w, wo, wi, wd = weights = mixer_in[0], mixer_out[0], channel_in[0], channel_out[0]
    hidden = wd.shape[0]
    half_size = width // HEADS // 2
    usual = lax.axis_size("seq") == 4 and lax.axis_size("dp") == 4
    place, line = lax.axis_index("seq"), lax.axis_index("dp")
    core, y_place = place % 2, place // 2

    own = (boundary[0, 0], boundary[0, 1])
    if usual:
        own = halves(*own)
        every = lax.all_gather(positions, "seq")
        chosen = lax.dynamic_index_in_dim(every, y_place, 1, keepdims=False)
        positions = lax.dynamic_slice_in_dim(chosen, 2 * core, 2, 0)
    cosine, sine = angle_tables(positions, half_size)

    roles = [
        2 * (1 - y_place) + 1 - core,
        2 * y_place + 1 - core,
        2 * (1 - y_place) + core,
        2 * y_place + core,
    ]
    if not usual:
        roles = [0, 1, 2, 3]
    roles = jnp.stack([jnp.asarray(r, jnp.int32) for r in (*roles, section)])
    edge = (line == 0) | (line == lax.axis_size("dp") - 1)
    flag = edge.astype(jnp.int32)[None]
    one = jnp.ones_like(slopes)
    factors = [jnp.stack([one, 0.0 * one])] * 2
    if usual:
        factors[1] = jnp.stack([jnp.exp(-slopes * BLK), one])
    roles, flag, slopes, *factors = lax.optimization_barrier((roles, flag, slopes, *factors))
    edge = flag[0] == 1
    order = Order()
    order.at(roles, flag)
    layers = [
        Layer(order, slopes, factors, usual, cosine, sine, weights, number == 0)
        for number in range(2)
    ]
    early, late = layers

    for b in range(2):
        early.first(b, own[b])
    arrived = [lax.ppermute(early.second(b), "section", [(0, 1)]) for b in range(2)]
    for b in range(2):
        late.first(b, arrived[b])
    outputs = [late.second(b) for b in range(2)]
    for b in (1, 0):
        late.back_first(b, own[b])
    returned = [None, None]
    for b in (1, 0):
        returned[b] = lax.ppermute(late.back_second(b), "section", [(1, 0)])

    def operands(*names):
        return [[[r[name] for r in layer.blocks] for name in names] for layer in layers]

    chunks = []
    spans = [(3, width), (3, width)] + [(2, 2 * hidden)] * 4 + [(1, width)] + [(0, 4 * width)] * 4
    numbers = [0, 1, 0, 1, 2, 3, 0, 0, 1, 2, 3]
    held = [None] * 4
    finished = []

    def settled(outer, inner):
        number = len(finished)
        index, total = spans[number]
        blocks, quarter = chunks[number][0].shape[0] // 2, chunks[number][0].shape[1]
        shape = (blocks, quarter, LANES)
        finished.append(number)
        held[index] = settle(
            flag, outer.reshape(shape), inner.reshape(shape), total, held[index], numbers[number]
        )
        return held[index]

    sums = Sums(edge, settled)

    def even(array):
        return array.reshape(array.shape[0] * array.shape[1] // 256, 256, LANES)

    def gradient(name, names, groups):
        left = [side[0] for side in operands(name)]
        found = weight_gradient(order.after(roles), left, operands(*names), groups)
        order.at(found[-1][1])
        chunks.extend(found)
        if usual:
            sums.load([(even(given), even(kept)) for given, kept in found])

    def move(*what):
        if not usual:
            return
        for way in what:
            way()
        order.at(*order.last, *sums.started())

    half, eight = hidden // LANES // 2, width // LANES
    early.back_first(1, returned[1])
    early.blocks[0]["dy"] = returned[0]
    gradient("product", ("dy",), [(0, 0, 4), (0, 4, 4)])
    move(sums.over_y)
    early.back_first(0, returned[0])
    pass
    gradient("h2", ("dg", "dup"), [(0, 0, half), (0, half, half), (1, 0, half), (1, half, half)])
    pass
    dx = [None, None]
    for b in (1, 0):
        dx[b] = early.back_second(b)
    move(sums.over_y, sums.over_z)
    gradient("gated", ("dm",), [(0, 0, eight)])
    gradient("h1", ("dq", "dkp", "dvp", "du"), [(s, 0, eight) for s in range(4)])

    ends = [jnp.where(is_first, dx[b], outputs[b]) for b in range(2)]
    joined = jnp.stack(quarters(*ends) if usual else ends)[None]
    if usual:
        while sums.waiting:
            move(sums.over_y, sums.over_z)
        while sums.over_z(last=True):
            pass
        return (joined, *(h[None] for h in held))
    found = [[], [], [], []]
    for (index, total), chunk in zip(spans, chunks):
        chunk = jnp.concatenate(chunk)
        blocks, quarter = chunk.shape[0] // 4, chunk.shape[1]
        rows_first = chunk.reshape(4, blocks, quarter, LANES).transpose(0, 2, 1, 3)
        found[index].append(rows_first.reshape(4 * quarter, blocks * LANES))
    summed = []
    for pieces in found:
        part = lax.psum_scatter(
            jnp.concatenate(pieces, axis=1), "seq", scatter_dimension=0, tiled=True
        )
        summed.append(lax.psum(part, "dp").astype(f32)[None])
    return (joined, *summed)


def solution(mesh):
    in_specs = (
        P("section", "dp", "seq", None),
        P("dp", "seq"),
        P("section", None),
        P("section", None, None),
        P("section", None, None),
        P("section", None, None),
        P("section", None, None),
    )
    out_specs = (
        P("section", "dp", "seq", None),
        P("section", "seq", None),
        P("section", "seq", None),
        P("section", "seq", None),
        P("section", "seq", None),
    )
    return jax.shard_map(
        per_device, mesh=mesh, in_specs=in_specs, out_specs=out_specs, check_vma=False
    )
```

```python
import functools
import math

import jax
import jax.numpy as jnp
from jax import lax
from jax.experimental import pallas as pl
from jax.experimental.pallas import tpu as pltpu
from jax.sharding import PartitionSpec as P

HEADS = 8
BLK = 256
LANES = 128
STEPS = 8

epsilon = 1e-06
theta_base = 10000.0
f32 = jnp.float32
bf16 = jnp.bfloat16


def nn(a, b):
    return jnp.dot(a, b, preferred_element_type=f32)


def nt(a, b):
    return lax.dot_general(a, b, (((1,), (1,)), ((), ())), preferred_element_type=f32)


def tn(a, b):
    return lax.dot_general(a, b, (((0,), (0,)), ((), ())), preferred_element_type=f32)


def sigmoid(v):
    return 1.0 / (1.0 + jnp.exp(-v))


def norm_factor(v, width):
    return lax.rsqrt(jnp.sum(v * v, axis=-1, keepdims=True) * (1.0 / width) + epsilon)


def norm_back(cotangent, normed, factor, width):
    mean = jnp.sum(cotangent * normed, axis=-1, keepdims=True) * (1.0 / width)
    return factor * (cotangent - normed * mean)


def row_index(rows, columns):
    return lax.broadcasted_iota(jnp.int32, (rows, columns), 0).astype(f32)


def decay_mask(slope, rows):
    row = lax.broadcasted_iota(jnp.int32, (rows, rows), 0)
    column = lax.broadcasted_iota(jnp.int32, (rows, rows), 1)
    distance = jnp.maximum(row - column, 0).astype(f32)
    return jnp.where(row >= column, jnp.exp(distance * (-slope)), 0.0)


def head(number):
    return slice(number * LANES, (number + 1) * LANES)


def half_turn(v):
    return pltpu.roll(v, LANES // 2, 1)


def whole(shape):
    return pl.BlockSpec(shape, lambda j: (0,) * len(shape))


def hbm(shape, kind):
    return pltpu.HBM(tuple(shape), kind)


def far_away(*arrays):
    return [pltpu.with_memory_space_constraint(a, pltpu.HBM) for a in arrays]


def close_by(*arrays):
    return [pltpu.with_memory_space_constraint(a, pltpu.VMEM) for a in arrays]


def params(megabytes):
    return pltpu.CompilerParams(vmem_limit_bytes=megabytes * 1024 * 1024)


SMEM = pl.BlockSpec(memory_space=pltpu.SMEM)
ANY = pl.BlockSpec(memory_space=pltpu.HBM)
VMEM = pl.BlockSpec(memory_space=pltpu.VMEM)
FREE = pl.BlockSpec(memory_space=pl.ANY)


def tables(position, rows):
    lane = lax.broadcasted_iota(jnp.int32, (rows, LANES), 1)
    half = LANES // 2
    feature = jnp.where(lane < half, lane, lane - half).astype(f32)
    frequency = jnp.exp(feature * (-math.log(theta_base) / half))
    angle = position * frequency
    return jnp.cos(angle), jnp.where(lane < half, -jnp.sin(angle), jnp.sin(angle))


def join(slope, before, own):
    decay = jnp.exp(jnp.full((LANES, LANES), -BLK, f32) * slope)
    return (decay * before.astype(f32) + own).astype(bf16)


def project_body(slope, x, cosine, sine, before, w, h1, r1, pre, qk, state, joined,
                 xv, cv, sv, bv, hv, rv, prev, qkv, stv, jv, isem, osem, qsem, *own):
    rows, width = x.shape
    steps = STEPS
    columns = w.shape[1] // steps
    heads = columns // LANES
    first = [
        pltpu.make_async_copy(source, target, isem.at[n])
        for n, (source, target) in enumerate(((x, xv), (cosine, cv), (sine, sv), (before, bv)))
    ]
    for copy in first:
        copy.start()

    def weight(j):
        at = pl.ds(pl.multiple_of(j * columns, LANES), columns)
        return pltpu.make_async_copy(w.at[:, at], own[0].at[j], own[1].at[j])

    if own:
        for j in range(steps):
            weight(j).start()
    first[0].wait()
    v = xv[...].astype(f32)
    factor = norm_factor(v, width)
    hv[...] = (v * factor).astype(bf16)
    rv[...] = jnp.broadcast_to(factor, rv.shape)
    for copy in first[1:]:
        copy.wait()
    outs = [pltpu.make_async_copy(hv, h1, osem.at[0]), pltpu.make_async_copy(rv, r1, osem.at[1])]
    for copy in outs:
        copy.start()

    def pre_out(j):
        at = pl.ds(pl.multiple_of(j * columns, LANES), columns)
        return pltpu.make_async_copy(prev.at[:, at], pre.at[:, at], osem.at[3 + j])

    def qk_out(j):
        at = pl.ds(pl.multiple_of(j * columns, LANES), columns)
        return pltpu.make_async_copy(qkv.at[:, at], qk.at[:, at], qsem.at[j])

    def step(j, carry):
        at = pl.multiple_of(j * columns, LANES)
        if own:
            weight(j).wait()
            p = nn(hv[...], own[0][j])
        else:
            p = nn(hv[...], w[:, pl.ds(at, columns)])
        prev[:, pl.ds(at, columns)] = p.astype(bf16)
        pre_out(j).start()

        @pl.when(j < steps // 2)
        def _():
            for n in range(heads):
                v = p[:, head(n)]
                v = v * sigmoid(v)
                turned = v * cv[...] + half_turn(v) * sv[...]
                qkv[:, pl.ds(at + n * LANES, LANES)] = turned.astype(bf16)
            qk_out(j).start()

        @pl.when((j >= steps // 2) & (j < 3 * steps // 4))
        def _():
            values = p.astype(bf16)
            ahead = rows - row_index(rows, LANES)
            for n in range(heads):
                number = (j - steps // 2) * heads + n
                decay = jnp.exp(ahead * (-slope[number]))
                key = qkv[:, pl.ds(at - width + n * LANES, LANES)]
                keyed = (key.astype(f32) * decay).astype(bf16)
                own = tn(keyed, values[:, head(n)])
                stv[number] = own.astype(bf16)
                jv[number] = join(slope[number], bv[number], own)

        return carry

    lax.fori_loop(0, steps, step, 0)
    last = [
        pltpu.make_async_copy(stv, state, osem.at[11]),
        pltpu.make_async_copy(jv, joined, osem.at[12]),
    ]
    for copy in last:
        copy.start()
    for copy in outs + last:
        copy.wait()
    for j in range(steps):
        pre_out(j).wait()
    for j in range(steps // 2):
        qk_out(j).wait()


def project(slopes, x, cosine, sine, before, w, streamed):
    rows, width = x.shape
    total = w.shape[1]
    states = (HEADS, LANES, LANES)
    return pl.pallas_call(
        project_body,
        in_specs=[SMEM, FREE] + [ANY] * 3 + [ANY if streamed else VMEM],
        out_specs=[ANY] * 6,
        out_shape=[
            hbm((rows, width), bf16),
            hbm((rows, LANES), f32),
            hbm((rows, total), bf16),
            hbm((rows, total // 2), bf16),
            hbm(states, bf16),
            hbm(states, bf16),
        ],
        scratch_shapes=[
            pltpu.VMEM((rows, width), bf16),
            pltpu.VMEM((rows, LANES), f32),
            pltpu.VMEM((rows, LANES), f32),
            pltpu.VMEM(states, bf16),
            pltpu.VMEM((rows, width), bf16),
            pltpu.VMEM((rows, LANES), f32),
            pltpu.VMEM((rows, total), bf16),
            pltpu.VMEM((rows, total // 2), bf16),
            pltpu.VMEM(states, bf16),
            pltpu.VMEM(states, bf16),
            pltpu.SemaphoreType.DMA((4,)),
            pltpu.SemaphoreType.DMA((13,)),
            pltpu.SemaphoreType.DMA((STEPS // 2,)),
        ]
        + [
            pltpu.VMEM((STEPS, width, total // STEPS), bf16),
            pltpu.SemaphoreType.DMA((STEPS,)),
        ]
        * streamed,
        compiler_params=params(18 if streamed else 8),
        cost_estimate=pl.CostEstimate(
            flops=2 * rows * width * total, bytes_accessed=2 * width * total, transcendentals=0
        ),
        name="project",
    )(slopes, x, *far_away(cosine, sine, before), *(far_away(w) if streamed else close_by(w)))


def moves(pairs, sem, start=0):
    return [
        pltpu.make_async_copy(source, target, sem.at[start + n])
        for n, (source, target) in enumerate(pairs)
    ]


def entering_state(factors, states, number):
    state = factors[0, number] * states[number].astype(f32)
    state += factors[1, number] * states[HEADS + number].astype(f32)
    return state.astype(bf16)


def finish_body(
    slope, factors, x, qk, pre, far, near, wo, wi, wd,
    mixed, gated, ra, h2, r2, low, g, up, product, y,
    xv, qkv, vuv, statev, mixedv, gatedv, rav, h2v, r2v, lowv, gv, upv, productv, yv,
    attended, total, held, isem, osem, csem,
):
    rows, width = x.shape
    hidden = wd.shape[0]
    columns = held.shape[1]
    steps = hidden // columns
    ins = moves(
        (
            (qk, qkv), (pre.at[:, pl.ds(2 * width, 2 * width)], vuv),
            (far, statev.at[pl.ds(0, HEADS)]), (near, statev.at[pl.ds(HEADS, HEADS)]), (x, xv),
        ),
        isem,
    )
    for copy in ins:
        copy.start()
    for copy in ins[:4]:
        copy.wait()
    ahead = row_index(rows, LANES)

    def pair(i, carry):
        for m in range(2):
            n = i * 2 + m
            at = pl.multiple_of(n * LANES, LANES)
            lane = pl.ds(at, LANES)
            state = entering_state(factors, statev, n)
            lowv[n] = state
            query = qkv[:, lane]
            key = qkv[:, pl.ds(at + width, LANES)]
            weights = (decay_mask(slope[n], rows) * nt(query, key)).astype(bf16)
            inner = nn(weights, vuv[:, lane])
            carried = nn(query, state)
            attended[:, lane] = inner + jnp.exp(ahead * (-slope[n])) * carried
        return carry

    lax.fori_loop(0, HEADS // 2, pair, 0)
    rows_out = attended[...]
    factor = norm_factor(rows_out, width)
    rav[...] = jnp.broadcast_to(factor, rav.shape)
    normed = rows_out * factor
    mixedv[...] = normed.astype(bf16)
    gatedv[...] = (normed * vuv[:, width:].astype(f32)).astype(bf16)
    outs = moves(((mixedv, mixed), (gatedv, gated), (rav, ra), (lowv, low)), osem)
    for copy in outs:
        copy.start()
    ins[4].wait()
    middle = xv[...].astype(f32) + nn(gatedv[...], wo[...])
    total[...] = middle
    factor = norm_factor(middle, width)
    r2v[...] = jnp.broadcast_to(factor, r2v.shape)
    h2v[...] = (middle * factor).astype(bf16)
    more = moves(((h2v, h2), (r2v, r2)), osem, 4)
    for copy in more:
        copy.start()
    held[...] = jnp.zeros_like(held)

    def chunk_out(i):
        at = pl.ds(pl.multiple_of(i * columns, LANES), columns)
        return [
            pltpu.make_async_copy(source.at[:, at], target.at[:, at], csem.at[n, i])
            for n, (source, target) in enumerate(((gv, g), (upv, up), (productv, product)))
        ]

    def step(i, carry):
        start = pl.multiple_of(i * columns, LANES)
        before = pl.multiple_of(jnp.maximum(i - 1, 0) * columns, LANES)
        at = pl.ds(start, columns)
        total[...] += nn(held[...], wd[pl.ds(before, columns), :])
        gate = nn(h2v[...], wi[:, at])
        rise = nn(h2v[...], wi[:, pl.ds(start + hidden, columns)])
        both = (gate * rise).astype(bf16)
        gv[:, at] = gate.astype(bf16)
        upv[:, at] = rise.astype(bf16)
        productv[:, at] = both
        held[...] = both
        for copy in chunk_out(i):
            copy.start()
        return carry

    lax.fori_loop(0, steps, step, 0)
    yv[...] = (total[...] + nn(held[...], wd[hidden - columns :, :])).astype(bf16)
    last = moves(((yv, y),), osem, 6)
    for copy in last:
        copy.start()
    for copy in outs + more + last:
        copy.wait()

    def drain(i, carry):
        for copy in chunk_out(i):
            copy.wait()
        return carry

    lax.fori_loop(0, steps, drain, 0)


def finish(slopes, factors, x, qk, pre, entering, wo, wi, wd):
    rows, width = x.shape
    hidden = wd.shape[0]
    columns = 256
    steps = hidden // columns
    states = (HEADS, LANES, LANES)
    act = hbm((rows, width), bf16)
    factor = hbm((rows, LANES), f32)
    unit = hbm((rows, hidden), bf16)
    outs = [
        act, act, factor, act, factor, hbm(states, bf16), unit, unit, unit, act,
    ]
    return pl.pallas_call(
        finish_body,
        in_specs=[SMEM] * 2 + [FREE] + [ANY] * 2 + [FREE] * 2 + [VMEM] * 3,
        out_specs=[ANY] * len(outs),
        out_shape=outs,
        scratch_shapes=[
            pltpu.VMEM((rows, width), bf16),
            pltpu.VMEM((rows, 2 * width), bf16),
            pltpu.VMEM((rows, 2 * width), bf16),
            pltpu.VMEM((2 * HEADS, LANES, LANES), bf16),
        ]
        + [pltpu.VMEM(o.shape, o.dtype) for o in outs]
        + [
            pltpu.VMEM((rows, width), f32),
            pltpu.VMEM((rows, width), f32),
            pltpu.VMEM((rows, columns), bf16),
            pltpu.SemaphoreType.DMA((5,)),
            pltpu.SemaphoreType.DMA((7,)),
            pltpu.SemaphoreType.DMA((3, steps)),
        ],
        compiler_params=params(18),
        cost_estimate=pl.CostEstimate(
            flops=2 * rows * width * (width + 3 * hidden),
            bytes_accessed=2 * width * (width + 3 * hidden),
            transcendentals=0,
        ),
        name="finish",
    )(slopes, factors, x, *far_away(qk, pre), *entering, *close_by(wo, wi, wd))


def back_channel_body(
    slope, dy, wo, wi, wd, g, up, h2, r2, mixed, ra, qk, pre, low, cosine, sine, behind,
    dg, dup, dmid, dm, dq, du, dk, dv, state, joined,
    dyv, gv, upv, h2v, r2v, mixedv, rav, qkv, qpv, vuv, lowv, cv, sv, bv,
    dgv, dupv, dmidv, dmv, dqv, duv, dkv, dvv, statev, jv,
    total, datt, heldg, heldu, isem, osem, csem, psem,
):
    rows, width = dy.shape
    hidden = wd.shape[0]
    columns = heldg.shape[1]
    steps = hidden // columns
    ins = moves(
        (
            (dy, dyv), (g, gv), (up, upv), (h2, h2v), (r2, r2v), (mixed, mixedv), (ra, rav),
            (qk, qkv), (pre.at[:, pl.ds(0, width)], qpv),
            (pre.at[:, pl.ds(2 * width, 2 * width)], vuv), (low, lowv), (cosine, cv), (sine, sv),
            (behind, bv),
        ),
        isem,
    )
    for copy in ins[:3]:
        copy.start()
    for copy in ins[:3]:
        copy.wait()
    for copy in ins[3:]:
        copy.start()
    heldg[...] = jnp.zeros_like(heldg)
    heldu[...] = jnp.zeros_like(heldu)
    total[...] = jnp.zeros_like(total)

    def chunk_out(i):
        at = pl.ds(pl.multiple_of(i * columns, LANES), columns)
        return [
            pltpu.make_async_copy(source.at[:, at], target.at[:, at], csem.at[n, i])
            for n, (source, target) in enumerate(((dgv, dg), (dupv, dup)))
        ]

    def step(i, carry):
        at = pl.ds(pl.multiple_of(i * columns, LANES), columns)
        before = pl.multiple_of(jnp.maximum(i - 1, 0) * columns, LANES)
        total[...] += nt(heldg[...], wi[:, pl.ds(before, columns)]) + nt(
            heldu[...], wi[:, pl.ds(before + hidden, columns)]
        )
        product = nt(dyv[...], wd[at, :])
        left = (product * upv[:, at].astype(f32)).astype(bf16)
        right = (product * gv[:, at].astype(f32)).astype(bf16)
        dgv[:, at] = left
        dupv[:, at] = right
        heldg[...] = left
        heldu[...] = right
        for copy in chunk_out(i):
            copy.start()
        return carry

    lax.fori_loop(0, steps, step, 0)
    for copy in ins[3:]:
        copy.wait()
    dh2 = (
        total[...]
        + nt(heldg[...], wi[:, hidden - columns : hidden])
        + nt(heldu[...], wi[:, 2 * hidden - columns :])
    )
    middle = dyv[...].astype(f32) + norm_back(dh2, h2v[...].astype(f32), r2v[:, 0:1], width)
    dmidv[...] = middle
    dmv[...] = middle.astype(bf16)
    outs = moves(((dmidv, dmid), (dmv, dm)), osem)
    for copy in outs:
        copy.start()
    dgated = nt(dmv[...], wo[...])
    normed = mixedv[...].astype(f32)
    duv[...] = (dgated * normed).astype(bf16)
    back = norm_back(dgated * vuv[:, width:].astype(f32), normed, rav[:, 0:1], width)
    datt[...] = back.astype(bf16)
    ahead = row_index(rows, LANES)
    row = lax.broadcasted_iota(jnp.int32, (rows, rows), 0)
    column = lax.broadcasted_iota(jnp.int32, (rows, rows), 1)
    distance = (row - column).astype(f32)

    early = moves(((duv, du),), osem, 2)
    for copy in early:
        copy.start()

    def pair_out(i):
        at = pl.ds(pl.multiple_of(i * 2 * LANES, LANES), 2 * LANES)
        return [
            pltpu.make_async_copy(source.at[:, at], target.at[:, at], psem.at[n, i])
            for n, (source, target) in enumerate(((dqv, dq), (dkv, dk), (dvv, dv)))
        ]

    def some(i, carry):
        for m in range(2):
            n = i * 2 + m
            at = pl.multiple_of(n * LANES, LANES)
            lane = pl.ds(at, LANES)
            query, key = qkv[:, lane], qkv[:, pl.ds(at + width, LANES)]
            value, cot = vuv[:, lane], datt[:, lane]
            power = jnp.exp(jnp.abs(distance) * (-slope[n]))
            mask = jnp.where(distance >= 0.0, power, 0.0)
            flipped = jnp.where(distance <= 0.0, power, 0.0)
            weights_t = (flipped * nt(key, query)).astype(bf16)
            scores = (mask * nt(cot, value)).astype(bf16)
            scores_t = (flipped * nt(value, cot)).astype(bf16)
            scaled = (jnp.exp(ahead * (-slope[n])) * cot.astype(f32)).astype(bf16)
            own = tn(query, scaled)
            statev[n] = own.astype(bf16)
            jv[n] = join(slope[n], bv[n], own)
            dquery = nn(scores, key) + nt(scaled, lowv[n])
            turned = dquery * cv[...] + half_turn(dquery * sv[...])
            p = qpv[:, lane].astype(f32)
            s = sigmoid(p)
            dqv[:, lane] = (turned * (s * (1.0 + p * (1.0 - s)))).astype(bf16)
            dkv[:, lane] = nn(scores_t, query).astype(bf16)
            dvv[:, lane] = nn(weights_t, cot).astype(bf16)
        for copy in pair_out(i):
            copy.start()
        return carry

    lax.fori_loop(0, HEADS // 2, some, 0)
    last = moves(((statev, state), (jv, joined)), osem, 3)
    for copy in last:
        copy.start()
    for copy in outs + early + last:
        copy.wait()
    for i in range(HEADS // 2):
        for copy in pair_out(i):
            copy.wait()

    def drain(i, carry):
        for copy in chunk_out(i):
            copy.wait()
        return carry

    lax.fori_loop(0, steps, drain, 0)


def back_channel(slopes, dy, r, cosine, sine, behind, wo, wi, wd):
    rows, width = dy.shape
    hidden = wd.shape[0]
    columns = 256
    steps = hidden // columns
    states = (HEADS, LANES, LANES)
    act = hbm((rows, width), bf16)
    full = hbm((rows, width), f32)
    unit = hbm((rows, hidden), bf16)
    state = hbm(states, bf16)
    outs = [unit, unit, full, act, act, act, act, act, state, state]
    wide = pltpu.VMEM((rows, width), bf16)
    thin = pltpu.VMEM((rows, LANES), f32)
    twice = pltpu.VMEM((rows, 2 * width), bf16)
    tall = pltpu.VMEM((rows, hidden), bf16)
    return pl.pallas_call(
        back_channel_body,
        in_specs=[SMEM] + [FREE] + [VMEM] * 3 + [ANY] * 12,
        out_specs=[ANY] * len(outs),
        out_shape=outs,
        scratch_shapes=[
            wide, tall, tall, wide, thin, wide, thin, twice, wide, twice,
            pltpu.VMEM(states, bf16), thin, thin, pltpu.VMEM(states, bf16),
        ]
        + [pltpu.VMEM(o.shape, o.dtype) for o in outs]
        + [
            pltpu.VMEM((rows, width), f32),
            wide,
            pltpu.VMEM((rows, columns), bf16),
            pltpu.VMEM((rows, columns), bf16),
            pltpu.SemaphoreType.DMA((14,)),
            pltpu.SemaphoreType.DMA((5,)),
            pltpu.SemaphoreType.DMA((2, steps)),
            pltpu.SemaphoreType.DMA((3, HEADS // 2)),
        ],
        compiler_params=params(22),
        cost_estimate=pl.CostEstimate(
            flops=2 * rows * width * (width + 3 * hidden),
            bytes_accessed=2 * width * (width + 3 * hidden),
            transcendentals=0,
        ),
        name="back_channel",
    )(
        slopes, dy, *close_by(wo, wi, wd),
        *far_away(
            r["g"], r["up"], r["h2"], r["r2"], r["mixed"], r["ra"], r["qk"], r["pre"], r["low"],
            cosine, sine, behind,
        ),
    )


def back_mixer_body(
    slope, factors, dq, du, dk, dv, qk, pre, far, near, cosine, sine, h1, r1, dmid, w,
    dkp, dvp, dx,
    dkin, dvin, kvv, kpv, vv, statev, cv, sv, h1v, r1v, dmidv, parts, dxv, total, isem, osem,
):
    rows, width = dq.shape
    ins = moves(
        (
            (dk, dkin), (dv, dvin), (qk.at[:, pl.ds(width, width)], kvv),
            (pre.at[:, pl.ds(width, width)], kpv), (pre.at[:, pl.ds(2 * width, width)], vv),
            (far, statev.at[pl.ds(0, HEADS)]), (near, statev.at[pl.ds(HEADS, HEADS)]),
            (cosine, cv), (sine, sv),
            (dq, parts.at[:, pl.ds(0, width)]), (du, parts.at[:, pl.ds(3 * width, width)]),
            (h1, h1v), (r1, r1v), (dmid, dmidv),
        ),
        isem,
    )
    for copy in ins:
        copy.start()
    for copy in ins[:9]:
        copy.wait()
    ahead = rows - row_index(rows, LANES)

    def some(i, carry):
        for m in range(4):
            n = i * 4 + m
            at = pl.multiple_of(n * LANES, LANES)
            lane = pl.ds(at, LANES)
            state = entering_state(factors, statev, n)
            decay = jnp.exp(ahead * (-slope[n]))
            keyed = (kvv[:, lane].astype(f32) * decay).astype(bf16)
            dkey = dkin[:, lane].astype(f32) + decay * nt(vv[:, lane], state)
            turned = dkey * cv[...] + half_turn(dkey * sv[...])
            p = kpv[:, lane].astype(f32)
            s = sigmoid(p)
            parts[:, pl.ds(at + width, LANES)] = (turned * (s * (1.0 + p * (1.0 - s)))).astype(bf16)
            parts[:, pl.ds(at + 2 * width, LANES)] = (
                dvin[:, lane].astype(f32) + nn(keyed, state)
            ).astype(bf16)
        return carry

    lax.fori_loop(0, HEADS // 4, some, 0)
    outs = moves(
        ((parts.at[:, pl.ds(width, width)], dkp), (parts.at[:, pl.ds(2 * width, width)], dvp)), osem
    )
    for copy in outs:
        copy.start()
    for copy in ins[9:]:
        copy.wait()
    columns = 256

    def step(j, carry):
        at = pl.ds(pl.multiple_of(j * columns, LANES), columns)
        total[:, at] = nt(parts[...], w[at, :])
        return carry

    lax.fori_loop(0, width // columns, step, 0)
    back = norm_back(total[...], h1v[...].astype(f32), r1v[:, 0:1], width)
    dxv[...] = (dmidv[...] + back).astype(bf16)
    last = moves(((dxv, dx),), osem, 2)
    for copy in last:
        copy.start()
    for copy in outs + last:
        copy.wait()


def back_mixer(slopes, factors, r, entering, cosine, sine, w):
    rows, width = r["dq"].shape
    act = hbm((rows, width), bf16)
    wide = pltpu.VMEM((rows, width), bf16)
    full = pltpu.VMEM((rows, width), f32)
    thin = pltpu.VMEM((rows, LANES), f32)
    return pl.pallas_call(
        back_mixer_body,
        in_specs=[SMEM] * 2 + [ANY] * 6 + [FREE] * 2 + [ANY] * 5 + [VMEM],
        out_specs=[ANY] * 3,
        out_shape=[act, act, act],
        scratch_shapes=[
            wide, wide, wide, wide, wide, pltpu.VMEM((2 * HEADS, LANES, LANES), bf16), thin, thin,
            wide, thin,
            full,
            pltpu.VMEM((rows, w.shape[1]), bf16), wide, full,
            pltpu.SemaphoreType.DMA((14,)),
            pltpu.SemaphoreType.DMA((3,)),
        ],
        compiler_params=params(14),
        cost_estimate=pl.CostEstimate(
            flops=2 * rows * width * w.shape[1],
            bytes_accessed=2 * width * w.shape[1],
            transcendentals=0,
        ),
        name="back_mixer",
    )(
        slopes, factors,
        *far_away(r["dq"], r["du"], r["dk"], r["dv"], r["qk"], r["pre"]),
        *entering,
        *far_away(cosine, sine, r["h1"], r["r1"], r["dmid"]),
        *close_by(w),
    )


def weight_body(*refs, batch, sides, groups):
    place = refs[0]
    lefts = refs[1 : 1 + 2 * batch]
    rights = refs[1 + 2 * batch : 1 + 2 * batch + 2 * batch * sides]
    outs = refs[1 + 2 * batch + 2 * batch * sides : -7]
    x, xt, ys, stage, xsem, ysem, osem = refs[-7:]
    rows = lefts[0].shape[0]
    columns = x.shape[1]
    quarter = columns // 4
    blocks = groups[0][2]

    def left_copies(section):
        return [
            pltpu.make_async_copy(
                lefts[section * batch + b], x.at[pl.ds(b * rows, rows)], xsem.at[b]
            )
            for b in range(batch)
        ]

    def right_copies(section, s):
        return [
            pltpu.make_async_copy(
                rights[(section * sides + s) * batch + b],
                ys.at[s, pl.ds(b * rows, rows)],
                ysem.at[s, b],
            )
            for b in range(batch)
        ]

    for section in range(2):

        @pl.when(place[4] == section)
        def _():
            for copy in left_copies(section):
                copy.start()
            for s in range(sides):
                for copy in right_copies(section, s):
                    copy.start()

    for copy in left_copies(0):
        copy.wait()
    def turn(piece, carry):
        at = pl.ds(pl.multiple_of(piece * 2 * LANES, LANES), 2 * LANES)
        xt[at, :] = x[:, at].T
        return carry

    lax.fori_loop(0, columns // (2 * LANES), turn, 0)

    def move(number, role, out):
        slot = number * 4 + role
        return pltpu.make_async_copy(
            stage.at[slot], out.at[pl.ds((role % 2) * blocks, blocks)], osem.at[slot]
        )

    def one(role, number, side, start):
        left = xt[pl.ds(pl.multiple_of(place[role] * quarter, 16), quarter), :]
        tile = nn(left, ys[side, :, start * LANES : (start + blocks) * LANES]).astype(bf16)
        for n in range(blocks):
            stage[number * 4 + role, n] = tile[:, head(n)]

    for number, (side, start, _) in enumerate(groups):
        if all(side != done for done, _, _ in groups[:number]):
            for copy in right_copies(0, side):
                copy.wait()

        def step(role, carry, number=number, side=side, start=start):
            one(role, number, side, start)

            @pl.when(role < 2)
            def _():
                move(number, role, outs[2 * number]).start()

            @pl.when(role >= 2)
            def _():
                move(number, role, outs[2 * number + 1]).start()

            return carry

        lax.fori_loop(0, 4, step, 0)
    for number in range(len(groups)):
        for role in range(4):
            move(number, role, outs[2 * number + role // 2]).wait()


def weight_gradient(place, lefts, rights, groups):
    batch = len(lefts[0])
    sides = len(rights[0])
    rows, columns = lefts[0][0].shape
    span = rights[0][0][0].shape[1]
    quarter = columns // 4
    blocks = groups[0][2]
    flat_left = [a for section in lefts for a in section]
    flat_right = [a for section in rights for side in section for a in side]
    out = pl.pallas_call(
        functools.partial(weight_body, batch=batch, sides=sides, groups=groups),
        in_specs=[SMEM] + [ANY] * (len(flat_left) + len(flat_right)),
        out_specs=[ANY] * (2 * len(groups)),
        out_shape=[hbm((2 * blocks, quarter, LANES), bf16)] * (2 * len(groups)),
        scratch_shapes=[
            pltpu.VMEM((batch * rows, columns), bf16),
            pltpu.VMEM((columns, batch * rows), bf16),
            pltpu.VMEM((sides, batch * rows, span), bf16),
            pltpu.VMEM((4 * len(groups), blocks, quarter, LANES), bf16),
            pltpu.SemaphoreType.DMA((batch,)),
            pltpu.SemaphoreType.DMA((sides, batch)),
            pltpu.SemaphoreType.DMA((4 * len(groups),)),
        ],
        compiler_params=params(24),
        cost_estimate=pl.CostEstimate(
            flops=2 * batch * rows * columns * sides * span,
            bytes_accessed=2 * columns * sides * span,
            transcendentals=0,
        ),
        name="weight_gradient",
    )(place, *far_away(*flat_left, *flat_right))
    return [(out[2 * n], out[2 * n + 1]) for n in range(len(groups))]


def settle_body(edge, outer, inner, *rest):
    out = rest[-1]

    def write(source):
        def one(n, carry):
            out[:, pl.ds(pl.multiple_of(n * LANES, LANES), LANES)] = source[n].astype(f32)
            return carry

        lax.fori_loop(0, source.shape[0], one, 0)

    @pl.when(edge[0] == 1)
    def _():
        write(outer)

    @pl.when(edge[0] == 0)
    def _():
        write(inner)


def settle(edge, outer, inner, total, held, number):
    blocks, quarter, _ = outer.shape
    more = [] if held is None else [held]
    return pl.pallas_call(
        settle_body,
        grid=(1,),
        in_specs=[SMEM, whole(outer.shape), whole(inner.shape)] + [ANY] * len(more),
        out_specs=pl.BlockSpec((quarter, blocks * LANES), lambda j: (0, number)),
        out_shape=hbm((quarter, total), f32),
        input_output_aliases={3: 0} if more else {},
        compiler_params=params(8),
        name="settle",
    )(edge, outer, inner, *more)


def add(a, b):
    return (a.astype(f32) + b.astype(f32)).astype(bf16)


def gathered_state(own, slopes, forward):
    count = lax.axis_size("seq")
    place = lax.axis_index("seq")
    gathered = lax.all_gather(own, "seq").astype(f32)
    device = jnp.arange(count)
    distance = place - 1 - device if forward else device - place - 1
    power = jnp.maximum(distance, 0).astype(f32) * BLK
    weight = jnp.where(distance[:, None] >= 0, jnp.exp(-slopes[None] * power[:, None]), 0.0)
    return jnp.sum(weight[:, :, None, None] * gathered, axis=0).astype(bf16)


def halves(first, second):
    place = lax.axis_index("seq")
    sent = jnp.where(place % 2 == 1, first, second)
    one = lax.ppermute(sent, "seq", [(1, 0), (2, 3), (0, 2), (3, 1)])
    two = lax.ppermute(jnp.where(place == 1, second, first), "seq", [(2, 1), (1, 2)])
    return (
        jnp.where(place == 0, first, jnp.where(place == 1, two, one)),
        jnp.where(place == 3, second, jnp.where(place == 2, two, one)),
    )


def quarters(low, high):
    place = lax.axis_index("seq")
    one = lax.ppermute(jnp.where(place < 2, high, low), "seq", [(0, 1), (3, 2), (2, 0), (1, 3)])
    two = lax.ppermute(jnp.where(place == 1, low, high), "seq", [(1, 2), (2, 1)])
    return (
        jnp.where(place == 0, low, jnp.where(place == 2, two, one)),
        jnp.where(place == 3, high, jnp.where(place == 1, two, one)),
    )


class Sums:
    def __init__(self, edge, settled):
        self.edge = edge
        self.settled = settled
        self.waiting, self.parts, self.partial, self.across = [], [], [], []
        self.previous = None
        self.step = 0
        self.marks = []
        self.written = None

    def load(self, chunks):
        for given, kept in chunks:
            blocks = given.shape[0] // 2
            taken = lax.ppermute(given, "seq", [(0, 1), (1, 0), (2, 3), (3, 2)])
            self.waiting.append((add(kept[:blocks], taken[:blocks]), kept[blocks:], taken[blocks:]))

    def over_y(self):
        if not self.waiting:
            return
        far, own, other = self.waiting.pop(0)
        if self.previous is not None:
            far, _ = lax.optimization_barrier((far, self.previous))
        self.marks.append(far)
        self.previous = lax.ppermute(far, "seq", [(0, 2), (2, 0), (1, 3), (3, 1)])
        total = own.astype(f32) + other.astype(f32) + self.previous.astype(f32)
        self.parts.append(total.astype(bf16))

    def over_z(self, last=False):
        step, count = self.step, len(self.parts)
        if step >= count + 2 or (step >= count and not last):
            return False
        part = self.parts[step] if step < count else None
        done = None
        if step >= 2:
            done = self.partial[step - 2].astype(f32) + self.across[step - 2].astype(f32)
        if part is not None and self.written is not None:
            part, _ = lax.optimization_barrier((part, self.written))
            self.written = None
        if 1 <= step <= count:
            self.marks.append(self.partial[step - 1])
            self.across.append(lax.ppermute(self.partial[step - 1], "dp", [(1, 2), (2, 1)]))
        if part is not None and done is not None and part.shape == done.shape:
            sent = jnp.where(self.edge, part.astype(f32), done).astype(bf16)
            self.marks.append(sent)
            got = lax.ppermute(sent, "dp", [(0, 1), (1, 0), (2, 3), (3, 2)])
            self.partial.append(add(part, got))
            self.written = self.settled(got, sent)
        else:
            if part is not None:
                self.marks.append(part)
                self.partial.append(add(part, lax.ppermute(part, "dp", [(0, 1), (3, 2)])))
            if done is not None:
                done = done.astype(bf16)
                self.marks.append(done)
                self.written = self.settled(lax.ppermute(done, "dp", [(1, 0), (2, 3)]), done)
        self.step += 1
        return True

    def started(self):
        marks, self.marks = self.marks, []
        return marks


def angle_tables(position_row, half_size):
    frequency = jnp.exp(
        jnp.arange(half_size, dtype=jnp.float32) * (-math.log(theta_base) / half_size)
    )
    angles = position_row.astype(jnp.float32)[..., None] * frequency
    cosine = jnp.cos(angles)
    sine_rows = jnp.sin(angles)
    return (
        jnp.concatenate([cosine, cosine], axis=-1),
        jnp.concatenate([-sine_rows, sine_rows], axis=-1),
    )


class Order:
    def __init__(self):
        self.last = []

    def after(self, value):
        if self.last:
            value = lax.optimization_barrier((value, *self.last))[0]
        return value

    def at(self, *values):
        self.last = list(values)


class Layer:
    def __init__(self, order, slopes, factors, chained, cosine, sine, weights, first_of_all):
        self.first_of_all = first_of_all
        self.order, self.slopes, self.factors, self.chained = order, slopes, factors, chained
        self.cosine, self.sine = cosine, sine
        self.w, self.wo, self.wi, self.wd = weights
        self.blocks = [None, None]
        self.entering = [None, None]
        self.later = [None, None]
        self.zero = jnp.zeros((HEADS, LANES, LANES), bf16)

    def first(self, b, x):
        before = self.blocks[0]["state"] if b == 1 else self.zero
        h1, r1, pre, qk, state, joined = project(
            self.order.after(self.slopes), x, self.cosine[b], self.sine[b], before, self.w,
            self.first_of_all and b == 0,
        )
        self.order.at(r1)
        self.blocks[b] = dict(x=x, h1=h1, r1=r1, pre=pre, qk=qk, state=state)
        if not self.chained:
            self.entering[b] = gathered_state(state, self.slopes, True)
        elif b == 1:
            near = lax.ppermute(joined, "seq", [(0, 1), (2, 3)])
            self.entering = [near, near]

    def second(self, b):
        r = self.blocks[b]
        near = self.blocks[0]["state"] if b == 1 else self.entering[b]
        mixed, gated, ra, h2, r2, low, g, up, product, y = finish(
            self.order.after(self.slopes), self.factors[b], r["x"], r["qk"], r["pre"],
            (self.entering[b], near), self.wo, self.wi, self.wd,
        )
        self.order.at(ra)
        r.update(
            mixed=mixed, gated=gated, ra=ra, h2=h2, r2=r2, low=low, g=g, up=up, product=product
        )
        return y

    def back_first(self, b, dy):
        r = self.blocks[b]
        behind = self.blocks[1]["dstate"] if b == 0 else self.zero
        dg, dup, dmid, dm, dq, du, dk, dv, state, joined = back_channel(
            self.order.after(self.slopes), dy, r, self.cosine[b], self.sine[b], behind,
            self.wo, self.wi, self.wd,
        )
        self.order.at(dm)
        r.update(dy=dy, dg=dg, dup=dup, dmid=dmid, dm=dm, dq=dq, du=du, dk=dk, dv=dv, dstate=state)
        if not self.chained:
            self.later[b] = gathered_state(state, self.slopes, False)
        elif b == 0:
            near = lax.ppermute(joined, "seq", [(1, 0), (3, 2)])
            self.later = [near, near]

    def back_second(self, b):
        r = self.blocks[b]
        near = self.blocks[1]["dstate"] if b == 0 else self.later[b]
        dkp, dvp, dx = back_mixer(
            self.order.after(self.slopes), self.factors[1 - b], r, (self.later[b], near),
            self.cosine[b], self.sine[b], self.w,
        )
        self.order.at(dkp)
        r.update(dkp=dkp, dvp=dvp)
        return dx


def per_device(boundary, positions, decay_exp, mixer_in, mixer_out, channel_in, channel_out):
    section = lax.axis_index("section")
    is_first = section == 0
    batch, rows, width = boundary.shape[1:]
    assert rows == BLK and batch == 2
    slopes = jnp.exp2(-0.5 * decay_exp[0].astype(jnp.float32))
    w, wo, wi, wd = weights = mixer_in[0], mixer_out[0], channel_in[0], channel_out[0]
    hidden = wd.shape[0]
    half_size = width // HEADS // 2
    usual = lax.axis_size("seq") == 4 and lax.axis_size("dp") == 4
    place, line = lax.axis_index("seq"), lax.axis_index("dp")
    core, y_place = place % 2, place // 2

    own = (boundary[0, 0], boundary[0, 1])
    if usual:
        own = halves(*own)
        every = lax.all_gather(positions, "seq")
        chosen = lax.dynamic_index_in_dim(every, y_place, 1, keepdims=False)
        positions = lax.dynamic_slice_in_dim(chosen, 2 * core, 2, 0)
    cosine, sine = angle_tables(positions, half_size)

    roles = [
        2 * (1 - y_place) + 1 - core,
        2 * y_place + 1 - core,
        2 * (1 - y_place) + core,
        2 * y_place + core,
    ]
    if not usual:
        roles = [0, 1, 2, 3]
    roles = jnp.stack([jnp.asarray(r, jnp.int32) for r in (*roles, section)])
    edge = (line == 0) | (line == lax.axis_size("dp") - 1)
    flag = edge.astype(jnp.int32)[None]
    one = jnp.ones_like(slopes)
    factors = [jnp.stack([one, 0.0 * one])] * 2
    if usual:
        factors[1] = jnp.stack([jnp.exp(-slopes * BLK), one])
    roles, flag, slopes, *factors = lax.optimization_barrier((roles, flag, slopes, *factors))
    edge = flag[0] == 1
    order = Order()
    order.at(roles, flag)
    layers = [
        Layer(order, slopes, factors, usual, cosine, sine, weights, number == 0)
        for number in range(2)
    ]
    early, late = layers

    for b in range(2):
        early.first(b, own[b])
    arrived = [lax.ppermute(early.second(b), "section", [(0, 1)]) for b in range(2)]
    for b in range(2):
        late.first(b, arrived[b])
    outputs = [late.second(b) for b in range(2)]
    for b in (1, 0):
        late.back_first(b, own[b])
    returned = [None, None]
    for b in (1, 0):
        returned[b] = lax.ppermute(late.back_second(b), "section", [(1, 0)])

    def operands(*names):
        return [[[r[name] for r in layer.blocks] for name in names] for layer in layers]

    chunks = []
    spans = [(3, width), (3, width)] + [(2, 2 * hidden)] * 4 + [(1, width)] + [(0, 4 * width)] * 4
    numbers = [0, 1, 0, 1, 2, 3, 0, 0, 1, 2, 3]
    held = [None] * 4
    finished = []

    def settled(outer, inner):
        number = len(finished)
        index, total = spans[number]
        blocks, quarter = chunks[number][0].shape[0] // 2, chunks[number][0].shape[1]
        shape = (blocks, quarter, LANES)
        finished.append(number)
        held[index] = settle(
            flag, outer.reshape(shape), inner.reshape(shape), total, held[index], numbers[number]
        )
        return held[index]

    sums = Sums(edge, settled)

    def even(array):
        return array.reshape(array.shape[0] * array.shape[1] // 256, 256, LANES)

    def gradient(name, names, groups):
        left = [side[0] for side in operands(name)]
        found = weight_gradient(order.after(roles), left, operands(*names), groups)
        order.at(found[-1][1])
        chunks.extend(found)
        if usual:
            sums.load([(even(given), even(kept)) for given, kept in found])

    def move(*what):
        if not usual:
            return
        for way in what:
            way()
        order.at(*order.last, *sums.started())

    half, eight = hidden // LANES // 2, width // LANES
    early.back_first(1, returned[1])
    early.blocks[0]["dy"] = returned[0]
    gradient("product", ("dy",), [(0, 0, 4), (0, 4, 4)])
    move(sums.over_y)
    early.back_first(0, returned[0])
    pass
    gradient("h2", ("dg", "dup"), [(0, 0, half), (0, half, half), (1, 0, half), (1, half, half)])
    pass
    dx = [None, None]
    for b in (1, 0):
        dx[b] = early.back_second(b)
    move(sums.over_y, sums.over_z)
    gradient("gated", ("dm",), [(0, 0, eight)])
    gradient("h1", ("dq", "dkp", "dvp", "du"), [(s, 0, eight) for s in range(4)])

    ends = [jnp.where(is_first, dx[b], outputs[b]) for b in range(2)]
    joined = jnp.stack(quarters(*ends) if usual else ends)[None]
    if usual:
        while sums.waiting:
            move(sums.over_y, sums.over_z)
        while sums.over_z(last=True):
            pass
        return (joined, *(h[None] for h in held))
    found = [[], [], [], []]
    for (index, total), chunk in zip(spans, chunks):
        chunk = jnp.concatenate(chunk)
        blocks, quarter = chunk.shape[0] // 4, chunk.shape[1]
        rows_first = chunk.reshape(4, blocks, quarter, LANES).transpose(0, 2, 1, 3)
        found[index].append(rows_first.reshape(4 * quarter, blocks * LANES))
    summed = []
    for pieces in found:
        part = lax.psum_scatter(
            jnp.concatenate(pieces, axis=1), "seq", scatter_dimension=0, tiled=True
        )
        summed.append(lax.psum(part, "dp").astype(f32)[None])
    return (joined, *summed)


def solution(mesh):
    in_specs = (
        P("section", "dp", "seq", None),
        P("dp", "seq"),
        P("section", None),
        P("section", None, None),
        P("section", None, None),
        P("section", None, None),
        P("section", None, None),
    )
    out_specs = (
        P("section", "dp", "seq", None),
        P("section", "seq", None),
        P("section", "seq", None),
        P("section", "seq", None),
        P("section", "seq", None),
    )
    return jax.shard_map(
        per_device, mesh=mesh, in_specs=in_specs, out_specs=out_specs, check_vma=False
    )
```
